32 devices in a mesh: grp: 2 (over x), slab: 16 (over z, y, core).
Axes of the slice: x: 2, y: 2, z: 4, core: 2. Of those that a mesh axis runs over, the one named last changes fastest.
Arguments:
- image: float32 [2, 384, 192, 256], P(None, ('grp', 'slab')), parts along dimension 1, may hold values from -6 to 6
- adjoint_data: bfloat16 [2, 384, 192, 256], P(None, ('grp', 'slab')), parts along dimension 1, may hold values from -6 to 6
- coil_maps: bfloat16 [8, 2, 384, 192, 256], P(None, None, ('grp', 'slab')), parts along dimension 2, may hold values from -2.5 to 2.5
- masks: int32 [1, 384, 192], P(None, 'grp'), parts along dimension 1, may hold values 0 or 1
- sources: int32 [1, 1152, 2], P(None, ('grp', 'slab')), parts along dimension 1, may hold values from 0 to 575, as said below
- weights: bfloat16 [1, 1152, 8192], P(None, ('grp', 'slab')), parts along dimension 1, may hold values from -0.5 to 0.5
Outputs:
- updated: float32 [2, 384, 192, 256], P(None, ('grp', 'slab')), parts along dimension 1
The draws below stay inside these ranges and needn't reach their ends.
There are 2 independent parts, one for each index of `grp`. The reference program is written for one: setup_inputs(seed, part) draws one part's arguments, and reference() takes and returns one part's arrays. A program takes and returns all parts, laid end to end along the dimension named above; each array names one. Nothing has to cross between parts.
Inputs may be any that keep to these rules, and one draw needn't show every extreme that they name: sources[s, t, j] is a block number (plane * 3 + y block); its plane lies within 24 planes of target block t's plane, and its y block within one of t's y block.
All inputs are finite; a program needn't handle non-finite values.
Results may differ from the reference program's by a relative error of at most 0.005.
Values may be sent and summed in bfloat16 or wider, within the bound.
No kernel may reach another device: no remote copies, remote signals or barrier semaphores. Data moves between devices by JAX's collectives and lax.ppermute only.
A program may use at most 256 MiB of HBM per device.

```python
import math
import jax
import jax.numpy as jnp
from jax import lax

NX = 192
NY = 192
NZ = 256
COILS = 8
BLK = 64
REACH = 2
STATES = 1
SLAB_ROWS = 12
TBLOCKS = 576


def draw_sources(key, part):
    y_blocks = NY // BLK
    reach_planes = REACH * SLAB_ROWS
    targets = jnp.arange(TBLOCKS, dtype=jnp.int32)
    target_plane = targets // y_blocks
    column = targets % y_blocks
    moving_zone = (target_plane >= NX // 4) & (target_plane < NX - NX // 4)
    spread = jnp.where(moving_zone, reach_planes, 1).astype(jnp.int32)
    key_shift, key_side = jax.random.split(jax.random.fold_in(key, 11))
    moved_by = jax.random.randint(key_shift, (STATES, TBLOCKS), -spread, spread)
    sideways = jax.random.randint(key_side, (STATES, TBLOCKS, 2), -1, 2)
    pair_step = jnp.arange(2, dtype=jnp.int32)
    source_plane = jnp.clip(target_plane[None, :, None] + moved_by[:, :, None] + pair_step, 0, NX - 1)
    source_column = jnp.clip(column[None, :, None] + sideways, 0, y_blocks - 1)
    linked = source_plane * y_blocks + source_column
    middle = TBLOCKS // 2
    mid_plane = middle // y_blocks
    mid_column = middle % y_blocks
    linked = linked.at[:, middle, 0].set((mid_plane - reach_planes) * y_blocks + mid_column)
    linked = linked.at[:, middle, 1].set((mid_plane + reach_planes) * y_blocks + mid_column)
    linked = linked.at[:, 0, 0].set(0)
    linked = linked.at[:, TBLOCKS - 1, 1].set(TBLOCKS - 1)
    return linked.astype(jnp.int32)


def set_ends(drawn, stream_key, low, top_value):
    shape = drawn.shape
    index_at = [jax.random.randint(jax.random.fold_in(stream_key, axis), (), 0, shape[axis]) for axis in range(len(shape))]
    drawn = drawn.at[tuple(index_at)].set(low)
    longest = shape.index(max(shape))
    index_at[longest] = (index_at[longest] + 1) % shape[longest]
    return drawn.at[tuple(index_at)].set(top_value)


def steps_of(stream_key, shape, pieces, low, top_value):
    def one(position, shards_of):
        steps = jax.random.uniform(jax.random.fold_in(jax.random.fold_in(stream_key, 6), position), (shards_of,), jnp.float32, low / len(pieces), top_value / len(pieces))
        return jnp.repeat(jnp.exp(steps), shape[position] // shards_of).reshape((-1,) + (1,) * (len(shape) - position - 1))

    factor_of = one(*pieces[0])
    for cut in pieces[1:]:
        factor_of = factor_of * one(*cut)
    return factor_of


def scatter_about(rng, dims, width, most, cuts=(), kind=jnp.bfloat16):
    level = steps_of(rng, dims, cuts, -0.22, 0.18) if cuts else 1.0
    values = jax.random.normal(rng, dims, jnp.float32) * width * level
    return jnp.minimum(jnp.maximum(values, -most), most).astype(kind)


def setup_inputs(seed: int = 0, part: int = 0) -> dict:
    splits = jax.random.split(jax.random.key(seed), 7)
    part_keys = jax.random.split(jax.random.fold_in(splits[6], part), 7)
    image = scatter_about(part_keys[0], (2, NX, NY, NZ), 1.0, 6.0, ((1, 16),), jnp.float32)
    adjoint_data = scatter_about(part_keys[1], (2, NX, NY, NZ), 1.0, 6.0, ((1, 16),))
    coil_maps = scatter_about(part_keys[2], (COILS, 2, NX, NY, NZ), 0.35, 2.5, ((2, 16),))
    masks = set_ends((jax.random.randint(part_keys[3], (STATES, NX, NY), 0, 3) < 1).astype(jnp.int32), jax.random.fold_in(part_keys[3], 1), 0, 1)
    sources = draw_sources(jax.random.fold_in(jax.random.fold_in(splits[6], part), 71), part)
    weights = scatter_about(part_keys[5], (STATES, TBLOCKS, 2 * BLK * BLK), (2 * BLK) ** -0.5, 0.5, ((1, 16),))
    return {"image": image, "adjoint_data": adjoint_data, "coil_maps": coil_maps, "masks": masks, "sources": sources, "weights": weights}


def dft_table(length, direction):
    positions = jnp.arange(length, dtype=jnp.int32)
    product = positions[:, None] * positions[None, :] % length
    phases = product.astype(jnp.float32) * (2.0 * math.pi / length)
    factor = 1.0 / math.sqrt(length)
    cosine = jnp.cos(phases) * factor
    sine_part = jnp.sin(phases) * (direction * factor)
    upper_rows = jnp.stack([cosine, -sine_part], axis=1)
    lower_rows = jnp.stack([sine_part, cosine], axis=1)
    return jnp.stack([upper_rows, lower_rows], axis=0).astype(jnp.bfloat16)

def keep_bf(values):
    return lax.optimization_barrier(values.astype(jnp.bfloat16))

def along_y(volume, matrix):
    return jnp.einsum('cpxjz,qkpj->cqxkz', volume.astype(jnp.float32), matrix.astype(jnp.float32))

def along_x(volume, matrix):
    return jnp.einsum('cpjyz,qkpj->cqkyz', volume.astype(jnp.float32), matrix.astype(jnp.float32))

def reference(image, adjoint_data, coil_maps, masks, sources, weights):
    rounded = keep_bf(image).astype(jnp.float32).reshape(2, TBLOCKS, BLK, NZ)
    forward_y = dft_table(NY, -1.0)
    inverse_y = dft_table(NY, 1.0)
    forward_x = dft_table(NX, -1.0)
    inverse_x = dft_table(NX, 1.0)
    gradient = jnp.zeros((2, TBLOCKS, BLK, NZ), jnp.float32)
    for motion in range(STATES):
        link_ids = sources[motion]
        matrices = weights[motion].reshape(TBLOCKS, 2, BLK, BLK).astype(jnp.float32)
        warped = jnp.zeros((2, TBLOCKS, BLK, NZ), jnp.float32)
        for member in range(2):
            picked = jnp.take(rounded, link_ids[:, member], axis=1)
            warped = warped + jnp.einsum('tij,rtjz->rtiz', matrices[:, member], picked)
        warped = warped.reshape(2, NX, NY, NZ)
        sampled = masks[motion].astype(jnp.float32)[None, None, :, :, None]

        def one_coil(summed, sensitivity):
            real_map = sensitivity[0].astype(jnp.float32)
            imag_map = sensitivity[1].astype(jnp.float32)
            real_part = real_map * warped[0] - imag_map * warped[1]
            imag_part = real_map * warped[1] + imag_map * warped[0]
            coil_image = keep_bf(jnp.stack([real_part, imag_part])[None])
            spectra = keep_bf(along_y(coil_image, forward_y))
            middle = keep_bf(along_x(spectra, forward_x) * sampled)
            restored = keep_bf(along_x(middle, inverse_x))
            returned = along_y(restored, inverse_y)[0]
            real_back = real_map * returned[0] + imag_map * returned[1]
            imag_back = real_map * returned[1] - imag_map * returned[0]
            return (summed + jnp.stack([real_back, imag_back]), None)
        combined, _ = lax.scan(one_coil, jnp.zeros((2, NX, NY, NZ), jnp.float32), coil_maps)
        grad_blocks = keep_bf(combined).astype(jnp.float32).reshape(2, TBLOCKS, BLK, NZ)
        for member in range(2):
            product = jnp.einsum('tij,rtiz->rtjz', matrices[:, member], grad_blocks)
            gradient = gradient.at[:, link_ids[:, member]].add(product)
    gradient = gradient.reshape(2, NX, NY, NZ)
    return image - 0.5 * (gradient - adjoint_data.astype(jnp.float32))
```

```python
import functools
import math

import jax
import jax.numpy as jnp
import numpy as np
from jax import lax
from jax.experimental import pallas as pl
from jax.experimental.pallas import tpu as pltpu
from jax.sharding import PartitionSpec as P

BLK = 64
LANES = 384
HALF = 256
VMEM_LIMIT = 56 * 1024 * 1024
BF = jnp.bfloat16
F32 = jnp.float32


def lane_order(length):
    lo, rest = 128, length - 128
    part = np.concatenate([np.zeros(lo), np.ones(lo), np.zeros(rest), np.ones(rest)])
    pos = np.concatenate([np.arange(lo), np.arange(lo), lo + np.arange(rest), lo + np.arange(rest)])
    return part.astype(np.int32), pos.astype(np.int32)


def dft_table(length, direction):
    positions = np.arange(length)
    phases = (positions[:, None] * positions[None, :] % length).astype(np.float32)
    phases = phases * np.float32(2.0 * math.pi / length)
    factor = np.float32(1.0 / math.sqrt(length))
    cosine = np.cos(phases) * factor
    sine = np.sin(phases) * (np.float32(direction) * factor)
    upper = np.stack([cosine, -sine], axis=1)
    lower = np.stack([sine, cosine], axis=1)
    return np.stack([upper, lower], axis=0)


def tables(nx, ny):
    part, pos = lane_order(ny)
    fwd_y, inv_y = dft_table(ny, -1.0), dft_table(ny, 1.0)
    into_y = np.zeros((2 * ny, 2, HALF), np.float32)
    into_y[:, :, :ny] = np.transpose(fwd_y[:, :, part, pos], (2, 0, 1))
    from_y = np.zeros((2, HALF, 2 * ny), np.float32)
    from_y[:, :ny, :] = np.transpose(inv_y[part, pos], (1, 2, 0))
    fwd_x = dft_table(nx, -1.0).reshape(2 * nx, 2 * nx)
    inv_x = dft_table(nx, 1.0).reshape(2 * nx, 2 * nx)
    out = (into_y.reshape(2 * ny, 2 * HALF), fwd_x, inv_x, from_y.reshape(2 * HALF, 2 * ny))
    return tuple(jnp.asarray(t, BF) for t in out)


def params():
    return pltpu.CompilerParams(vmem_limit_bytes=VMEM_LIMIT)


def to_rows(parts):
    stacked = jnp.concatenate(
        [parts[0, :128], parts[1, :128], parts[0, 128:], parts[1, 128:]], axis=0
    )
    return stacked.T


def spread_rows(out, rows, scratch, count, deep):
    if deep % 16 == 0:
        out[...] = rows.reshape(count, deep, LANES)
    else:
        scratch[...] = rows.astype(F32)
        for d in range(count):
            out[d] = scratch[pl.ds(d * deep, deep), :].astype(BF)


def image_kernel(count, deep, x_ref, o_ref, scratch):
    spread_rows(o_ref.at[:, 0], to_rows(x_ref[:, 0].astype(BF)), scratch, count, deep)


def image_columns(image, count):
    _, planes, ny, nz = image.shape
    deep = nz // count
    return pl.pallas_call(
        functools.partial(image_kernel, count, deep),
        out_shape=jax.ShapeDtypeStruct((count, planes, deep, LANES), BF),
        grid=(planes,),
        in_specs=[pl.BlockSpec((2, 1, ny, nz), lambda x: (0, x, 0, 0))],
        out_specs=pl.BlockSpec((count, 1, deep, LANES), lambda x: (0, x, 0, 0)),
        scratch_shapes=[pltpu.VMEM((nz, LANES), F32)],
        compiler_params=params(),
        cost_estimate=pl.CostEstimate(flops=0, bytes_accessed=image.size * 6, transcendentals=0),
        name="image_columns",
    )(image)


def maps_kernel(count, deep, x_ref, o_ref, scratch):
    spread_rows(o_ref.at[:, 0, 0], to_rows(x_ref[0, :, 0]), scratch, count, deep)


def maps_columns(coil_maps, count, first, coils):
    _, _, planes, ny, nz = coil_maps.shape
    deep = nz // count
    return pl.pallas_call(
        functools.partial(maps_kernel, count, deep),
        out_shape=jax.ShapeDtypeStruct((count, planes, coils, deep, LANES), BF),
        grid=(planes, coils),
        in_specs=[pl.BlockSpec((1, 2, 1, ny, nz), lambda x, c: (first + c, 0, x, 0, 0))],
        out_specs=pl.BlockSpec((count, 1, 1, deep, LANES), lambda x, c: (0, x, c, 0, 0)),
        scratch_shapes=[pltpu.VMEM((nz, LANES), F32)],
        compiler_params=params(),
        cost_estimate=pl.CostEstimate(
            flops=0, bytes_accessed=coils * 2 * planes * ny * nz * 4, transcendentals=0
        ),
        name="maps_columns",
    )(coil_maps)


def low_half(shape):
    return lax.broadcasted_iota(jnp.int32, shape, len(shape) - 1) < BLK


def warp_kernel(nx, deep, pad, links, g_ref, w_ref, o_ref, twice):
    planes = o_ref.shape[0]
    step = pl.program_id(0)

    @pl.when(step == 0)
    def _():
        def split(x, carry):
            low = low_half((deep, 128))
            for v in range(3):
                row = g_ref[x, :, v * 128 : (v + 1) * 128].astype(F32)
                turned = pltpu.roll(row, BLK, 1)
                first = jnp.where(low, row, turned).astype(BF)
                second = jnp.where(low, turned, row).astype(BF)
                if v < 2:
                    twice[3 * x, pl.ds(v * pad, deep), :] = first
                    twice[3 * x + 1, pl.ds(v * pad, deep), :] = second
                else:
                    twice[3 * x + 2, pl.ds(0, deep), :] = first
                    twice[3 * x + 2, pl.ds(pad, deep), :] = second
            return carry

        lax.fori_loop(0, nx, split, 0)

    low = low_half((2 * pad, 128))

    def plane(x, carry):
        outs = []
        for b in range(3):
            t = 3 * x + b
            g = 2 * (3 * planes * step + t)
            both = jnp.where(low, twice[links[g]], twice[links[g + 1]])
            outs.append(
                lax.dot_general(
                    both, w_ref[t], (((1,), (1,)), ((), ())), preferred_element_type=F32
                )
            )
        a, b, c = outs
        re = jnp.concatenate([a[:deep], b[:deep]], axis=1)
        im = jnp.concatenate([a[pad : pad + deep], b[pad : pad + deep]], axis=1)
        rest = jnp.concatenate([c[:deep], c[pad : pad + deep]], axis=1)
        o_ref[x, :, 0:128] = re
        o_ref[x, :, 128:256] = im
        o_ref[x, :, 256:384] = rest
        return carry

    lax.fori_loop(0, planes, plane, 0, unroll=True)


def warp(columns, weights, links, planes):
    nx, deep, _ = columns.shape
    blocks = weights.shape[0]
    pad = max(16, deep)
    return pl.pallas_call(
        functools.partial(warp_kernel, nx, deep, pad),
        out_shape=jax.ShapeDtypeStruct((nx, deep, LANES), F32),
        grid_spec=pltpu.PrefetchScalarGridSpec(
            num_scalar_prefetch=1,
            grid=(nx // planes,),
            in_specs=[
                pl.BlockSpec((nx, deep, LANES), lambda s, l: (0, 0, 0)),
                pl.BlockSpec((3 * planes, BLK, 2 * BLK), lambda s, l: (s, 0, 0)),
            ],
            out_specs=pl.BlockSpec((planes, deep, LANES), lambda s, l: (s, 0, 0)),
            scratch_shapes=[pltpu.VMEM((blocks, 2 * pad, 128), BF)],
        ),
        compiler_params=params(),
        cost_estimate=pl.CostEstimate(
            flops=2 * blocks * 256 * 256 * 32, bytes_accessed=20 << 20, transcendentals=0
        ),
        name="warp",
    )(links, columns, weights)


def spread_kernel(nx, deep, pad, links, c_ref, w_ref, o_ref, total):
    planes = c_ref.shape[0]
    step = pl.program_id(0)

    @pl.when(step == 0)
    def _():
        def clear(i, carry):
            total[pl.ds(i * 3, 3)] = jnp.zeros((3, 2 * pad, 128), F32)
            return carry

        lax.fori_loop(0, nx, clear, 0)

    low = low_half((2 * pad, 128))

    def tall(a, b):
        if deep == pad:
            return jnp.concatenate([a, b], axis=0)
        fill = jnp.zeros((pad - deep, a.shape[1]), a.dtype)
        return jnp.concatenate([a, fill, b, fill], axis=0)

    def plane(x, carry):
        re, im, rest = (c_ref[x, :, v * 128 : (v + 1) * 128] for v in range(3))
        blocks = (
            tall(re[:, :BLK], im[:, :BLK]),
            tall(re[:, BLK:], im[:, BLK:]),
            tall(rest[:, :BLK], rest[:, BLK:]),
        )
        for b in range(3):
            t = 3 * x + b
            g = 2 * (3 * planes * step + t)
            out = jnp.dot(blocks[b].astype(BF), w_ref[t], preferred_element_type=F32)
            zero = jnp.zeros_like(out)
            total[links[g]] += jnp.where(low, out, zero)
            total[links[g + 1]] += jnp.where(low, zero, out)
        return carry

    lax.fori_loop(0, planes, plane, 0, unroll=True)

    @pl.when(step == pl.num_programs(0) - 1)
    def _():
        low_row = low_half((deep, 128))

        def gather(x, carry):
            sums = []
            for b in range(3):
                value = total[3 * x + b]
                sums.append(value + pltpu.roll(value, BLK, 1))
            a, b, c = sums
            o_ref[x, :, 0:128] = jnp.where(low_row, a[:deep], b[:deep]).astype(BF)
            o_ref[x, :, 128:256] = jnp.where(
                low_row, a[pad : pad + deep], b[pad : pad + deep]
            ).astype(BF)
            o_ref[x, :, 256:384] = jnp.where(low_row, c[:deep], c[pad : pad + deep]).astype(BF)
            return carry

        lax.fori_loop(0, nx, gather, 0)


def spread(combined, weights, links, planes):
    nx, deep, _ = combined.shape
    blocks = weights.shape[0]
    pad = max(16, deep)
    return pl.pallas_call(
        functools.partial(spread_kernel, nx, deep, pad),
        out_shape=jax.ShapeDtypeStruct((nx, deep, LANES), BF),
        grid_spec=pltpu.PrefetchScalarGridSpec(
            num_scalar_prefetch=1,
            grid=(nx // planes,),
            in_specs=[
                pl.BlockSpec((planes, deep, LANES), lambda s, l: (s, 0, 0)),
                pl.BlockSpec((3 * planes, BLK, 2 * BLK), lambda s, l: (s, 0, 0)),
            ],
            out_specs=pl.BlockSpec((nx, deep, LANES), lambda s, l: (0, 0, 0)),
            scratch_shapes=[pltpu.VMEM((blocks, 2 * pad, 128), F32)],
        ),
        compiler_params=params(),
        cost_estimate=pl.CostEstimate(
            flops=2 * blocks * 256 * 256 * 32, bytes_accessed=20 << 20, transcendentals=0
        ),
        name="spread",
    )(links, combined, weights)


def coil_kernel(nx, deep, pad, fresh, *refs):
    if fresh:
        s_ref, w_ref, mask, iy, fx, bx, oy, o_ref, rows = refs
    else:
        s_ref, w_ref, mask, iy, fx, bx, oy, before, o_ref, rows = refs
    group = 8 if nx % 8 == 0 else 1
    cube = rows.reshape(3, nx, pad, 128)
    low = low_half((group, deep, 128))

    def thirds(ref, at):
        return tuple(ref[at, :, v * 128 : (v + 1) * 128].astype(F32) for v in range(3))

    def expand(i, carry):
        at = pl.ds(i * group, group)
        s0, s1, s2 = thirds(s_ref.at[:, 0], at)
        w0, w1, w2 = thirds(w_ref, at)
        turned = pltpu.roll(s2, BLK, 2)
        other = pltpu.roll(w2, BLK, 2)
        real = jnp.where(low, s2, turned)
        imag = jnp.where(low, turned, s2)
        cube[0, at, pl.ds(0, deep), :] = s0 * w0 - s1 * w1
        cube[1, at, pl.ds(0, deep), :] = s0 * w1 + s1 * w0
        cube[2, at, pl.ds(0, deep), :] = real * w2 + imag * jnp.where(low, -other, other)
        return carry

    lax.fori_loop(0, nx // group, expand, 0)

    def column(z, carry):
        at = pl.ds(z, nx, stride=pad)
        line = jnp.concatenate(
            [rows[v, at, :] for v in range(3)], axis=1
        ).astype(BF)
        y = jnp.dot(line, iy[...], preferred_element_type=F32).astype(BF)
        y = jnp.concatenate([y[:, :HALF], y[:, HALF:]], axis=0)
        y = jnp.dot(fx[...], y, preferred_element_type=F32) * mask[...]
        y = jnp.dot(bx[...], y.astype(BF), preferred_element_type=F32).astype(BF)
        y = jnp.concatenate([y[:nx], y[nx:]], axis=1)
        y = jnp.dot(y, oy[...], preferred_element_type=F32)
        for v in range(3):
            rows[v, at, :] = y[:, v * 128 : (v + 1) * 128]
        return carry

    lax.fori_loop(0, deep, column, 0)

    first = pl.program_id(0) == 0

    def combine(i, carry):
        at = pl.ds(i * group, group)
        s0, s1, s2 = thirds(s_ref.at[:, 0], at)
        r0, r1, r2 = (cube[v, at, pl.ds(0, deep), :] for v in range(3))
        turned = pltpu.roll(s2, BLK, 2)
        other = pltpu.roll(r2, BLK, 2)
        real = jnp.where(low, s2, turned)
        imag = jnp.where(low, turned, s2)
        terms = (
            s0 * r0 + s1 * r1,
            s0 * r1 - s1 * r0,
            real * r2 + imag * jnp.where(low, other, -other),
        )
        for v in range(3):
            lanes = slice(v * 128, (v + 1) * 128)
            old = o_ref[at, :, lanes]
            start = jnp.zeros_like(old) if fresh else before[at, :, lanes]
            o_ref[at, :, lanes] = jnp.where(first, start, old) + terms[v]
        return carry

    lax.fori_loop(0, nx // group, combine, 0)


def coils(maps, warped, mask, tabs, before):
    nx, deep, _ = warped.shape
    count = maps.shape[1]
    pad = max(8, deep)
    fresh = before is None
    whole = lambda shape: pl.BlockSpec(
        shape, lambda c: (0,) * len(shape), pipeline_mode=pl.Buffered(1)
    )
    in_specs = [pl.BlockSpec((nx, 1, deep, LANES), lambda c: (0, c, 0, 0))]
    args = [maps, warped, mask, *tabs] + ([] if fresh else [before])
    in_specs += [whole(a.shape) for a in args[1:]]
    return pl.pallas_call(
        functools.partial(coil_kernel, nx, deep, pad, fresh),
        out_shape=jax.ShapeDtypeStruct((nx, deep, LANES), F32),
        grid=(count,),
        in_specs=in_specs,
        out_specs=pl.BlockSpec((nx, deep, LANES), lambda c: (0, 0, 0)),
        scratch_shapes=[pltpu.VMEM((3, nx * pad, 128), F32)],
        compiler_params=params(),
        cost_estimate=pl.CostEstimate(
            flops=count * deep * 4 * 8 * nx * nx * 192 * 2,
            bytes_accessed=count * nx * deep * LANES * 2 + (14 << 20),
            transcendentals=0,
        ),
        name="coils",
    )(*args)


def update_kernel(count, deep, g_ref, i_ref, a_ref, o_ref, scratch):
    if deep % 16 == 0:
        rows = g_ref[:, 0].reshape(count * deep, LANES)
    else:
        for d in range(count):
            scratch[pl.ds(d * deep, deep), :] = g_ref[d, 0].astype(F32)
        rows = scratch[...]
    grad = rows.astype(F32).T
    real = jnp.concatenate([grad[0:128], grad[256:320]], axis=0)
    imag = jnp.concatenate([grad[128:256], grad[320:384]], axis=0)
    for part, value in enumerate((real, imag)):
        o_ref[part, 0] = i_ref[part, 0] - 0.5 * (value - a_ref[part, 0].astype(F32))


def update(back, image, adjoint):
    count, planes, deep, _ = back.shape
    _, _, ny, nz = image.shape
    block = pl.BlockSpec((2, 1, ny, nz), lambda x: (0, x, 0, 0))
    return pl.pallas_call(
        functools.partial(update_kernel, count, deep),
        out_shape=jax.ShapeDtypeStruct(image.shape, F32),
        grid=(planes,),
        in_specs=[
            pl.BlockSpec((count, 1, deep, LANES), lambda x: (0, x, 0, 0)),
            block,
            block,
        ],
        out_specs=block,
        scratch_shapes=[pltpu.VMEM((nz, LANES), F32)],
        compiler_params=params(),
        cost_estimate=pl.CostEstimate(flops=0, bytes_accessed=image.size * 12, transcendentals=0),
        name="update",
    )(back, image, adjoint)


def exchange(parts):
    return lax.all_to_all(parts, "slab", split_axis=0, concat_axis=0, tiled=True)


def split_coils(total):
    sizes = []
    left = total
    while left:
        size = 1 if left <= 2 else min(3, left - 1)
        sizes.append(size)
        left -= size
    return sizes


def per_device(image, adjoint_data, coil_maps, masks, sources, weights):
    count = lax.axis_size("slab")
    planes, ny, nz = image.shape[1:]
    nx = planes * count
    deep = nz // count
    tabs = tables(nx, ny)
    matrices = weights[0].reshape(3 * planes, 2, BLK, BLK)
    matrices = jnp.transpose(matrices, (0, 2, 1, 3)).reshape(3 * planes, BLK, 2 * BLK)
    matrices = lax.all_gather(matrices, "slab", axis=0, tiled=True)
    links = lax.all_gather(sources[0], "slab", axis=0, tiled=True).reshape(-1)
    sampled = jnp.pad(masks[0].astype(F32), ((0, 0), (0, HALF - ny)))
    mask = jnp.concatenate([sampled, sampled], axis=0)

    columns = exchange(image_columns(image, count)).reshape(nx, deep, LANES)
    sizes = split_coils(coil_maps.shape[0])
    sent, first = [], 0
    for size in sizes:
        sent.append(exchange(maps_columns(coil_maps, count, first, size)))
        first += size
    warped = warp(columns, matrices, links, planes)
    combined = None
    for size, part in zip(sizes, sent):
        maps = part.reshape(nx, size, deep, LANES)
        combined = coils(maps, warped, mask, tabs, combined)
    grad = spread(combined, matrices, links, planes)
    back = exchange(grad.reshape(count, planes, deep, LANES))
    return update(back, image, adjoint_data)


def solution(mesh):
    return jax.shard_map(
        per_device,
        mesh=mesh,
        in_specs=(
            P(None, ("grp", "slab"), None, None),
            P(None, ("grp", "slab"), None, None),
            P(None, None, ("grp", "slab"), None, None),
            P(None, "grp", None),
            P(None, ("grp", "slab"), None),
            P(None, ("grp", "slab"), None),
        ),
        out_specs=P(None, ("grp", "slab"), None, None),
        check_vma=False,
    )
```

```python
import functools
import math

import jax
import jax.numpy as jnp
import numpy as np
from jax import lax
from jax.experimental import pallas as pl
from jax.experimental.pallas import tpu as pltpu
from jax.sharding import PartitionSpec as P

BLK = 64
LANES = 384
HALF = 256
VMEM_LIMIT = 56 * 1024 * 1024
BF = jnp.bfloat16
F32 = jnp.float32


def lane_order(length):
    lo, rest = 128, length - 128
    part = np.concatenate([np.zeros(lo), np.ones(lo), np.zeros(rest), np.ones(rest)])
    pos = np.concatenate([np.arange(lo), np.arange(lo), lo + np.arange(rest), lo + np.arange(rest)])
    return part.astype(np.int32), pos.astype(np.int32)


def dft_table(length, direction):
    positions = np.arange(length)
    phases = (positions[:, None] * positions[None, :] % length).astype(np.float32)
    phases = phases * np.float32(2.0 * math.pi / length)
    factor = np.float32(1.0 / math.sqrt(length))
    cosine = np.cos(phases) * factor
    sine = np.sin(phases) * (np.float32(direction) * factor)
    upper = np.stack([cosine, -sine], axis=1)
    lower = np.stack([sine, cosine], axis=1)
    return np.stack([upper, lower], axis=0)


def tables(nx, ny):
    part, pos = lane_order(ny)
    fwd_y, inv_y = dft_table(ny, -1.0), dft_table(ny, 1.0)
    into_y = np.zeros((2 * ny, 2, HALF), np.float32)
    into_y[:, :, :ny] = np.transpose(fwd_y[:, :, part, pos], (2, 0, 1))
    from_y = np.zeros((2, HALF, 2 * ny), np.float32)
    from_y[:, :ny, :] = np.transpose(inv_y[part, pos], (1, 2, 0))
    fwd_x = dft_table(nx, -1.0).reshape(2 * nx, 2 * nx)
    inv_x = dft_table(nx, 1.0).reshape(2 * nx, 2 * nx)
    out = (into_y.reshape(2 * ny, 2 * HALF), fwd_x, inv_x, from_y.reshape(2 * HALF, 2 * ny))
    return tuple(jnp.asarray(t, BF) for t in out)


def params():
    return pltpu.CompilerParams(vmem_limit_bytes=VMEM_LIMIT)


def to_rows(parts):
    stacked = jnp.concatenate(
        [parts[0, :128], parts[1, :128], parts[0, 128:], parts[1, 128:]], axis=0
    )
    return stacked.T


def spread_rows(outs, rows, scratch, count, deep):
    if len(outs) == 1 and deep % 16 == 0:
        outs[0][...] = rows.reshape(count, deep, LANES)
        return
    part = deep // len(outs)
    scratch[...] = rows.astype(F32)
    for h, out in enumerate(outs):
        for d in range(count):
            out[d] = scratch[pl.ds(d * deep + h * part, part), :].astype(BF)


def image_kernel(count, deep, x_ref, o_ref, scratch):
    spread_rows([o_ref.at[:, 0]], to_rows(x_ref[:, 0].astype(BF)), scratch, count, deep)


def image_columns(image, count):
    _, planes, ny, nz = image.shape
    deep = nz // count
    return pl.pallas_call(
        functools.partial(image_kernel, count, deep),
        out_shape=jax.ShapeDtypeStruct((count, planes, deep, LANES), BF),
        grid=(planes,),
        in_specs=[pl.BlockSpec((2, 1, ny, nz), lambda x: (0, x, 0, 0))],
        out_specs=pl.BlockSpec((count, 1, deep, LANES), lambda x: (0, x, 0, 0)),
        scratch_shapes=[pltpu.VMEM((nz, LANES), F32)],
        compiler_params=params(),
        cost_estimate=pl.CostEstimate(flops=0, bytes_accessed=image.size * 6, transcendentals=0),
        name="image_columns",
    )(image)


def maps_kernel(count, deep, x_ref, *refs):
    outs = [o.at[:, 0, 0] for o in refs[:-1]]
    spread_rows(outs, to_rows(x_ref[0, :, 0]), refs[-1], count, deep)


def maps_columns(coil_maps, count, first, coils, parts):
    _, _, planes, ny, nz = coil_maps.shape
    deep = nz // count
    part = deep // parts
    return pl.pallas_call(
        functools.partial(maps_kernel, count, deep),
        out_shape=[jax.ShapeDtypeStruct((count, planes, coils, part, LANES), BF)] * parts,
        grid=(planes, coils),
        in_specs=[pl.BlockSpec((1, 2, 1, ny, nz), lambda x, c: (first + c, 0, x, 0, 0))],
        out_specs=[pl.BlockSpec((count, 1, 1, part, LANES), lambda x, c: (0, x, c, 0, 0))] * parts,
        scratch_shapes=[pltpu.VMEM((nz, LANES), F32)],
        compiler_params=params(),
        cost_estimate=pl.CostEstimate(
            flops=0, bytes_accessed=coils * 2 * planes * ny * nz * 4, transcendentals=0
        ),
        name="maps_columns",
    )(coil_maps)


def low_half(shape):
    return lax.broadcasted_iota(jnp.int32, shape, len(shape) - 1) < BLK


def warp_kernel(nx, deep, pad, links, g_ref, w_ref, o_ref, twice):
    planes = o_ref.shape[0]
    step = pl.program_id(0)

    @pl.when(step == 0)
    def _():
        def split(x, carry):
            low = low_half((deep, 128))
            for v in range(3):
                row = g_ref[x, :, v * 128 : (v + 1) * 128].astype(F32)
                turned = pltpu.roll(row, BLK, 1)
                first = jnp.where(low, row, turned).astype(BF)
                second = jnp.where(low, turned, row).astype(BF)
                if v < 2:
                    twice[3 * x, pl.ds(v * pad, deep), :] = first
                    twice[3 * x + 1, pl.ds(v * pad, deep), :] = second
                else:
                    twice[3 * x + 2, pl.ds(0, deep), :] = first
                    twice[3 * x + 2, pl.ds(pad, deep), :] = second
            return carry

        lax.fori_loop(0, nx, split, 0)

    low = low_half((2 * pad, 128))

    def plane(x, carry):
        outs = []
        for b in range(3):
            t = 3 * x + b
            g = 2 * (3 * planes * step + t)
            both = jnp.where(low, twice[links[g]], twice[links[g + 1]])
            outs.append(
                lax.dot_general(
                    both, w_ref[t], (((1,), (1,)), ((), ())), preferred_element_type=F32
                )
            )
        a, b, c = outs
        re = jnp.concatenate([a[:deep], b[:deep]], axis=1)
        im = jnp.concatenate([a[pad : pad + deep], b[pad : pad + deep]], axis=1)
        rest = jnp.concatenate([c[:deep], c[pad : pad + deep]], axis=1)
        o_ref[x, :, 0:128] = re
        o_ref[x, :, 128:256] = im
        o_ref[x, :, 256:384] = rest
        return carry

    lax.fori_loop(0, planes, plane, 0, unroll=True)


def warp(columns, weights, links, planes):
    nx, deep, _ = columns.shape
    blocks = weights.shape[0]
    pad = max(16, deep)
    return pl.pallas_call(
        functools.partial(warp_kernel, nx, deep, pad),
        out_shape=jax.ShapeDtypeStruct((nx, deep, LANES), F32),
        grid_spec=pltpu.PrefetchScalarGridSpec(
            num_scalar_prefetch=1,
            grid=(nx // planes,),
            in_specs=[
                pl.BlockSpec((nx, deep, LANES), lambda s, l: (0, 0, 0)),
                pl.BlockSpec((3 * planes, BLK, 2 * BLK), lambda s, l: (s, 0, 0)),
            ],
            out_specs=pl.BlockSpec((planes, deep, LANES), lambda s, l: (s, 0, 0)),
            scratch_shapes=[pltpu.VMEM((blocks, 2 * pad, 128), BF)],
        ),
        compiler_params=params(),
        cost_estimate=pl.CostEstimate(
            flops=2 * blocks * 256 * 256 * 32, bytes_accessed=20 << 20, transcendentals=0
        ),
        name="warp",
    )(links, columns, weights)


def spread_kernel(nx, deep, pad, links, c_ref, w_ref, o_ref, total):
    planes = c_ref.shape[0]
    step = pl.program_id(0)

    @pl.when(step == 0)
    def _():
        def clear(i, carry):
            total[pl.ds(i * 3, 3)] = jnp.zeros((3, 2 * pad, 128), F32)
            return carry

        lax.fori_loop(0, nx, clear, 0)

    low = low_half((2 * pad, 128))

    def tall(a, b):
        if deep == pad:
            return jnp.concatenate([a, b], axis=0)
        fill = jnp.zeros((pad - deep, a.shape[1]), a.dtype)
        return jnp.concatenate([a, fill, b, fill], axis=0)

    def plane(x, carry):
        re, im, rest = (c_ref[x, :, v * 128 : (v + 1) * 128] for v in range(3))
        blocks = (
            tall(re[:, :BLK], im[:, :BLK]),
            tall(re[:, BLK:], im[:, BLK:]),
            tall(rest[:, :BLK], rest[:, BLK:]),
        )
        for b in range(3):
            t = 3 * x + b
            g = 2 * (3 * planes * step + t)
            out = jnp.dot(blocks[b].astype(BF), w_ref[t], preferred_element_type=F32)
            zero = jnp.zeros_like(out)
            total[links[g]] += jnp.where(low, out, zero)
            total[links[g + 1]] += jnp.where(low, zero, out)
        return carry

    lax.fori_loop(0, planes, plane, 0, unroll=True)

    @pl.when(step == pl.num_programs(0) - 1)
    def _():
        low_row = low_half((deep, 128))

        def gather(x, carry):
            sums = []
            for b in range(3):
                value = total[3 * x + b]
                sums.append(value + pltpu.roll(value, BLK, 1))
            a, b, c = sums
            o_ref[x, :, 0:128] = jnp.where(low_row, a[:deep], b[:deep]).astype(BF)
            o_ref[x, :, 128:256] = jnp.where(
                low_row, a[pad : pad + deep], b[pad : pad + deep]
            ).astype(BF)
            o_ref[x, :, 256:384] = jnp.where(low_row, c[:deep], c[pad : pad + deep]).astype(BF)
            return carry

        lax.fori_loop(0, nx, gather, 0)


def spread(combined, weights, links, planes):
    nx, deep, _ = combined.shape
    blocks = weights.shape[0]
    pad = max(8, deep)
    return pl.pallas_call(
        functools.partial(spread_kernel, nx, deep, pad),
        out_shape=jax.ShapeDtypeStruct((nx, deep, LANES), BF),
        grid_spec=pltpu.PrefetchScalarGridSpec(
            num_scalar_prefetch=1,
            grid=(nx // planes,),
            in_specs=[
                pl.BlockSpec((planes, deep, LANES), lambda s, l: (s, 0, 0)),
                pl.BlockSpec((3 * planes, BLK, 2 * BLK), lambda s, l: (s, 0, 0)),
            ],
            out_specs=pl.BlockSpec((nx, deep, LANES), lambda s, l: (0, 0, 0)),
            scratch_shapes=[pltpu.VMEM((blocks, 2 * pad, 128), F32)],
        ),
        compiler_params=params(),
        cost_estimate=pl.CostEstimate(
            flops=2 * blocks * 256 * 256 * 32, bytes_accessed=20 << 20, transcendentals=0
        ),
        name="spread",
    )(links, combined, weights)


def coil_kernel(nx, deep, pad, fresh, *refs):
    if fresh:
        s_ref, w_ref, mask, iy, fx, bx, oy, o_ref, rows = refs
    else:
        s_ref, w_ref, mask, iy, fx, bx, oy, before, o_ref, rows = refs
    group = 8 if nx % 8 == 0 else 1
    cube = rows.reshape(3, nx, pad, 128)
    low = low_half((group, deep, 128))

    def thirds(ref, at):
        return tuple(ref[at, :, v * 128 : (v + 1) * 128].astype(F32) for v in range(3))

    def expand(i, carry):
        at = pl.ds(i * group, group)
        s0, s1, s2 = thirds(s_ref.at[:, 0], at)
        w0, w1, w2 = thirds(w_ref, at)
        turned = pltpu.roll(s2, BLK, 2)
        other = pltpu.roll(w2, BLK, 2)
        real = jnp.where(low, s2, turned)
        imag = jnp.where(low, turned, s2)
        cube[0, at, pl.ds(0, deep), :] = s0 * w0 - s1 * w1
        cube[1, at, pl.ds(0, deep), :] = s0 * w1 + s1 * w0
        cube[2, at, pl.ds(0, deep), :] = real * w2 + imag * jnp.where(low, -other, other)
        return carry

    lax.fori_loop(0, nx // group, expand, 0)

    def column(z, carry):
        at = pl.ds(z, nx, stride=pad)
        line = jnp.concatenate(
            [rows[v, at, :] for v in range(3)], axis=1
        ).astype(BF)
        y = jnp.dot(line, iy[...], preferred_element_type=F32).astype(BF)
        y = jnp.concatenate([y[:, :HALF], y[:, HALF:]], axis=0)
        y = jnp.dot(fx[...], y, preferred_element_type=F32) * mask[...]
        y = jnp.dot(bx[...], y.astype(BF), preferred_element_type=F32).astype(BF)
        y = jnp.concatenate([y[:nx], y[nx:]], axis=1)
        y = jnp.dot(y, oy[...], preferred_element_type=F32)
        for v in range(3):
            rows[v, at, :] = y[:, v * 128 : (v + 1) * 128]
        return carry

    lax.fori_loop(0, deep, column, 0)

    first = pl.program_id(0) == 0

    def combine(i, carry):
        at = pl.ds(i * group, group)
        s0, s1, s2 = thirds(s_ref.at[:, 0], at)
        r0, r1, r2 = (cube[v, at, pl.ds(0, deep), :] for v in range(3))
        turned = pltpu.roll(s2, BLK, 2)
        other = pltpu.roll(r2, BLK, 2)
        real = jnp.where(low, s2, turned)
        imag = jnp.where(low, turned, s2)
        terms = (
            s0 * r0 + s1 * r1,
            s0 * r1 - s1 * r0,
            real * r2 + imag * jnp.where(low, other, -other),
        )
        for v in range(3):
            lanes = slice(v * 128, (v + 1) * 128)
            old = o_ref[at, :, lanes]
            start = jnp.zeros_like(old) if fresh else before[at, :, lanes]
            o_ref[at, :, lanes] = jnp.where(first, start, old) + terms[v]
        return carry

    lax.fori_loop(0, nx // group, combine, 0)


def coils(maps, warped, mask, tabs, before, part):
    nx, count, deep, _ = maps.shape
    pad = max(8, deep)
    fresh = before is None
    whole = lambda shape: pl.BlockSpec(
        shape, lambda c: (0,) * len(shape), pipeline_mode=pl.Buffered(1)
    )
    in_specs = [pl.BlockSpec((nx, 1, deep, LANES), lambda c: (0, c, 0, 0))]
    args = [maps, warped, mask, *tabs] + ([] if fresh else [before])
    columns = pl.BlockSpec(
        (nx, deep, LANES), lambda c: (0, part, 0), pipeline_mode=pl.Buffered(1)
    )
    in_specs += [columns] + [whole(a.shape) for a in (mask, *tabs)]
    in_specs += [] if fresh else [columns]
    return pl.pallas_call(
        functools.partial(coil_kernel, nx, deep, pad, fresh),
        out_shape=jax.ShapeDtypeStruct((nx, deep, LANES), F32),
        grid=(count,),
        in_specs=in_specs,
        out_specs=pl.BlockSpec((nx, deep, LANES), lambda c: (0, 0, 0)),
        scratch_shapes=[pltpu.VMEM((3, nx * pad, 128), F32)],
        compiler_params=params(),
        cost_estimate=pl.CostEstimate(
            flops=count * deep * 4 * 8 * nx * nx * 192 * 2,
            bytes_accessed=count * nx * deep * LANES * 2 + (14 << 20),
            transcendentals=0,
        ),
        name="coils",
    )(*args)


def update_kernel(count, parts, *refs):
    backs = refs[:parts]
    i_ref, a_ref, o_ref, scratch = refs[parts:]
    part = backs[0].shape[2]
    for h, back in enumerate(backs):
        for d in range(count):
            scratch[pl.ds((d * parts + h) * part, part), :] = back[d, 0].astype(F32)
    grad = scratch[...].T
    real = jnp.concatenate([grad[0:128], grad[256:320]], axis=0)
    imag = jnp.concatenate([grad[128:256], grad[320:384]], axis=0)
    for p, value in enumerate((real, imag)):
        o_ref[p, 0] = i_ref[p, 0] - 0.5 * (value - a_ref[p, 0].astype(F32))


def update(backs, image, adjoint):
    parts = len(backs)
    count, planes, part, _ = backs[0].shape
    _, _, ny, nz = image.shape
    block = pl.BlockSpec((2, 1, ny, nz), lambda x: (0, x, 0, 0))
    back = pl.BlockSpec((count, 1, part, LANES), lambda x: (0, x, 0, 0))
    return pl.pallas_call(
        functools.partial(update_kernel, count, parts),
        out_shape=jax.ShapeDtypeStruct(image.shape, F32),
        grid=(planes,),
        in_specs=[back] * parts + [block, block],
        out_specs=block,
        scratch_shapes=[pltpu.VMEM((nz, LANES), F32)],
        compiler_params=params(),
        cost_estimate=pl.CostEstimate(flops=0, bytes_accessed=image.size * 12, transcendentals=0),
        name="update",
    )(*backs, image, adjoint)


def exchange(parts):
    return lax.all_to_all(parts, "slab", split_axis=0, concat_axis=0, tiled=True)


def after(value, *others):
    return lax.optimization_barrier((value, *others))[0]


def split_coils(total):
    sizes = []
    while total > 1:
        sizes.append(total // 2)
        total -= total // 2
    return sizes + [1]


def per_device(image, adjoint_data, coil_maps, masks, sources, weights):
    count = lax.axis_size("slab")
    planes, ny, nz = image.shape[1:]
    nx = planes * count
    deep = nz // count
    parts = 2 if deep % 16 == 0 else 1
    tabs = tables(nx, ny)
    sampled = jnp.pad(masks[0].astype(F32), ((0, 0), (0, HALF - ny)))
    mask = jnp.concatenate([sampled, sampled], axis=0)

    matrices = weights[0].reshape(3 * planes, 2, BLK, BLK)
    matrices = jnp.transpose(matrices, (0, 2, 1, 3)).reshape(3 * planes, BLK, 2 * BLK)
    digits = jnp.concatenate([sources[0] // BLK, sources[0] % BLK], axis=1).astype(BF)
    digits = jnp.pad(digits[:, None, :], ((0, 0), (0, 7), (0, 2 * BLK - 4)))
    packed = jnp.concatenate([matrices, digits], axis=1)
    packed = lax.all_gather(packed, "slab", axis=0, tiled=True)
    digits = packed[:, BLK, :4].astype(jnp.int32)
    links = (digits[:, :2] * BLK + digits[:, 2:]).reshape(-1)

    columns = exchange(image_columns(image, count))
    sizes = split_coils(coil_maps.shape[0])
    outgoing, first = [], 0
    for i, size in enumerate(sizes):
        cut = parts if i == len(sizes) - 1 else 1
        pieces = maps_columns(coil_maps, count, first, size, cut)
        outgoing += [(size, h if cut > 1 else 0, piece) for h, piece in enumerate(pieces)]
        first += size
    whole = len(sizes) - 1 if parts > 1 else len(sizes)

    before = columns
    columns = columns.reshape(nx, deep, LANES)
    warped = warp(columns, packed, links, planes)
    received, done, combined, backs, grad = [], [], None, [], None
    for k, (size, h, piece) in enumerate(outgoing):
        needs = [before] + (done[k - 2 : k - 1] if k >= 2 else [])
        before = exchange(after(piece, *needs))
        received.append((size, h, before))
        if k >= 1:
            size, h, got = received[k - 1]
            combined_k = coils(
                got.reshape(nx, size, -1, LANES), warped, mask, tabs, combined, h
            )
            done.append(combined_k)
            if k - 1 < whole:
                combined = combined_k
            else:
                grad = spread(combined_k, packed, links, planes)
                backs.append(exchange(after(grad, before).reshape(count, planes, -1, LANES)))
    size, h, got = received[-1]
    if grad is not None:
        got = after(got, grad)
    combined = coils(got.reshape(nx, size, -1, LANES), warped, mask, tabs, combined, h)
    grad = spread(combined, packed, links, planes)
    backs.append(exchange(grad.reshape(count, planes, -1, LANES)))
    return update(backs, image, adjoint_data)


def solution(mesh):
    return jax.shard_map(
        per_device,
        mesh=mesh,
        in_specs=(
            P(None, ("grp", "slab"), None, None),
            P(None, ("grp", "slab"), None, None),
            P(None, None, ("grp", "slab"), None, None),
            P(None, "grp", None),
            P(None, ("grp", "slab"), None),
            P(None, ("grp", "slab"), None),
        ),
        out_specs=P(None, ("grp", "slab"), None, None),
        check_vma=False,
    )
```

```python
import functools
import math

import jax
import jax.numpy as jnp
import numpy as np
from jax import lax
from jax.experimental import pallas as pl
from jax.experimental.pallas import tpu as pltpu
from jax.sharding import PartitionSpec as P

BLK = 64
LANES = 384
HALF = 256
VMEM_LIMIT = 56 * 1024 * 1024
BF = jnp.bfloat16
F32 = jnp.float32


def lane_order(length):
    lo, rest = 128, length - 128
    part = np.concatenate([np.zeros(lo), np.ones(lo), np.zeros(rest), np.ones(rest)])
    pos = np.concatenate([np.arange(lo), np.arange(lo), lo + np.arange(rest), lo + np.arange(rest)])
    return part.astype(np.int32), pos.astype(np.int32)


def dft_table(length, direction):
    positions = np.arange(length)
    phases = (positions[:, None] * positions[None, :] % length).astype(np.float32)
    phases = phases * np.float32(2.0 * math.pi / length)
    factor = np.float32(1.0 / math.sqrt(length))
    cosine = np.cos(phases) * factor
    sine = np.sin(phases) * (np.float32(direction) * factor)
    upper = np.stack([cosine, -sine], axis=1)
    lower = np.stack([sine, cosine], axis=1)
    return np.stack([upper, lower], axis=0)


def tables(nx, ny):
    part, pos = lane_order(ny)
    fwd_y, inv_y = dft_table(ny, -1.0), dft_table(ny, 1.0)
    into_y = np.zeros((2 * ny, 2, HALF), np.float32)
    into_y[:, :, :ny] = np.transpose(fwd_y[:, :, part, pos], (2, 0, 1))
    from_y = np.zeros((2, HALF, 2 * ny), np.float32)
    from_y[:, :ny, :] = np.transpose(inv_y[part, pos], (1, 2, 0))
    fwd_x = dft_table(nx, -1.0).reshape(2 * nx, 2 * nx)
    inv_x = dft_table(nx, 1.0).reshape(2 * nx, 2 * nx)
    out = (into_y.reshape(2 * ny, 2 * HALF), fwd_x, inv_x, from_y.reshape(2 * HALF, 2 * ny))
    return tuple(jnp.asarray(t, BF) for t in out)


def params():
    return pltpu.CompilerParams(vmem_limit_bytes=VMEM_LIMIT)


def to_rows(parts):
    stacked = jnp.concatenate(
        [parts[0, :128], parts[1, :128], parts[0, 128:], parts[1, 128:]], axis=0
    )
    return stacked.T


def spread_rows(outs, rows, scratch, count, deep):
    if len(outs) == 1 and deep % 16 == 0:
        outs[0][...] = rows.reshape(count, deep, LANES)
        return
    part = deep // len(outs)
    scratch[...] = rows.astype(F32)
    for h, out in enumerate(outs):
        for d in range(count):
            out[d] = scratch[pl.ds(d * deep + h * part, part), :].astype(BF)


def image_kernel(count, deep, x_ref, o_ref, scratch):
    for x in range(x_ref.shape[1]):
        rows = to_rows(x_ref[:, x].astype(BF))
        spread_rows([o_ref.at[:, x]], rows, scratch, count, deep)


def image_columns(image, count):
    _, planes, ny, nz = image.shape
    deep = nz // count
    group = 3 if planes % 3 == 0 else 1
    return pl.pallas_call(
        functools.partial(image_kernel, count, deep),
        out_shape=jax.ShapeDtypeStruct((count, planes, deep, LANES), BF),
        grid=(planes // group,),
        in_specs=[pl.BlockSpec((2, group, ny, nz), lambda x: (0, x, 0, 0))],
        out_specs=pl.BlockSpec((count, group, deep, LANES), lambda x: (0, x, 0, 0)),
        scratch_shapes=[pltpu.VMEM((nz, LANES), F32)],
        compiler_params=params(),
        cost_estimate=pl.CostEstimate(flops=0, bytes_accessed=image.size * 6, transcendentals=0),
        name="image_columns",
    )(image)


def maps_kernel(count, deep, x_ref, o_ref, scratch):
    spread_rows([o_ref.at[:, 0, 0]], to_rows(x_ref[0, :, 0]), scratch, count, deep)


def last_maps_kernel(count, deep, x_ref, both_ref, first_ref, second_ref, scratch):
    part = deep // 2
    scratch[...] = to_rows(x_ref[0, :, 0]).astype(F32)
    coil = pl.program_id(1)
    for d in range(count):
        both_ref[d, 0, 0] = scratch[pl.ds(d * deep, part), :].astype(BF)

    def rest(out):
        for d in range(count):
            out[d, 0, 0] = scratch[pl.ds(d * deep + part, part), :].astype(BF)

    @pl.when(coil == 0)
    def _():
        rest(first_ref)

    @pl.when(coil == 1)
    def _():
        rest(second_ref)


def maps_columns(coil_maps, count, first, coils):
    _, _, planes, ny, nz = coil_maps.shape
    deep = nz // count
    return pl.pallas_call(
        functools.partial(maps_kernel, count, deep),
        out_shape=jax.ShapeDtypeStruct((count, planes, coils, deep, LANES), BF),
        grid=(planes, coils),
        in_specs=[pl.BlockSpec((1, 2, 1, ny, nz), lambda x, c: (first + c, 0, x, 0, 0))],
        out_specs=pl.BlockSpec((count, 1, 1, deep, LANES), lambda x, c: (0, x, c, 0, 0)),
        scratch_shapes=[pltpu.VMEM((nz, LANES), F32)],
        compiler_params=params(),
        cost_estimate=pl.CostEstimate(
            flops=0, bytes_accessed=coils * 2 * planes * ny * nz * 4, transcendentals=0
        ),
        name="maps_columns",
    )(coil_maps)


def last_maps_columns(coil_maps, count, first):
    _, _, planes, ny, nz = coil_maps.shape
    deep = nz // count
    part = deep // 2
    shapes = [(count, planes, coils, part, LANES) for coils in (2, 1, 1)]
    alone = pl.BlockSpec((count, 1, 1, part, LANES), lambda x, c: (0, x, 0, 0, 0))
    return pl.pallas_call(
        functools.partial(last_maps_kernel, count, deep),
        out_shape=[jax.ShapeDtypeStruct(shape, BF) for shape in shapes],
        grid=(planes, 2),
        in_specs=[pl.BlockSpec((1, 2, 1, ny, nz), lambda x, c: (first + c, 0, x, 0, 0))],
        out_specs=[
            pl.BlockSpec((count, 1, 1, part, LANES), lambda x, c: (0, x, c, 0, 0)),
            alone,
            alone,
        ],
        scratch_shapes=[pltpu.VMEM((nz, LANES), F32)],
        compiler_params=params(),
        cost_estimate=pl.CostEstimate(
            flops=0, bytes_accessed=4 * planes * ny * nz * 4, transcendentals=0
        ),
        name="last_maps_columns",
    )(coil_maps)


def low_half(shape):
    return lax.broadcasted_iota(jnp.int32, shape, len(shape) - 1) < BLK


def fetch(w_hbm, held, sems, k):
    size = held.shape[0] // sems.shape[0]
    at = pl.ds(k * size, size)
    return pltpu.make_async_copy(w_hbm.at[at, pl.ds(0, BLK), :], held.at[at], sems.at[k])


def fetch_all(w_hbm, held, sems):
    for k in range(sems.shape[0]):
        fetch(w_hbm, held, sems, k).start()


def warp_kernel(nx, deep, pad, links, owner, g_ref, w_hbm, o_ref, held, twice, sems):
    fetch_all(w_hbm, held, sems)
    count = sems.shape[0]
    planes = nx // count
    low = low_half((deep, 128))

    def split(x, carry):
        for v in range(3):
            row = g_ref[x, :, v * 128 : (v + 1) * 128].astype(F32)
            turned = pltpu.roll(row, BLK, 1)
            first = jnp.where(low, row, turned).astype(BF)
            second = jnp.where(low, turned, row).astype(BF)
            if v < 2:
                twice[3 * x, pl.ds(v * pad, deep), :] = first
                twice[3 * x + 1, pl.ds(v * pad, deep), :] = second
            else:
                twice[3 * x + 2, pl.ds(0, deep), :] = first
                twice[3 * x + 2, pl.ds(pad, deep), :] = second
        return carry

    lax.fori_loop(0, nx, split, 0, unroll=8)
    low_both = low_half((2 * pad, 128))

    def block(k, carry):
        fetch(w_hbm, held, sems, k).wait()
        row = owner[k] * planes
        start = k * 3 * planes
        for x in range(planes):
            outs = []
            for b in range(3):
                t = start + 3 * x + b
                both = jnp.where(low_both, twice[links[2 * t]], twice[links[2 * t + 1]])
                outs.append(
                    lax.dot_general(
                        both, held[t], (((1,), (1,)), ((), ())), preferred_element_type=F32
                    )
                )
            a, b, c = outs
            re = jnp.concatenate([a[:deep], b[:deep]], axis=1)
            im = jnp.concatenate([a[pad : pad + deep], b[pad : pad + deep]], axis=1)
            rest = jnp.concatenate([c[:deep], c[pad : pad + deep]], axis=1)
            o_ref[row + x, :, 0:128] = re
            o_ref[row + x, :, 128:256] = im
            o_ref[row + x, :, 256:384] = rest
        return carry

    lax.fori_loop(0, count, block, 0)


def warp(columns, weights, links, owner):
    nx, deep, _ = columns.shape
    blocks = weights.shape[0]
    pad = max(16, deep)
    whole = pl.BlockSpec((nx, deep, LANES), lambda i, l, p: (0, 0, 0))
    return pl.pallas_call(
        functools.partial(warp_kernel, nx, deep, pad),
        out_shape=jax.ShapeDtypeStruct((nx, deep, LANES), F32),
        grid_spec=pltpu.PrefetchScalarGridSpec(
            num_scalar_prefetch=2,
            grid=(1,),
            in_specs=[whole, pl.BlockSpec(memory_space=pl.ANY)],
            out_specs=whole,
            scratch_shapes=[
                pltpu.VMEM((blocks, BLK, 2 * BLK), BF),
                pltpu.VMEM((blocks, 2 * pad, 128), BF),
                pltpu.SemaphoreType.DMA((owner.shape[0],)),
            ],
        ),
        compiler_params=params(),
        cost_estimate=pl.CostEstimate(
            flops=2 * blocks * 256 * 256 * 32, bytes_accessed=20 << 20, transcendentals=0
        ),
        name="warp",
    )(links, owner, columns, weights)


def spread_kernel(nx, deep, pad, links, owner, c_ref, w_hbm, o_ref, held, total, sems):
    fetch_all(w_hbm, held, sems)
    count = sems.shape[0]
    planes = nx // count

    def clear(i, carry):
        total[pl.ds(i * 3, 3)] = jnp.zeros((3, 2 * pad, 128), F32)
        return carry

    lax.fori_loop(0, nx, clear, 0, unroll=8)
    low = low_half((2 * pad, 128))

    def tall(a, b):
        if deep == pad:
            return jnp.concatenate([a, b], axis=0)
        fill = jnp.zeros((pad - deep, a.shape[1]), a.dtype)
        return jnp.concatenate([a, fill, b, fill], axis=0)

    def block(k, carry):
        fetch(w_hbm, held, sems, k).wait()
        row = owner[k] * planes
        start = k * 3 * planes
        for x in range(planes):
            re, im, rest = (c_ref[row + x, :, v * 128 : (v + 1) * 128] for v in range(3))
            tiles = (
                tall(re[:, :BLK], im[:, :BLK]),
                tall(re[:, BLK:], im[:, BLK:]),
                tall(rest[:, :BLK], rest[:, BLK:]),
            )
            for b in range(3):
                t = start + 3 * x + b
                out = jnp.dot(tiles[b].astype(BF), held[t], preferred_element_type=F32)
                zero = jnp.zeros_like(out)
                total[links[2 * t]] += jnp.where(low, out, zero)
                total[links[2 * t + 1]] += jnp.where(low, zero, out)
        return carry

    lax.fori_loop(0, count, block, 0)
    low_row = low_half((deep, 128))

    def gather(x, carry):
        sums = []
        for b in range(3):
            value = total[3 * x + b]
            sums.append(value + pltpu.roll(value, BLK, 1))
        a, b, c = sums
        o_ref[x, :, 0:128] = jnp.where(low_row, a[:deep], b[:deep]).astype(BF)
        o_ref[x, :, 128:256] = jnp.where(
            low_row, a[pad : pad + deep], b[pad : pad + deep]
        ).astype(BF)
        o_ref[x, :, 256:384] = jnp.where(low_row, c[:deep], c[pad : pad + deep]).astype(BF)
        return carry

    lax.fori_loop(0, nx, gather, 0, unroll=8)


def spread(combined, weights, links, owner):
    nx, deep, _ = combined.shape
    blocks = weights.shape[0]
    pad = max(8, deep)
    whole = pl.BlockSpec((nx, deep, LANES), lambda i, l, p: (0, 0, 0))
    return pl.pallas_call(
        functools.partial(spread_kernel, nx, deep, pad),
        out_shape=jax.ShapeDtypeStruct((nx, deep, LANES), BF),
        grid_spec=pltpu.PrefetchScalarGridSpec(
            num_scalar_prefetch=2,
            grid=(1,),
            in_specs=[whole, pl.BlockSpec(memory_space=pl.ANY)],
            out_specs=whole,
            scratch_shapes=[
                pltpu.VMEM((blocks, BLK, 2 * BLK), BF),
                pltpu.VMEM((blocks, 2 * pad, 128), F32),
                pltpu.SemaphoreType.DMA((owner.shape[0],)),
            ],
        ),
        compiler_params=params(),
        cost_estimate=pl.CostEstimate(
            flops=2 * blocks * 256 * 256 * 32, bytes_accessed=20 << 20, transcendentals=0
        ),
        name="spread",
    )(links, owner, combined, weights)


def coil_kernel(nx, deep, pad, fresh, *refs):
    if fresh:
        s_ref, w_ref, mask, iy, fx, bx, oy, o_ref, rows = refs
    else:
        s_ref, w_ref, mask, iy, fx, bx, oy, before, o_ref, rows = refs
    group = 8 if nx % 8 == 0 else 1
    cube = rows.reshape(3, nx, pad, 128)
    low = low_half((group, deep, 128))

    def thirds(ref, at):
        return tuple(ref[at, :, v * 128 : (v + 1) * 128].astype(F32) for v in range(3))

    def expand(i, carry):
        at = pl.ds(i * group, group)
        s0, s1, s2 = thirds(s_ref.at[:, 0], at)
        w0, w1, w2 = thirds(w_ref, at)
        turned = pltpu.roll(s2, BLK, 2)
        other = pltpu.roll(w2, BLK, 2)
        real = jnp.where(low, s2, turned)
        imag = jnp.where(low, turned, s2)
        cube[0, at, pl.ds(0, deep), :] = s0 * w0 - s1 * w1
        cube[1, at, pl.ds(0, deep), :] = s0 * w1 + s1 * w0
        cube[2, at, pl.ds(0, deep), :] = real * w2 + imag * jnp.where(low, -other, other)
        return carry

    lax.fori_loop(0, nx // group, expand, 0, unroll=4)

    batch = 4 if deep % 4 == 0 else 1

    def column(i, carry):
        ats = [pl.ds(i * batch + b, nx, stride=pad) for b in range(batch)]
        line = jnp.concatenate(
            [jnp.concatenate([rows[v, at, :] for v in range(3)], axis=1) for at in ats], axis=0
        ).astype(BF)
        y = jnp.dot(line, iy[...], preferred_element_type=F32).astype(BF)
        y = jnp.concatenate(
            [
                jnp.concatenate([y[b * nx : (b + 1) * nx, h * HALF : (h + 1) * HALF] for b in range(batch)], axis=1)
                for h in range(2)
            ],
            axis=0,
        )
        y = jnp.dot(fx[...], y, preferred_element_type=F32)
        y = jnp.concatenate([(y[:, b * HALF : (b + 1) * HALF] * mask[...]).astype(BF) for b in range(batch)], axis=1)
        y = jnp.dot(bx[...], y, preferred_element_type=F32).astype(BF)
        y = jnp.concatenate(
            [
                jnp.concatenate([y[h * nx : (h + 1) * nx, b * HALF : (b + 1) * HALF] for h in range(2)], axis=1)
                for b in range(batch)
            ],
            axis=0,
        )
        y = jnp.dot(y, oy[...], preferred_element_type=F32)
        for b, at in enumerate(ats):
            for v in range(3):
                rows[v, at, :] = y[b * nx : (b + 1) * nx, v * 128 : (v + 1) * 128]
        return carry

    lax.fori_loop(0, deep // batch, column, 0)

    first = pl.program_id(0) == 0

    def combine(i, carry):
        at = pl.ds(i * group, group)
        s0, s1, s2 = thirds(s_ref.at[:, 0], at)
        r0, r1, r2 = (cube[v, at, pl.ds(0, deep), :] for v in range(3))
        turned = pltpu.roll(s2, BLK, 2)
        other = pltpu.roll(r2, BLK, 2)
        real = jnp.where(low, s2, turned)
        imag = jnp.where(low, turned, s2)
        terms = (
            s0 * r0 + s1 * r1,
            s0 * r1 - s1 * r0,
            real * r2 + imag * jnp.where(low, other, -other),
        )
        for v in range(3):
            lanes = slice(v * 128, (v + 1) * 128)
            old = o_ref[at, :, lanes]
            start = jnp.zeros_like(old) if fresh else before[at, :, lanes]
            o_ref[at, :, lanes] = jnp.where(first, start, old) + terms[v]
        return carry

    lax.fori_loop(0, nx // group, combine, 0, unroll=4)


def coils(maps, warped, mask, tabs, before, part):
    nx, count, deep, _ = maps.shape
    pad = max(8, deep)
    fresh = before is None
    whole = lambda shape: pl.BlockSpec(
        shape, lambda c: (0,) * len(shape), pipeline_mode=pl.Buffered(1)
    )
    in_specs = [pl.BlockSpec((nx, 1, deep, LANES), lambda c: (0, c, 0, 0))]
    args = [maps, warped, mask, *tabs] + ([] if fresh else [before])
    def columns(array):
        at = part if array.shape[1] > deep else 0
        return pl.BlockSpec(
            (nx, deep, LANES), lambda c: (0, at, 0), pipeline_mode=pl.Buffered(1)
        )

    in_specs += [columns(warped)] + [whole(a.shape) for a in (mask, *tabs)]
    in_specs += [] if fresh else [columns(before)]
    return pl.pallas_call(
        functools.partial(coil_kernel, nx, deep, pad, fresh),
        out_shape=jax.ShapeDtypeStruct((nx, deep, LANES), F32),
        grid=(count,),
        in_specs=in_specs,
        out_specs=pl.BlockSpec((nx, deep, LANES), lambda c: (0, 0, 0)),
        scratch_shapes=[pltpu.VMEM((3, nx * pad, 128), F32)],
        compiler_params=params(),
        cost_estimate=pl.CostEstimate(
            flops=count * deep * 4 * 8 * nx * nx * 192 * 2,
            bytes_accessed=count * nx * deep * LANES * 2 + (14 << 20),
            transcendentals=0,
        ),
        name="coils",
    )(*args)


def update_kernel(count, parts, *refs):
    backs = refs[:parts]
    i_ref, a_ref, o_ref, scratch = refs[parts:]
    part = backs[0].shape[2]
    for x in range(o_ref.shape[1]):
        for h, back in enumerate(backs):
            for d in range(count):
                scratch[x, pl.ds((d * parts + h) * part, part), :] = back[d, x].astype(F32)
        grad = scratch[x].astype(BF).T.astype(F32)
        real = jnp.concatenate([grad[0:128], grad[256:320]], axis=0)
        imag = jnp.concatenate([grad[128:256], grad[320:384]], axis=0)
        for p, value in enumerate((real, imag)):
            o_ref[p, x] = i_ref[p, x] - 0.5 * (value - a_ref[p, x].astype(F32))


def update(backs, image, adjoint):
    parts = len(backs)
    count, planes, part, _ = backs[0].shape
    _, _, ny, nz = image.shape
    group = 3 if planes % 3 == 0 else 1
    block = pl.BlockSpec((2, group, ny, nz), lambda x: (0, x, 0, 0))
    back = pl.BlockSpec((count, group, part, LANES), lambda x: (0, x, 0, 0))
    return pl.pallas_call(
        functools.partial(update_kernel, count, parts),
        out_shape=jax.ShapeDtypeStruct(image.shape, F32),
        grid=(planes // group,),
        in_specs=[back] * parts + [block, block],
        out_specs=block,
        scratch_shapes=[pltpu.VMEM((group, nz, LANES), F32)],
        compiler_params=params(),
        cost_estimate=pl.CostEstimate(flops=0, bytes_accessed=image.size * 12, transcendentals=0),
        name="update",
    )(*backs, image, adjoint)


def exchange(parts):
    return lax.all_to_all(parts, "slab", split_axis=0, concat_axis=0, tiled=True)


def after(value, *others):
    return lax.optimization_barrier((value, *others))[0]


def gather_doubling(value):
    count = lax.axis_size("slab")
    order = [0]
    bit = count // 2
    while bit:
        other = lax.ppermute(value, "slab", [(i, i ^ bit) for i in range(count)])
        value = jnp.concatenate([value, other], axis=0)
        order += [k ^ bit for k in order]
        bit //= 2
    return value, jnp.asarray(order, jnp.int32) ^ lax.axis_index("slab")


def per_device(image, adjoint_data, coil_maps, masks, sources, weights):
    count = lax.axis_size("slab")
    planes, ny, nz = image.shape[1:]
    nx = planes * count
    deep = nz // count
    total = coil_maps.shape[0]
    tabs = tables(nx, ny)
    sampled = jnp.pad(masks[0].astype(F32), ((0, 0), (0, HALF - ny)))
    mask = jnp.concatenate([sampled, sampled], axis=0)

    matrices = weights[0].reshape(3 * planes, 2, BLK, BLK)
    matrices = jnp.transpose(matrices, (0, 2, 1, 3)).reshape(3 * planes, BLK, 2 * BLK)
    digits = jnp.concatenate([sources[0] // BLK, sources[0] % BLK], axis=1).astype(BF)
    digits = jnp.pad(digits[:, None, :], ((0, 0), (0, 7), (0, 2 * BLK - 4)))
    packed, owner = gather_doubling(jnp.concatenate([matrices, digits], axis=1))
    digits = packed[:, BLK, :4].astype(jnp.int32)
    links = (digits[:, :2] * BLK + digits[:, 2:]).reshape(-1)

    columns = exchange(image_columns(image, count))
    halves = deep % 16 == 0
    sizes = [total // 2, total // 4] if halves else [total // 2, total // 4, total // 8]
    sizes += [] if halves else [total - sum(sizes)]
    outgoing = []
    for i, size in enumerate(sizes):
        outgoing.append(maps_columns(coil_maps, count, sum(sizes[:i]), size))
    last = columns
    warped = warp(columns.reshape(nx, deep, LANES), packed, links, owner)

    def run(received, before, part):
        size = received.shape[2]
        return coils(received.reshape(nx, size, -1, LANES), warped, mask, tabs, before, part)

    def back(combined, *needs):
        grad = spread(combined, packed, links, owner)
        return exchange(after(grad, *needs).reshape(count, planes, -1, LANES))

    combined, waiting, ready = None, None, []
    for piece in outgoing:
        arrived = exchange(after(piece, last, *ready))
        if waiting is not None:
            combined = run(waiting, combined, 0)
            ready = [combined]
        last = waiting = arrived
    if not halves:
        combined = run(waiting, combined, 0)
        return update([back(combined)], image, adjoint_data)

    both, first, second = last_maps_columns(coil_maps, count, sum(sizes))
    got_both = exchange(after(both, last, *ready))
    combined = run(waiting, combined, 0)
    got_first = exchange(after(first, got_both, combined))
    half = run(got_both, combined, 0)
    back_first = back(half, got_first)
    half = run(got_first, combined, 1)
    got_second = exchange(after(second, back_first, half))
    half = run(got_second, half, 1)
    return update([back_first, back(half)], image, adjoint_data)


def solution(mesh):
    return jax.shard_map(
        per_device,
        mesh=mesh,
        in_specs=(
            P(None, ("grp", "slab"), None, None),
            P(None, ("grp", "slab"), None, None),
            P(None, None, ("grp", "slab"), None, None),
            P(None, "grp", None),
            P(None, ("grp", "slab"), None),
            P(None, ("grp", "slab"), None),
        ),
        out_specs=P(None, ("grp", "slab"), None, None),
        check_vma=False,
    )
```

```python
import functools
import math

import jax
import jax.numpy as jnp
import numpy as np
from jax import lax
from jax.experimental import pallas as pl
from jax.experimental.pallas import tpu as pltpu
from jax.sharding import PartitionSpec as P

BLK = 64
LANES = 384
HALF = 256
VMEM_LIMIT = 56 * 1024 * 1024
BF = jnp.bfloat16
F32 = jnp.float32


def lane_order(length):
    lo, rest = 128, length - 128
    part = np.concatenate([np.zeros(lo), np.ones(lo), np.zeros(rest), np.ones(rest)])
    pos = np.concatenate([np.arange(lo), np.arange(lo), lo + np.arange(rest), lo + np.arange(rest)])
    return part.astype(np.int32), pos.astype(np.int32)


def dft_table(length, direction):
    positions = np.arange(length)
    phases = (positions[:, None] * positions[None, :] % length).astype(np.float32)
    phases = phases * np.float32(2.0 * math.pi / length)
    factor = np.float32(1.0 / math.sqrt(length))
    cosine = np.cos(phases) * factor
    sine = np.sin(phases) * (np.float32(direction) * factor)
    upper = np.stack([cosine, -sine], axis=1)
    lower = np.stack([sine, cosine], axis=1)
    return np.stack([upper, lower], axis=0)


def tables(nx, ny):
    part, pos = lane_order(ny)
    fwd_y, inv_y = dft_table(ny, -1.0), dft_table(ny, 1.0)
    into_y = np.zeros((2 * ny, 2, HALF), np.float32)
    into_y[:, :, :ny] = np.transpose(fwd_y[:, :, part, pos], (2, 0, 1))
    from_y = np.zeros((2, HALF, 2 * ny), np.float32)
    from_y[:, :ny, :] = np.transpose(inv_y[part, pos], (1, 2, 0))
    fwd_x = dft_table(nx, -1.0).reshape(2 * nx, 2 * nx)
    inv_x = dft_table(nx, 1.0).reshape(2 * nx, 2 * nx)
    out = (into_y.reshape(2 * ny, 2 * HALF), fwd_x, inv_x, from_y.reshape(2 * HALF, 2 * ny))
    return tuple(jnp.asarray(t, BF) for t in out)


def params():
    return pltpu.CompilerParams(vmem_limit_bytes=VMEM_LIMIT)


def to_rows(parts):
    stacked = jnp.concatenate(
        [parts[0, :128], parts[1, :128], parts[0, 128:], parts[1, 128:]], axis=0
    )
    return stacked.T


def spread_rows(outs, rows, scratch, count, deep):
    if len(outs) == 1 and deep % 16 == 0:
        outs[0][...] = rows.reshape(count, deep, LANES)
        return
    part = deep // len(outs)
    scratch[...] = rows.astype(F32)
    for h, out in enumerate(outs):
        for d in range(count):
            out[d] = scratch[pl.ds(d * deep + h * part, part), :].astype(BF)


def image_kernel(count, deep, x_ref, o_ref, scratch):
    for x in range(x_ref.shape[1]):
        rows = to_rows(x_ref[:, x].astype(BF))
        spread_rows([o_ref.at[:, x]], rows, scratch, count, deep)


def image_columns(image, count):
    _, planes, ny, nz = image.shape
    deep = nz // count
    group = 3 if planes % 3 == 0 else 1
    return pl.pallas_call(
        functools.partial(image_kernel, count, deep),
        out_shape=jax.ShapeDtypeStruct((count, planes, deep, LANES), BF),
        grid=(planes // group,),
        in_specs=[pl.BlockSpec((2, group, ny, nz), lambda x: (0, x, 0, 0))],
        out_specs=pl.BlockSpec((count, group, deep, LANES), lambda x: (0, x, 0, 0)),
        scratch_shapes=[pltpu.VMEM((nz, LANES), F32)],
        compiler_params=params(),
        cost_estimate=pl.CostEstimate(flops=0, bytes_accessed=image.size * 6, transcendentals=0),
        name="image_columns",
    )(image)


def maps_kernel(count, deep, x_ref, o_ref, scratch):
    spread_rows([o_ref.at[:, 0, 0]], to_rows(x_ref[0, :, 0]), scratch, count, deep)


def last_maps_kernel(count, deep, x_ref, both_ref, first_ref, second_ref, scratch):
    part = deep // 2
    scratch[...] = to_rows(x_ref[0, :, 0]).astype(F32)
    coil = pl.program_id(1)
    for d in range(count):
        both_ref[d, 0, 0] = scratch[pl.ds(d * deep, part), :].astype(BF)

    def rest(out):
        for d in range(count):
            out[d, 0, 0] = scratch[pl.ds(d * deep + part, part), :].astype(BF)

    @pl.when(coil == 0)
    def _():
        rest(first_ref)

    @pl.when(coil == 1)
    def _():
        rest(second_ref)


def maps_columns(coil_maps, count, first, coils):
    _, _, planes, ny, nz = coil_maps.shape
    deep = nz // count
    return pl.pallas_call(
        functools.partial(maps_kernel, count, deep),
        out_shape=jax.ShapeDtypeStruct((count, planes, coils, deep, LANES), BF),
        grid=(planes, coils),
        in_specs=[pl.BlockSpec((1, 2, 1, ny, nz), lambda x, c: (first + c, 0, x, 0, 0))],
        out_specs=pl.BlockSpec((count, 1, 1, deep, LANES), lambda x, c: (0, x, c, 0, 0)),
        scratch_shapes=[pltpu.VMEM((nz, LANES), F32)],
        compiler_params=params(),
        cost_estimate=pl.CostEstimate(
            flops=0, bytes_accessed=coils * 2 * planes * ny * nz * 4, transcendentals=0
        ),
        name="maps_columns",
    )(coil_maps)


def last_maps_columns(coil_maps, count, first):
    _, _, planes, ny, nz = coil_maps.shape
    deep = nz // count
    part = deep // 2
    shapes = [(count, planes, coils, part, LANES) for coils in (2, 1, 1)]
    alone = pl.BlockSpec((count, 1, 1, part, LANES), lambda x, c: (0, x, 0, 0, 0))
    return pl.pallas_call(
        functools.partial(last_maps_kernel, count, deep),
        out_shape=[jax.ShapeDtypeStruct(shape, BF) for shape in shapes],
        grid=(planes, 2),
        in_specs=[pl.BlockSpec((1, 2, 1, ny, nz), lambda x, c: (first + c, 0, x, 0, 0))],
        out_specs=[
            pl.BlockSpec((count, 1, 1, part, LANES), lambda x, c: (0, x, c, 0, 0)),
            alone,
            alone,
        ],
        scratch_shapes=[pltpu.VMEM((nz, LANES), F32)],
        compiler_params=params(),
        cost_estimate=pl.CostEstimate(
            flops=0, bytes_accessed=4 * planes * ny * nz * 4, transcendentals=0
        ),
        name="last_maps_columns",
    )(coil_maps)


def low_half(shape):
    return lax.broadcasted_iota(jnp.int32, shape, len(shape) - 1) < BLK


def fetch(w_hbm, held, sems, k):
    size = held.shape[0] // sems.shape[0]
    at = pl.ds(k * size, size)
    return pltpu.make_async_copy(w_hbm.at[at, pl.ds(0, BLK), :], held.at[at], sems.at[k])


def fetch_all(w_hbm, held, sems):
    for k in range(sems.shape[0]):
        fetch(w_hbm, held, sems, k).start()


def warp_kernel(nx, deep, pad, links, owner, g_ref, w_hbm, o_ref, held, twice, sems):
    fetch_all(w_hbm, held, sems)
    count = sems.shape[0]
    planes = nx // count
    low = low_half((deep, 128))

    def split(x, carry):
        for v in range(3):
            row = g_ref[x, :, v * 128 : (v + 1) * 128].astype(F32)
            turned = pltpu.roll(row, BLK, 1)
            first = jnp.where(low, row, turned).astype(BF)
            second = jnp.where(low, turned, row).astype(BF)
            if v < 2:
                twice[3 * x, pl.ds(v * pad, deep), :] = first
                twice[3 * x + 1, pl.ds(v * pad, deep), :] = second
            else:
                twice[3 * x + 2, pl.ds(0, deep), :] = first
                twice[3 * x + 2, pl.ds(pad, deep), :] = second
        return carry

    lax.fori_loop(0, nx, split, 0, unroll=8)
    low_both = low_half((2 * pad, 128))

    def block(k, carry):
        fetch(w_hbm, held, sems, k).wait()
        row = owner[k] * planes
        start = k * 3 * planes
        for x in range(planes):
            outs = []
            for b in range(3):
                t = start + 3 * x + b
                both = jnp.where(low_both, twice[links[2 * t]], twice[links[2 * t + 1]])
                outs.append(
                    lax.dot_general(
                        both, held[t], (((1,), (1,)), ((), ())), preferred_element_type=F32
                    )
                )
            a, b, c = outs
            re = jnp.concatenate([a[:deep], b[:deep]], axis=1)
            im = jnp.concatenate([a[pad : pad + deep], b[pad : pad + deep]], axis=1)
            rest = jnp.concatenate([c[:deep], c[pad : pad + deep]], axis=1)
            o_ref[row + x, :, 0:128] = re
            o_ref[row + x, :, 128:256] = im
            o_ref[row + x, :, 256:384] = rest
        return carry

    lax.fori_loop(0, count, block, 0)


def warp(columns, weights, links, owner):
    nx, deep, _ = columns.shape
    blocks = weights.shape[0]
    pad = max(16, deep)
    whole = pl.BlockSpec((nx, deep, LANES), lambda i, l, p: (0, 0, 0))
    return pl.pallas_call(
        functools.partial(warp_kernel, nx, deep, pad),
        out_shape=jax.ShapeDtypeStruct((nx, deep, LANES), F32),
        grid_spec=pltpu.PrefetchScalarGridSpec(
            num_scalar_prefetch=2,
            grid=(1,),
            in_specs=[whole, pl.BlockSpec(memory_space=pl.ANY)],
            out_specs=whole,
            scratch_shapes=[
                pltpu.VMEM((blocks, BLK, 2 * BLK), BF),
                pltpu.VMEM((blocks, 2 * pad, 128), BF),
                pltpu.SemaphoreType.DMA((owner.shape[0],)),
            ],
        ),
        compiler_params=params(),
        cost_estimate=pl.CostEstimate(
            flops=2 * blocks * 256 * 256 * 32, bytes_accessed=20 << 20, transcendentals=0
        ),
        name="warp",
    )(links, owner, columns, weights)


def spread_kernel(nx, deep, pad, links, owner, c_ref, w_hbm, o_ref, held, total, sems):
    fetch_all(w_hbm, held, sems)
    count = sems.shape[0]
    planes = nx // count

    def clear(i, carry):
        total[pl.ds(i * 3, 3)] = jnp.zeros((3, 2 * pad, 128), F32)
        return carry

    lax.fori_loop(0, nx, clear, 0, unroll=8)
    low = low_half((2 * pad, 128))

    def tall(a, b):
        if deep == pad:
            return jnp.concatenate([a, b], axis=0)
        fill = jnp.zeros((pad - deep, a.shape[1]), a.dtype)
        return jnp.concatenate([a, fill, b, fill], axis=0)

    def block(k, carry):
        fetch(w_hbm, held, sems, k).wait()
        row = owner[k] * planes
        start = k * 3 * planes
        for x in range(planes):
            re, im, rest = (c_ref[row + x, :, v * 128 : (v + 1) * 128] for v in range(3))
            tiles = (
                tall(re[:, :BLK], im[:, :BLK]),
                tall(re[:, BLK:], im[:, BLK:]),
                tall(rest[:, :BLK], rest[:, BLK:]),
            )
            for b in range(3):
                t = start + 3 * x + b
                out = jnp.dot(tiles[b].astype(BF), held[t], preferred_element_type=F32)
                zero = jnp.zeros_like(out)
                total[links[2 * t]] += jnp.where(low, out, zero)
                total[links[2 * t + 1]] += jnp.where(low, zero, out)
        return carry

    lax.fori_loop(0, count, block, 0)
    low_row = low_half((deep, 128))

    def gather(x, carry):
        sums = []
        for b in range(3):
            value = total[3 * x + b]
            sums.append(value + pltpu.roll(value, BLK, 1))
        a, b, c = sums
        o_ref[x, :, 0:128] = jnp.where(low_row, a[:deep], b[:deep]).astype(BF)
        o_ref[x, :, 128:256] = jnp.where(
            low_row, a[pad : pad + deep], b[pad : pad + deep]
        ).astype(BF)
        o_ref[x, :, 256:384] = jnp.where(low_row, c[:deep], c[pad : pad + deep]).astype(BF)
        return carry

    lax.fori_loop(0, nx, gather, 0, unroll=8)


def spread(combined, weights, links, owner):
    nx, deep, _ = combined.shape
    blocks = weights.shape[0]
    pad = max(8, deep)
    whole = pl.BlockSpec((nx, deep, LANES), lambda i, l, p: (0, 0, 0))
    return pl.pallas_call(
        functools.partial(spread_kernel, nx, deep, pad),
        out_shape=jax.ShapeDtypeStruct((nx, deep, LANES), BF),
        grid_spec=pltpu.PrefetchScalarGridSpec(
            num_scalar_prefetch=2,
            grid=(1,),
            in_specs=[whole, pl.BlockSpec(memory_space=pl.ANY)],
            out_specs=whole,
            scratch_shapes=[
                pltpu.VMEM((blocks, BLK, 2 * BLK), BF),
                pltpu.VMEM((blocks, 2 * pad, 128), F32),
                pltpu.SemaphoreType.DMA((owner.shape[0],)),
            ],
        ),
        compiler_params=params(),
        cost_estimate=pl.CostEstimate(
            flops=2 * blocks * 256 * 256 * 32, bytes_accessed=20 << 20, transcendentals=0
        ),
        name="spread",
    )(links, owner, combined, weights)


def coil_kernel(nx, deep, pad, fresh, *refs):
    if fresh:
        s_ref, w_ref, mask, iy, fx, bx, oy, o_ref, rows = refs
    else:
        s_ref, w_ref, mask, iy, fx, bx, oy, before, o_ref, rows = refs
    group = 8 if nx % 8 == 0 else 1
    cube = rows.reshape(3, nx, pad, 128)
    low = low_half((group, deep, 128))

    def thirds(ref, at):
        return tuple(ref[at, :, v * 128 : (v + 1) * 128].astype(F32) for v in range(3))

    def expand(i, carry):
        at = pl.ds(i * group, group)
        s0, s1, s2 = thirds(s_ref.at[:, 0], at)
        w0, w1, w2 = thirds(w_ref, at)
        turned = pltpu.roll(s2, BLK, 2)
        other = pltpu.roll(w2, BLK, 2)
        real = jnp.where(low, s2, turned)
        imag = jnp.where(low, turned, s2)
        cube[0, at, pl.ds(0, deep), :] = s0 * w0 - s1 * w1
        cube[1, at, pl.ds(0, deep), :] = s0 * w1 + s1 * w0
        cube[2, at, pl.ds(0, deep), :] = real * w2 + imag * jnp.where(low, -other, other)
        return carry

    lax.fori_loop(0, nx // group, expand, 0, unroll=4)

    batch = 4 if deep % 4 == 0 else 1

    def column(i, carry):
        ats = [pl.ds(i * batch + b, nx, stride=pad) for b in range(batch)]
        line = jnp.concatenate(
            [jnp.concatenate([rows[v, at, :] for v in range(3)], axis=1) for at in ats], axis=0
        ).astype(BF)
        y = jnp.dot(line, iy[...], preferred_element_type=F32).astype(BF)
        y = jnp.concatenate(
            [
                jnp.concatenate([y[b * nx : (b + 1) * nx, h * HALF : (h + 1) * HALF] for b in range(batch)], axis=1)
                for h in range(2)
            ],
            axis=0,
        )
        y = jnp.dot(fx[...], y, preferred_element_type=F32)
        y = jnp.concatenate([(y[:, b * HALF : (b + 1) * HALF] * mask[...]).astype(BF) for b in range(batch)], axis=1)
        y = jnp.dot(bx[...], y, preferred_element_type=F32).astype(BF)
        y = jnp.concatenate(
            [
                jnp.concatenate([y[h * nx : (h + 1) * nx, b * HALF : (b + 1) * HALF] for h in range(2)], axis=1)
                for b in range(batch)
            ],
            axis=0,
        )
        y = jnp.dot(y, oy[...], preferred_element_type=F32)
        for b, at in enumerate(ats):
            for v in range(3):
                rows[v, at, :] = y[b * nx : (b + 1) * nx, v * 128 : (v + 1) * 128]
        return carry

    lax.fori_loop(0, deep // batch, column, 0)

    first = pl.program_id(0) == 0

    def combine(i, carry):
        at = pl.ds(i * group, group)
        s0, s1, s2 = thirds(s_ref.at[:, 0], at)
        r0, r1, r2 = (cube[v, at, pl.ds(0, deep), :] for v in range(3))
        turned = pltpu.roll(s2, BLK, 2)
        other = pltpu.roll(r2, BLK, 2)
        real = jnp.where(low, s2, turned)
        imag = jnp.where(low, turned, s2)
        terms = (
            s0 * r0 + s1 * r1,
            s0 * r1 - s1 * r0,
            real * r2 + imag * jnp.where(low, other, -other),
        )
        for v in range(3):
            lanes = slice(v * 128, (v + 1) * 128)
            old = o_ref[at, :, lanes]
            start = jnp.zeros_like(old) if fresh else before[at, :, lanes]
            o_ref[at, :, lanes] = jnp.where(first, start, old) + terms[v]
        return carry

    lax.fori_loop(0, nx // group, combine, 0, unroll=4)


def coils(maps, warped, mask, tabs, before, part):
    nx, count, deep, _ = maps.shape
    pad = max(8, deep)
    fresh = before is None
    whole = lambda shape: pl.BlockSpec(
        shape, lambda c: (0,) * len(shape), pipeline_mode=pl.Buffered(1)
    )
    in_specs = [pl.BlockSpec((nx, 1, deep, LANES), lambda c: (0, c, 0, 0))]
    args = [maps, warped, mask, *tabs] + ([] if fresh else [before])
    def columns(array):
        at = part if array.shape[1] > deep else 0
        return pl.BlockSpec(
            (nx, deep, LANES), lambda c: (0, at, 0), pipeline_mode=pl.Buffered(1)
        )

    in_specs += [columns(warped)] + [whole(a.shape) for a in (mask, *tabs)]
    in_specs += [] if fresh else [columns(before)]
    return pl.pallas_call(
        functools.partial(coil_kernel, nx, deep, pad, fresh),
        out_shape=jax.ShapeDtypeStruct((nx, deep, LANES), F32),
        grid=(count,),
        in_specs=in_specs,
        out_specs=pl.BlockSpec((nx, deep, LANES), lambda c: (0, 0, 0)),
        scratch_shapes=[pltpu.VMEM((3, nx * pad, 128), F32)],
        compiler_params=params(),
        cost_estimate=pl.CostEstimate(
            flops=count * deep * 4 * 8 * nx * nx * 192 * 2,
            bytes_accessed=count * nx * deep * LANES * 2 + (14 << 20),
            transcendentals=0,
        ),
        name="coils",
    )(*args)


def update_kernel(count, parts, *refs):
    backs = refs[:parts]
    i_ref, a_ref, o_ref, scratch = refs[parts:]
    part = backs[0].shape[2]
    for x in range(o_ref.shape[1]):
        for h, back in enumerate(backs):
            for d in range(count):
                scratch[x, pl.ds((d * parts + h) * part, part), :] = back[d, x].astype(F32)
        grad = scratch[x].astype(BF).T.astype(F32)
        real = jnp.concatenate([grad[0:128], grad[256:320]], axis=0)
        imag = jnp.concatenate([grad[128:256], grad[320:384]], axis=0)
        for p, value in enumerate((real, imag)):
            o_ref[p, x] = i_ref[p, x] - 0.5 * (value - a_ref[p, x].astype(F32))


def update(backs, image, adjoint):
    parts = len(backs)
    count, planes, part, _ = backs[0].shape
    _, _, ny, nz = image.shape
    group = 3 if planes % 3 == 0 else 1
    block = pl.BlockSpec((2, group, ny, nz), lambda x: (0, x, 0, 0))
    back = pl.BlockSpec((count, group, part, LANES), lambda x: (0, x, 0, 0))
    return pl.pallas_call(
        functools.partial(update_kernel, count, parts),
        out_shape=jax.ShapeDtypeStruct(image.shape, F32),
        grid=(planes // group,),
        in_specs=[back] * parts + [block, block],
        out_specs=block,
        scratch_shapes=[pltpu.VMEM((group, nz, LANES), F32)],
        compiler_params=params(),
        cost_estimate=pl.CostEstimate(flops=0, bytes_accessed=image.size * 12, transcendentals=0),
        name="update",
    )(*backs, image, adjoint)


def exchange(parts):
    return lax.all_to_all(parts, "slab", split_axis=0, concat_axis=0, tiled=True)


def after(value, *others):
    return lax.optimization_barrier((value, *others))[0]


def swap_halves(value):
    count = lax.axis_size("slab")
    half = count // 2
    other = lax.ppermute(value, "slab", [(i, i ^ half) for i in range(count)])
    return jnp.concatenate([value, other], axis=0)


def gather_half(pair):
    count = lax.axis_size("slab")
    half = count // 2
    groups = [list(range(half)), list(range(half, count))]
    gathered = lax.all_gather(pair, "slab", axis=0, tiled=True, axis_index_groups=groups)
    mine = lax.axis_index("slab") // half
    place = jnp.arange(count, dtype=jnp.int32)
    return gathered, place // 2 + half * ((place % 2) ^ mine)


def per_device(image, adjoint_data, coil_maps, masks, sources, weights):
    count = lax.axis_size("slab")
    planes, ny, nz = image.shape[1:]
    nx = planes * count
    deep = nz // count
    total = coil_maps.shape[0]
    tabs = tables(nx, ny)
    sampled = jnp.pad(masks[0].astype(F32), ((0, 0), (0, HALF - ny)))
    mask = jnp.concatenate([sampled, sampled], axis=0)

    matrices = weights[0].reshape(3 * planes, 2, BLK, BLK)
    matrices = jnp.transpose(matrices, (0, 2, 1, 3)).reshape(3 * planes, BLK, 2 * BLK)
    digits = jnp.concatenate([sources[0] // BLK, sources[0] % BLK], axis=1).astype(BF)
    digits = jnp.pad(digits[:, None, :], ((0, 0), (0, 7), (0, 2 * BLK - 4)))
    pair = swap_halves(jnp.concatenate([matrices, digits], axis=1))
    packed, owner = gather_half(pair)
    digits = packed[:, BLK, :4].astype(jnp.int32)
    links = (digits[:, :2] * BLK + digits[:, 2:]).reshape(-1)

    columns = exchange(image_columns(image, count))
    halves = deep % 16 == 0
    sizes = [total // 2, total // 4] if halves else [total // 2, total // 4, total // 8]
    sizes += [] if halves else [total - sum(sizes)]
    outgoing = []
    for i, size in enumerate(sizes):
        outgoing.append(maps_columns(coil_maps, count, sum(sizes[:i]), size))
    last = columns
    warped = warp(columns.reshape(nx, deep, LANES), packed, links, owner)

    def run(received, before, part):
        size = received.shape[2]
        return coils(received.reshape(nx, size, -1, LANES), warped, mask, tabs, before, part)

    def back(combined, *needs):
        grad = spread(combined, packed, links, owner)
        return exchange(after(grad, *needs).reshape(count, planes, -1, LANES))

    combined, waiting, ready = None, None, []
    for piece in outgoing:
        arrived = exchange(after(piece, last, pair, *ready))
        if waiting is not None:
            combined = run(waiting, combined, 0)
            ready = [combined]
        last = waiting = arrived
    if not halves:
        combined = run(waiting, combined, 0)
        return update([back(combined)], image, adjoint_data)

    both, first, second = last_maps_columns(coil_maps, count, sum(sizes))
    got_both = exchange(after(both, last, *ready))
    combined = run(waiting, combined, 0)
    got_first = exchange(after(first, got_both, combined))
    half = run(got_both, combined, 0)
    back_first = back(half, got_first)
    half = run(got_first, combined, 1)
    got_second = exchange(after(second, back_first, half))
    half = run(got_second, half, 1)
    return update([back_first, back(half)], image, adjoint_data)


def solution(mesh):
    return jax.shard_map(
        per_device,
        mesh=mesh,
        in_specs=(
            P(None, ("grp", "slab"), None, None),
            P(None, ("grp", "slab"), None, None),
            P(None, None, ("grp", "slab"), None, None),
            P(None, "grp", None),
            P(None, ("grp", "slab"), None),
            P(None, ("grp", "slab"), None),
        ),
        out_specs=P(None, ("grp", "slab"), None, None),
        check_vma=False,
    )
```

```python
import functools
import math

import jax
import jax.numpy as jnp
import numpy as np
from jax import lax
from jax.experimental import pallas as pl
from jax.experimental.pallas import tpu as pltpu
from jax.sharding import PartitionSpec as P

BLK = 64
LANES = 384
TAIL = 16
HALF = 256
VMEM_LIMIT = 56 * 1024 * 1024
BF = jnp.bfloat16
F32 = jnp.float32


def lane_order(length):
    lo, rest = 128, length - 128
    part = np.concatenate([np.zeros(lo), np.ones(lo), np.zeros(rest), np.ones(rest)])
    pos = np.concatenate([np.arange(lo), np.arange(lo), lo + np.arange(rest), lo + np.arange(rest)])
    return part.astype(np.int32), pos.astype(np.int32)


def dft_table(length, direction):
    positions = np.arange(length)
    phases = (positions[:, None] * positions[None, :] % length).astype(np.float32)
    phases = phases * np.float32(2.0 * math.pi / length)
    factor = np.float32(1.0 / math.sqrt(length))
    cosine = np.cos(phases) * factor
    sine = np.sin(phases) * (np.float32(direction) * factor)
    upper = np.stack([cosine, -sine], axis=1)
    lower = np.stack([sine, cosine], axis=1)
    return np.stack([upper, lower], axis=0)


def tables(nx, ny):
    part, pos = lane_order(ny)
    fwd_y, inv_y = dft_table(ny, -1.0), dft_table(ny, 1.0)
    into_y = np.zeros((2 * ny, 2, HALF), np.float32)
    into_y[:, :, :ny] = np.transpose(fwd_y[:, :, part, pos], (2, 0, 1))
    from_y = np.zeros((2, HALF, 2 * ny), np.float32)
    from_y[:, :ny, :] = np.transpose(inv_y[part, pos], (1, 2, 0))
    fwd_x = dft_table(nx, -1.0).reshape(2 * nx, 2 * nx)
    inv_x = dft_table(nx, 1.0).reshape(2 * nx, 2 * nx)
    out = (into_y.reshape(2 * ny, 2 * HALF), fwd_x, inv_x, from_y.reshape(2 * HALF, 2 * ny))
    return tuple(jnp.asarray(t, BF) for t in out)


def params():
    return pltpu.CompilerParams(vmem_limit_bytes=VMEM_LIMIT)


def to_rows(parts):
    stacked = jnp.concatenate(
        [parts[0, :128], parts[1, :128], parts[0, 128:], parts[1, 128:]], axis=0
    )
    return stacked.T


def spread_rows(outs, rows, scratch, count, deep):
    if len(outs) == 1 and deep % 16 == 0:
        outs[0][...] = rows.reshape(count, deep, LANES)
        return
    part = deep // len(outs)
    scratch[...] = rows.astype(F32)
    for h, out in enumerate(outs):
        for d in range(count):
            out[d] = scratch[pl.ds(d * deep + h * part, part), :].astype(BF)


def image_kernel(count, deep, x_ref, o_ref, scratch):
    for x in range(x_ref.shape[1]):
        rows = to_rows(x_ref[:, x].astype(BF))
        spread_rows([o_ref.at[:, x]], rows, scratch, count, deep)


def image_columns(image, count):
    _, planes, ny, nz = image.shape
    deep = nz // count
    group = 3 if planes % 3 == 0 else 1
    return pl.pallas_call(
        functools.partial(image_kernel, count, deep),
        out_shape=jax.ShapeDtypeStruct((count, planes, deep, LANES), BF),
        grid=(planes // group,),
        in_specs=[pl.BlockSpec((2, group, ny, nz), lambda x: (0, x, 0, 0))],
        out_specs=pl.BlockSpec((count, group, deep, LANES), lambda x: (0, x, 0, 0)),
        scratch_shapes=[pltpu.VMEM((nz, LANES), F32)],
        compiler_params=params(),
        cost_estimate=pl.CostEstimate(flops=0, bytes_accessed=image.size * 6, transcendentals=0),
        name="image_columns",
    )(image)


def maps_kernel(count, deep, x_ref, o_ref, scratch):
    spread_rows([o_ref.at[:, 0, 0]], to_rows(x_ref[0, :, 0]), scratch, count, deep)


def last_maps_kernel(count, deep, x_ref, first_ref, second_ref, scratch):
    outs = [first_ref.at[:, 0, 0], second_ref.at[:, 0, 0]]
    spread_rows(outs, to_rows(x_ref[0, :, 0]), scratch, count, deep)


def maps_columns(coil_maps, count, first, coils):
    _, _, planes, ny, nz = coil_maps.shape
    deep = nz // count
    return pl.pallas_call(
        functools.partial(maps_kernel, count, deep),
        out_shape=jax.ShapeDtypeStruct((count, planes, coils, deep, LANES), BF),
        grid=(planes, coils),
        in_specs=[pl.BlockSpec((1, 2, 1, ny, nz), lambda x, c: (first + c, 0, x, 0, 0))],
        out_specs=pl.BlockSpec((count, 1, 1, deep, LANES), lambda x, c: (0, x, c, 0, 0)),
        scratch_shapes=[pltpu.VMEM((nz, LANES), F32)],
        compiler_params=params(),
        cost_estimate=pl.CostEstimate(
            flops=0, bytes_accessed=coils * 2 * planes * ny * nz * 4, transcendentals=0
        ),
        name="maps_columns",
    )(coil_maps)


def last_maps_columns(coil_maps, count, first, coils):
    _, _, planes, ny, nz = coil_maps.shape
    deep = nz // count
    part = deep // 2
    return pl.pallas_call(
        functools.partial(last_maps_kernel, count, deep),
        out_shape=[jax.ShapeDtypeStruct((count, planes, coils, part, LANES), BF)] * 2,
        grid=(planes, coils),
        in_specs=[pl.BlockSpec((1, 2, 1, ny, nz), lambda x, c: (first + c, 0, x, 0, 0))],
        out_specs=[pl.BlockSpec((count, 1, 1, part, LANES), lambda x, c: (0, x, c, 0, 0))] * 2,
        scratch_shapes=[pltpu.VMEM((nz, LANES), F32)],
        compiler_params=params(),
        cost_estimate=pl.CostEstimate(
            flops=0, bytes_accessed=coils * 2 * planes * ny * nz * 4, transcendentals=0
        ),
        name="last_maps_columns",
    )(coil_maps)


def low_half(shape):
    return lax.broadcasted_iota(jnp.int32, shape, len(shape) - 1) < BLK


def fetch(w_hbm, held, sems, k):
    size = held.shape[0] // sems.shape[0]
    source = w_hbm.at[pl.ds(k * (size + TAIL), size)]
    return pltpu.make_async_copy(source, held.at[pl.ds(k * size, size)], sems.at[k])


def fetch_all(w_hbm, held, sems):
    for k in range(sems.shape[0]):
        fetch(w_hbm, held, sems, k).start()


def warp_kernel(nx, deep, pad, links, owner, g_ref, w_hbm, o_ref, held, twice, sems):
    fetch_all(w_hbm, held, sems)
    count = sems.shape[0]
    planes = nx // count
    low = low_half((deep, 128))

    def split(x, carry):
        for v in range(3):
            row = g_ref[x, :, v * 128 : (v + 1) * 128].astype(F32)
            turned = pltpu.roll(row, BLK, 1)
            first = jnp.where(low, row, turned).astype(BF)
            second = jnp.where(low, turned, row).astype(BF)
            if v < 2:
                twice[3 * x, pl.ds(v * pad, deep), :] = first
                twice[3 * x + 1, pl.ds(v * pad, deep), :] = second
            else:
                twice[3 * x + 2, pl.ds(0, deep), :] = first
                twice[3 * x + 2, pl.ds(pad, deep), :] = second
        return carry

    lax.fori_loop(0, nx, split, 0, unroll=8)
    low_both = low_half((2 * pad, 128))

    def block(k, carry):
        fetch(w_hbm, held, sems, k).wait()
        row = owner[k] * planes
        start = k * 3 * planes
        for x in range(planes):
            outs = []
            for b in range(3):
                t = 3 * x + b
                one, two = links[2 * start + t], links[2 * start + 3 * planes + t]
                both = jnp.where(low_both, twice[one], twice[two])
                weight = held[pl.ds((start + t) * BLK, BLK), :]
                outs.append(
                    lax.dot_general(
                        both, weight, (((1,), (1,)), ((), ())), preferred_element_type=F32
                    )
                )
            a, b, c = outs
            re = jnp.concatenate([a[:deep], b[:deep]], axis=1)
            im = jnp.concatenate([a[pad : pad + deep], b[pad : pad + deep]], axis=1)
            rest = jnp.concatenate([c[:deep], c[pad : pad + deep]], axis=1)
            o_ref[row + x, :, 0:128] = re
            o_ref[row + x, :, 128:256] = im
            o_ref[row + x, :, 256:384] = rest
        return carry

    lax.fori_loop(0, count, block, 0)


def warp(columns, weights, links, owner):
    nx, deep, _ = columns.shape
    blocks = 3 * nx
    pad = max(16, deep)
    whole = pl.BlockSpec((nx, deep, LANES), lambda i, l, p: (0, 0, 0))
    return pl.pallas_call(
        functools.partial(warp_kernel, nx, deep, pad),
        out_shape=jax.ShapeDtypeStruct((nx, deep, LANES), F32),
        grid_spec=pltpu.PrefetchScalarGridSpec(
            num_scalar_prefetch=2,
            grid=(1,),
            in_specs=[whole, pl.BlockSpec(memory_space=pl.ANY)],
            out_specs=whole,
            scratch_shapes=[
                pltpu.VMEM((blocks * BLK, 2 * BLK), BF),
                pltpu.VMEM((blocks, 2 * pad, 128), BF),
                pltpu.SemaphoreType.DMA((owner.shape[0],)),
            ],
        ),
        compiler_params=params(),
        cost_estimate=pl.CostEstimate(
            flops=2 * blocks * 256 * 256 * 32, bytes_accessed=20 << 20, transcendentals=0
        ),
        name="warp",
    )(links, owner, columns, weights)


def spread_kernel(nx, deep, pad, links, owner, c_ref, w_hbm, o_ref, held, total, sems):
    fetch_all(w_hbm, held, sems)
    count = sems.shape[0]
    planes = nx // count

    def clear(i, carry):
        total[pl.ds(i * 3, 3)] = jnp.zeros((3, 2 * pad, 128), F32)
        return carry

    lax.fori_loop(0, nx, clear, 0, unroll=8)
    low = low_half((2 * pad, 128))

    def tall(a, b):
        if deep == pad:
            return jnp.concatenate([a, b], axis=0)
        fill = jnp.zeros((pad - deep, a.shape[1]), a.dtype)
        return jnp.concatenate([a, fill, b, fill], axis=0)

    def block(k, carry):
        fetch(w_hbm, held, sems, k).wait()
        row = owner[k] * planes
        start = k * 3 * planes
        for x in range(planes):
            re, im, rest = (c_ref[row + x, :, v * 128 : (v + 1) * 128] for v in range(3))
            tiles = (
                tall(re[:, :BLK], im[:, :BLK]),
                tall(re[:, BLK:], im[:, BLK:]),
                tall(rest[:, :BLK], rest[:, BLK:]),
            )
            for b in range(3):
                t = 3 * x + b
                one, two = links[2 * start + t], links[2 * start + 3 * planes + t]
                weight = held[pl.ds((start + t) * BLK, BLK), :]
                out = jnp.dot(tiles[b].astype(BF), weight, preferred_element_type=F32)
                zero = jnp.zeros_like(out)
                total[one] += jnp.where(low, out, zero)
                total[two] += jnp.where(low, zero, out)
        return carry

    lax.fori_loop(0, count, block, 0)
    low_row = low_half((deep, 128))

    def gather(x, carry):
        sums = []
        for b in range(3):
            value = total[3 * x + b]
            sums.append(value + pltpu.roll(value, BLK, 1))
        a, b, c = sums
        o_ref[x, :, 0:128] = jnp.where(low_row, a[:deep], b[:deep]).astype(BF)
        o_ref[x, :, 128:256] = jnp.where(
            low_row, a[pad : pad + deep], b[pad : pad + deep]
        ).astype(BF)
        o_ref[x, :, 256:384] = jnp.where(low_row, c[:deep], c[pad : pad + deep]).astype(BF)
        return carry

    lax.fori_loop(0, nx, gather, 0, unroll=8)


def spread(combined, weights, links, owner):
    nx, deep, _ = combined.shape
    blocks = 3 * nx
    pad = max(8, deep)
    whole = pl.BlockSpec((nx, deep, LANES), lambda i, l, p: (0, 0, 0))
    return pl.pallas_call(
        functools.partial(spread_kernel, nx, deep, pad),
        out_shape=jax.ShapeDtypeStruct((nx, deep, LANES), BF),
        grid_spec=pltpu.PrefetchScalarGridSpec(
            num_scalar_prefetch=2,
            grid=(1,),
            in_specs=[whole, pl.BlockSpec(memory_space=pl.ANY)],
            out_specs=whole,
            scratch_shapes=[
                pltpu.VMEM((blocks * BLK, 2 * BLK), BF),
                pltpu.VMEM((blocks, 2 * pad, 128), F32),
                pltpu.SemaphoreType.DMA((owner.shape[0],)),
            ],
        ),
        compiler_params=params(),
        cost_estimate=pl.CostEstimate(
            flops=2 * blocks * 256 * 256 * 32, bytes_accessed=20 << 20, transcendentals=0
        ),
        name="spread",
    )(links, owner, combined, weights)


def coil_kernel(nx, deep, pad, fresh, *refs):
    if fresh:
        s_ref, w_ref, mask, iy, fx, bx, oy, o_ref, rows = refs
    else:
        s_ref, w_ref, mask, iy, fx, bx, oy, before, o_ref, rows = refs
    group = 8 if nx % 8 == 0 else 1
    cube = rows.reshape(3, nx, pad, 128)
    low = low_half((group, deep, 128))

    def thirds(ref, at):
        return tuple(ref[at, :, v * 128 : (v + 1) * 128].astype(F32) for v in range(3))

    def expand(i, carry):
        at = pl.ds(i * group, group)
        s0, s1, s2 = thirds(s_ref.at[:, 0], at)
        w0, w1, w2 = thirds(w_ref, at)
        turned = pltpu.roll(s2, BLK, 2)
        other = pltpu.roll(w2, BLK, 2)
        real = jnp.where(low, s2, turned)
        imag = jnp.where(low, turned, s2)
        cube[0, at, pl.ds(0, deep), :] = s0 * w0 - s1 * w1
        cube[1, at, pl.ds(0, deep), :] = s0 * w1 + s1 * w0
        cube[2, at, pl.ds(0, deep), :] = real * w2 + imag * jnp.where(low, -other, other)
        return carry

    lax.fori_loop(0, nx // group, expand, 0, unroll=4)

    batch = 4 if deep % 4 == 0 else 1

    def column(i, carry):
        ats = [pl.ds(i * batch + b, nx, stride=pad) for b in range(batch)]
        line = jnp.concatenate(
            [jnp.concatenate([rows[v, at, :] for v in range(3)], axis=1) for at in ats], axis=0
        ).astype(BF)
        y = jnp.dot(line, iy[...], preferred_element_type=F32).astype(BF)
        y = jnp.concatenate(
            [
                jnp.concatenate([y[b * nx : (b + 1) * nx, h * HALF : (h + 1) * HALF] for b in range(batch)], axis=1)
                for h in range(2)
            ],
            axis=0,
        )
        y = jnp.dot(fx[...], y, preferred_element_type=F32)
        y = jnp.concatenate([(y[:, b * HALF : (b + 1) * HALF] * mask[...]).astype(BF) for b in range(batch)], axis=1)
        y = jnp.dot(bx[...], y, preferred_element_type=F32).astype(BF)
        y = jnp.concatenate(
            [
                jnp.concatenate([y[h * nx : (h + 1) * nx, b * HALF : (b + 1) * HALF] for h in range(2)], axis=1)
                for b in range(batch)
            ],
            axis=0,
        )
        y = jnp.dot(y, oy[...], preferred_element_type=F32)
        for b, at in enumerate(ats):
            for v in range(3):
                rows[v, at, :] = y[b * nx : (b + 1) * nx, v * 128 : (v + 1) * 128]
        return carry

    lax.fori_loop(0, deep // batch, column, 0)

    first = pl.program_id(0) == 0

    def combine(i, carry):
        at = pl.ds(i * group, group)
        s0, s1, s2 = thirds(s_ref.at[:, 0], at)
        r0, r1, r2 = (cube[v, at, pl.ds(0, deep), :] for v in range(3))
        turned = pltpu.roll(s2, BLK, 2)
        other = pltpu.roll(r2, BLK, 2)
        real = jnp.where(low, s2, turned)
        imag = jnp.where(low, turned, s2)
        terms = (
            s0 * r0 + s1 * r1,
            s0 * r1 - s1 * r0,
            real * r2 + imag * jnp.where(low, other, -other),
        )
        for v in range(3):
            lanes = slice(v * 128, (v + 1) * 128)
            old = o_ref[at, :, lanes]
            start = jnp.zeros_like(old) if fresh else before[at, :, lanes]
            o_ref[at, :, lanes] = jnp.where(first, start, old) + terms[v]
        return carry

    lax.fori_loop(0, nx // group, combine, 0, unroll=4)


def coils(maps, warped, mask, tabs, before, part):
    nx, count, deep, _ = maps.shape
    pad = max(8, deep)
    fresh = before is None
    whole = lambda shape: pl.BlockSpec(
        shape, lambda c: (0,) * len(shape), pipeline_mode=pl.Buffered(1)
    )
    in_specs = [pl.BlockSpec((nx, 1, deep, LANES), lambda c: (0, c, 0, 0))]
    args = [maps, warped, mask, *tabs] + ([] if fresh else [before])
    def columns(array):
        at = part if array.shape[1] > deep else 0
        return pl.BlockSpec(
            (nx, deep, LANES), lambda c: (0, at, 0), pipeline_mode=pl.Buffered(1)
        )

    in_specs += [columns(warped)] + [whole(a.shape) for a in (mask, *tabs)]
    in_specs += [] if fresh else [columns(before)]
    return pl.pallas_call(
        functools.partial(coil_kernel, nx, deep, pad, fresh),
        out_shape=jax.ShapeDtypeStruct((nx, deep, LANES), F32),
        grid=(count,),
        in_specs=in_specs,
        out_specs=pl.BlockSpec((nx, deep, LANES), lambda c: (0, 0, 0)),
        scratch_shapes=[pltpu.VMEM((3, nx * pad, 128), F32)],
        compiler_params=params(),
        cost_estimate=pl.CostEstimate(
            flops=count * deep * 4 * 8 * nx * nx * 192 * 2,
            bytes_accessed=count * nx * deep * LANES * 2 + (14 << 20),
            transcendentals=0,
        ),
        name="coils",
    )(*args)


def update_kernel(count, parts, *refs):
    backs = refs[:parts]
    i_ref, a_ref, o_ref, scratch = refs[parts:]
    part = backs[0].shape[2]
    for x in range(o_ref.shape[1]):
        for h, back in enumerate(backs):
            for d in range(count):
                scratch[x, pl.ds((d * parts + h) * part, part), :] = back[d, x].astype(F32)
        grad = scratch[x].astype(BF).T.astype(F32)
        real = jnp.concatenate([grad[0:128], grad[256:320]], axis=0)
        imag = jnp.concatenate([grad[128:256], grad[320:384]], axis=0)
        for p, value in enumerate((real, imag)):
            o_ref[p, x] = i_ref[p, x] - 0.5 * (value - a_ref[p, x].astype(F32))


def update(backs, image, adjoint):
    parts = len(backs)
    count, planes, part, _ = backs[0].shape
    _, _, ny, nz = image.shape
    group = 3 if planes % 3 == 0 else 1
    block = pl.BlockSpec((2, group, ny, nz), lambda x: (0, x, 0, 0))
    back = pl.BlockSpec((count, group, part, LANES), lambda x: (0, x, 0, 0))
    return pl.pallas_call(
        functools.partial(update_kernel, count, parts),
        out_shape=jax.ShapeDtypeStruct(image.shape, F32),
        grid=(planes // group,),
        in_specs=[back] * parts + [block, block],
        out_specs=block,
        scratch_shapes=[pltpu.VMEM((group, nz, LANES), F32)],
        compiler_params=params(),
        cost_estimate=pl.CostEstimate(flops=0, bytes_accessed=image.size * 12, transcendentals=0),
        name="update",
    )(*backs, image, adjoint)


def exchange(parts):
    return lax.all_to_all(parts, "slab", split_axis=0, concat_axis=0, tiled=True)


def after(value, *others):
    return lax.optimization_barrier((value, *others))[0]


def swap_halves(value):
    count = lax.axis_size("slab")
    half = count // 2
    other = lax.ppermute(value, "slab", [(i, i ^ half) for i in range(count)])
    return jnp.concatenate([value, other], axis=0)


def gather_half(pair):
    count = lax.axis_size("slab")
    half = count // 2
    groups = [list(range(half)), list(range(half, count))]
    gathered = lax.all_gather(pair, "slab", axis=0, tiled=True, axis_index_groups=groups)
    mine = lax.axis_index("slab") // half
    place = jnp.arange(count, dtype=jnp.int32)
    return gathered, place // 2 + half * ((place % 2) ^ mine)


def per_device(image, adjoint_data, coil_maps, masks, sources, weights):
    count = lax.axis_size("slab")
    planes, ny, nz = image.shape[1:]
    nx = planes * count
    deep = nz // count
    total = coil_maps.shape[0]
    tabs = tables(nx, ny)
    sampled = jnp.pad(masks[0].astype(F32), ((0, 0), (0, HALF - ny)))
    mask = jnp.concatenate([sampled, sampled], axis=0)

    targets = 3 * planes
    matrices = weights[0].reshape(targets, 2, BLK, BLK)
    matrices = jnp.transpose(matrices, (0, 2, 1, 3)).reshape(targets * BLK, 2 * BLK)
    chosen = sources[0].T
    digits = jnp.concatenate([chosen // BLK, chosen % BLK], axis=0).astype(BF)
    digits = jnp.pad(digits, ((0, TAIL - 4), (0, 2 * BLK - targets)))
    pair = swap_halves(jnp.concatenate([matrices, digits], axis=0))
    packed, owner = gather_half(pair)
    digits = packed.reshape(count, targets * BLK + TAIL, 2 * BLK)[:, targets * BLK :]
    digits = digits[:, :4, :targets].astype(jnp.int32)
    links = (digits[:, :2] * BLK + digits[:, 2:]).reshape(-1)

    def run(received, before, part):
        size = received.shape[2]
        return coils(received.reshape(nx, size, -1, LANES), warped, mask, tabs, before, part)

    def back(combined, *needs):
        grad = spread(combined, packed, links, owner)
        return exchange(after(grad, *needs).reshape(count, planes, -1, LANES))

    columns = exchange(image_columns(image, count))
    warped = warp(columns.reshape(nx, deep, LANES), packed, links, owner)
    halves = deep % 16 == 0
    early = total - total // 4 if halves else total - 1
    late = total - early
    maps = maps_columns(coil_maps, count, 0, early)
    arrived = exchange(after(maps, columns, pair))
    if not halves:
        maps = maps_columns(coil_maps, count, early, late)
        last = exchange(after(maps, arrived, warped))
        combined = run(last, run(arrived, None, 0), 0)
        return update([back(combined)], image, adjoint_data)

    first, second = last_maps_columns(coil_maps, count, early, late)
    first = exchange(after(first, arrived, warped))
    combined = run(arrived, None, 0)
    second = exchange(after(second, first, combined))
    back_first = back(run(first, combined, 0), second)
    back_second = back(run(second, combined, 1), back_first)
    return update([back_first, back_second], image, adjoint_data)


def solution(mesh):
    return jax.shard_map(
        per_device,
        mesh=mesh,
        in_specs=(
            P(None, ("grp", "slab"), None, None),
            P(None, ("grp", "slab"), None, None),
            P(None, None, ("grp", "slab"), None, None),
            P(None, "grp", None),
            P(None, ("grp", "slab"), None),
            P(None, ("grp", "slab"), None),
        ),
        out_specs=P(None, ("grp", "slab"), None, None),
        check_vma=False,
    )
```

```python
import functools
import math

import jax
import jax.numpy as jnp
import numpy as np
from jax import lax
from jax.experimental import pallas as pl
from jax.experimental.pallas import tpu as pltpu
from jax.sharding import PartitionSpec as P

BLK = 64
LANES = 384
TAIL = 16
HALF = 256
VMEM_LIMIT = 56 * 1024 * 1024
BF = jnp.bfloat16
F32 = jnp.float32


def lane_order(length):
    lo, rest = 128, length - 128
    part = np.concatenate([np.zeros(lo), np.ones(lo), np.zeros(rest), np.ones(rest)])
    pos = np.concatenate([np.arange(lo), np.arange(lo), lo + np.arange(rest), lo + np.arange(rest)])
    return part.astype(np.int32), pos.astype(np.int32)


def dft_table(length, direction):
    positions = np.arange(length)
    phases = (positions[:, None] * positions[None, :] % length).astype(np.float32)
    phases = phases * np.float32(2.0 * math.pi / length)
    factor = np.float32(1.0 / math.sqrt(length))
    cosine = np.cos(phases) * factor
    sine = np.sin(phases) * (np.float32(direction) * factor)
    upper = np.stack([cosine, -sine], axis=1)
    lower = np.stack([sine, cosine], axis=1)
    return np.stack([upper, lower], axis=0)


def tables(nx, ny):
    part, pos = lane_order(ny)
    fwd_y, inv_y = dft_table(ny, -1.0), dft_table(ny, 1.0)
    into_y = np.zeros((2 * ny, 2, HALF), np.float32)
    into_y[:, :, :ny] = np.transpose(fwd_y[:, :, part, pos], (2, 0, 1))
    from_y = np.zeros((2, HALF, 2 * ny), np.float32)
    from_y[:, :ny, :] = np.transpose(inv_y[part, pos], (1, 2, 0))
    fwd_x = dft_table(nx, -1.0).reshape(2 * nx, 2 * nx)
    inv_x = dft_table(nx, 1.0).reshape(2 * nx, 2 * nx)
    out = (into_y.reshape(2 * ny, 2 * HALF), fwd_x, inv_x, from_y.reshape(2 * HALF, 2 * ny))
    return tuple(jnp.asarray(t, BF) for t in out)


def params():
    return pltpu.CompilerParams(vmem_limit_bytes=VMEM_LIMIT)


def to_rows(parts):
    stacked = jnp.concatenate(
        [parts[0, :128], parts[1, :128], parts[0, 128:], parts[1, 128:]], axis=0
    )
    return stacked.T


def spread_rows(outs, rows, scratch, count, deep):
    if len(outs) == 1 and deep % 16 == 0:
        outs[0][...] = rows.reshape(count, deep, LANES)
        return
    part = deep // len(outs)
    scratch[...] = rows.astype(F32)
    for h, out in enumerate(outs):
        for d in range(count):
            out[d] = scratch[pl.ds(d * deep + h * part, part), :].astype(BF)


def image_kernel(count, deep, x_ref, o_ref, scratch):
    for x in range(x_ref.shape[1]):
        rows = to_rows(x_ref[:, x].astype(BF))
        spread_rows([o_ref.at[:, x]], rows, scratch, count, deep)


def image_columns(image, count):
    _, planes, ny, nz = image.shape
    deep = nz // count
    group = 3 if planes % 3 == 0 else 1
    return pl.pallas_call(
        functools.partial(image_kernel, count, deep),
        out_shape=jax.ShapeDtypeStruct((count, planes, deep, LANES), BF),
        grid=(planes // group,),
        in_specs=[pl.BlockSpec((2, group, ny, nz), lambda x: (0, x, 0, 0))],
        out_specs=pl.BlockSpec((count, group, deep, LANES), lambda x: (0, x, 0, 0)),
        scratch_shapes=[pltpu.VMEM((nz, LANES), F32)],
        compiler_params=params(),
        cost_estimate=pl.CostEstimate(flops=0, bytes_accessed=image.size * 6, transcendentals=0),
        name="image_columns",
    )(image)


def maps_kernel(count, deep, x_ref, o_ref, scratch):
    spread_rows([o_ref.at[:, 0, 0]], to_rows(x_ref[0, :, 0]), scratch, count, deep)


def last_maps_kernel(count, deep, x_ref, first_ref, second_ref, scratch):
    outs = [first_ref.at[:, 0, 0], second_ref.at[:, 0, 0]]
    spread_rows(outs, to_rows(x_ref[0, :, 0]), scratch, count, deep)


def maps_columns(coil_maps, count, first, coils):
    _, _, planes, ny, nz = coil_maps.shape
    deep = nz // count
    return pl.pallas_call(
        functools.partial(maps_kernel, count, deep),
        out_shape=jax.ShapeDtypeStruct((count, planes, coils, deep, LANES), BF),
        grid=(planes, coils),
        in_specs=[pl.BlockSpec((1, 2, 1, ny, nz), lambda x, c: (first + c, 0, x, 0, 0))],
        out_specs=pl.BlockSpec((count, 1, 1, deep, LANES), lambda x, c: (0, x, c, 0, 0)),
        scratch_shapes=[pltpu.VMEM((nz, LANES), F32)],
        compiler_params=params(),
        cost_estimate=pl.CostEstimate(
            flops=0, bytes_accessed=coils * 2 * planes * ny * nz * 4, transcendentals=0
        ),
        name="maps_columns",
    )(coil_maps)


def last_maps_columns(coil_maps, count, first, coils):
    _, _, planes, ny, nz = coil_maps.shape
    deep = nz // count
    part = deep // 2
    return pl.pallas_call(
        functools.partial(last_maps_kernel, count, deep),
        out_shape=[jax.ShapeDtypeStruct((count, planes, coils, part, LANES), BF)] * 2,
        grid=(planes, coils),
        in_specs=[pl.BlockSpec((1, 2, 1, ny, nz), lambda x, c: (first + c, 0, x, 0, 0))],
        out_specs=[pl.BlockSpec((count, 1, 1, part, LANES), lambda x, c: (0, x, c, 0, 0))] * 2,
        scratch_shapes=[pltpu.VMEM((nz, LANES), F32)],
        compiler_params=params(),
        cost_estimate=pl.CostEstimate(
            flops=0, bytes_accessed=coils * 2 * planes * ny * nz * 4, transcendentals=0
        ),
        name="last_maps_columns",
    )(coil_maps)


def low_half(shape):
    return lax.broadcasted_iota(jnp.int32, shape, len(shape) - 1) < BLK


def fetch(w_hbm, held, sems, k):
    size = held.shape[0] // sems.shape[0]
    source = w_hbm.at[pl.ds(k * (size + TAIL), size)]
    return pltpu.make_async_copy(source, held.at[pl.ds(k * size, size)], sems.at[k])


def fetch_all(w_hbm, held, sems):
    for k in range(sems.shape[0]):
        fetch(w_hbm, held, sems, k).start()


def warp_kernel(nx, deep, pad, links, owner, g_ref, w_hbm, o_ref, held, twice, sems):
    fetch_all(w_hbm, held, sems)
    count = sems.shape[0]
    planes = nx // count
    low = low_half((deep, 128))

    def split(x, carry):
        for v in range(3):
            row = g_ref[x, :, v * 128 : (v + 1) * 128].astype(F32)
            turned = pltpu.roll(row, BLK, 1)
            first = jnp.where(low, row, turned).astype(BF)
            second = jnp.where(low, turned, row).astype(BF)
            if v < 2:
                twice[3 * x, pl.ds(v * pad, deep), :] = first
                twice[3 * x + 1, pl.ds(v * pad, deep), :] = second
            else:
                twice[3 * x + 2, pl.ds(0, deep), :] = first
                twice[3 * x + 2, pl.ds(pad, deep), :] = second
        return carry

    lax.fori_loop(0, nx, split, 0, unroll=8)
    low_both = low_half((2 * pad, 128))

    def block(k, carry):
        fetch(w_hbm, held, sems, k).wait()
        row = owner[k] * planes
        start = k * 3 * planes
        for x in range(planes):
            outs = []
            for b in range(3):
                t = 3 * x + b
                one, two = links[2 * start + t], links[2 * start + 3 * planes + t]
                both = jnp.where(low_both, twice[one], twice[two])
                weight = held[pl.ds((start + t) * BLK, BLK), :]
                outs.append(
                    lax.dot_general(
                        both, weight, (((1,), (1,)), ((), ())), preferred_element_type=F32
                    )
                )
            a, b, c = outs
            re = jnp.concatenate([a[:deep], b[:deep]], axis=1)
            im = jnp.concatenate([a[pad : pad + deep], b[pad : pad + deep]], axis=1)
            rest = jnp.concatenate([c[:deep], c[pad : pad + deep]], axis=1)
            o_ref[row + x, :, 0:128] = re
            o_ref[row + x, :, 128:256] = im
            o_ref[row + x, :, 256:384] = rest
        return carry

    lax.fori_loop(0, count, block, 0)


def warp(columns, weights, links, owner):
    nx, deep, _ = columns.shape
    blocks = 3 * nx
    pad = max(16, deep)
    whole = pl.BlockSpec((nx, deep, LANES), lambda i, l, p: (0, 0, 0))
    return pl.pallas_call(
        functools.partial(warp_kernel, nx, deep, pad),
        out_shape=jax.ShapeDtypeStruct((nx, deep, LANES), F32),
        grid_spec=pltpu.PrefetchScalarGridSpec(
            num_scalar_prefetch=2,
            grid=(1,),
            in_specs=[whole, pl.BlockSpec(memory_space=pl.ANY)],
            out_specs=whole,
            scratch_shapes=[
                pltpu.VMEM((blocks * BLK, 2 * BLK), BF),
                pltpu.VMEM((blocks, 2 * pad, 128), BF),
                pltpu.SemaphoreType.DMA((owner.shape[0],)),
            ],
        ),
        compiler_params=params(),
        cost_estimate=pl.CostEstimate(
            flops=2 * blocks * 256 * 256 * 32, bytes_accessed=20 << 20, transcendentals=0
        ),
        name="warp",
    )(links, owner, columns, weights)


def spread_kernel(nx, deep, pad, links, owner, c_ref, w_hbm, o_ref, held, total, sems):
    fetch_all(w_hbm, held, sems)
    count = sems.shape[0]
    planes = nx // count

    def clear(i, carry):
        total[pl.ds(i * 3, 3)] = jnp.zeros((3, 2 * pad, 128), F32)
        return carry

    lax.fori_loop(0, nx, clear, 0, unroll=8)
    low = low_half((2 * pad, 128))

    def tall(a, b):
        if deep == pad:
            return jnp.concatenate([a, b], axis=0)
        fill = jnp.zeros((pad - deep, a.shape[1]), a.dtype)
        return jnp.concatenate([a, fill, b, fill], axis=0)

    def block(k, carry):
        fetch(w_hbm, held, sems, k).wait()
        row = owner[k] * planes
        start = k * 3 * planes
        for x in range(planes):
            re, im, rest = (c_ref[row + x, :, v * 128 : (v + 1) * 128] for v in range(3))
            tiles = (
                tall(re[:, :BLK], im[:, :BLK]),
                tall(re[:, BLK:], im[:, BLK:]),
                tall(rest[:, :BLK], rest[:, BLK:]),
            )
            for b in range(3):
                t = 3 * x + b
                one, two = links[2 * start + t], links[2 * start + 3 * planes + t]
                weight = held[pl.ds((start + t) * BLK, BLK), :]
                out = jnp.dot(tiles[b].astype(BF), weight, preferred_element_type=F32)
                zero = jnp.zeros_like(out)
                total[one] += jnp.where(low, out, zero)
                total[two] += jnp.where(low, zero, out)
        return carry

    lax.fori_loop(0, count, block, 0)
    low_row = low_half((deep, 128))

    def gather(x, carry):
        sums = []
        for b in range(3):
            value = total[3 * x + b]
            sums.append(value + pltpu.roll(value, BLK, 1))
        a, b, c = sums
        o_ref[x, :, 0:128] = jnp.where(low_row, a[:deep], b[:deep]).astype(BF)
        o_ref[x, :, 128:256] = jnp.where(
            low_row, a[pad : pad + deep], b[pad : pad + deep]
        ).astype(BF)
        o_ref[x, :, 256:384] = jnp.where(low_row, c[:deep], c[pad : pad + deep]).astype(BF)
        return carry

    lax.fori_loop(0, nx, gather, 0, unroll=8)


def spread(combined, weights, links, owner):
    nx, deep, _ = combined.shape
    blocks = 3 * nx
    pad = max(8, deep)
    whole = pl.BlockSpec((nx, deep, LANES), lambda i, l, p: (0, 0, 0))
    return pl.pallas_call(
        functools.partial(spread_kernel, nx, deep, pad),
        out_shape=jax.ShapeDtypeStruct((nx, deep, LANES), BF),
        grid_spec=pltpu.PrefetchScalarGridSpec(
            num_scalar_prefetch=2,
            grid=(1,),
            in_specs=[whole, pl.BlockSpec(memory_space=pl.ANY)],
            out_specs=whole,
            scratch_shapes=[
                pltpu.VMEM((blocks * BLK, 2 * BLK), BF),
                pltpu.VMEM((blocks, 2 * pad, 128), F32),
                pltpu.SemaphoreType.DMA((owner.shape[0],)),
            ],
        ),
        compiler_params=params(),
        cost_estimate=pl.CostEstimate(
            flops=2 * blocks * 256 * 256 * 32, bytes_accessed=20 << 20, transcendentals=0
        ),
        name="spread",
    )(links, owner, combined, weights)


def coil_kernel(nx, deep, pad, fresh, *refs):
    if fresh:
        s_ref, w_ref, mask, iy, fx, bx, oy, o_ref, rows = refs
    else:
        s_ref, w_ref, mask, iy, fx, bx, oy, before, o_ref, rows = refs
    group = 8 if nx % 8 == 0 else 1
    cube = rows.reshape(3, nx, pad, 128)
    low = low_half((group, deep, 128))

    def thirds(ref, at):
        return tuple(ref[at, :, v * 128 : (v + 1) * 128].astype(F32) for v in range(3))

    def expand(i, carry):
        at = pl.ds(i * group, group)
        s0, s1, s2 = thirds(s_ref.at[:, 0], at)
        w0, w1, w2 = thirds(w_ref, at)
        turned = pltpu.roll(s2, BLK, 2)
        other = pltpu.roll(w2, BLK, 2)
        real = jnp.where(low, s2, turned)
        imag = jnp.where(low, turned, s2)
        cube[0, at, pl.ds(0, deep), :] = s0 * w0 - s1 * w1
        cube[1, at, pl.ds(0, deep), :] = s0 * w1 + s1 * w0
        cube[2, at, pl.ds(0, deep), :] = real * w2 + imag * jnp.where(low, -other, other)
        return carry

    lax.fori_loop(0, nx // group, expand, 0, unroll=4)

    batch = 4 if deep % 4 == 0 else 1

    def column(i, carry):
        ats = [pl.ds(i * batch + b, nx, stride=pad) for b in range(batch)]
        line = jnp.concatenate(
            [jnp.concatenate([rows[v, at, :] for v in range(3)], axis=1) for at in ats], axis=0
        ).astype(BF)
        y = jnp.dot(line, iy[...], preferred_element_type=F32).astype(BF)
        y = jnp.concatenate(
            [
                jnp.concatenate([y[b * nx : (b + 1) * nx, h * HALF : (h + 1) * HALF] for b in range(batch)], axis=1)
                for h in range(2)
            ],
            axis=0,
        )
        y = jnp.dot(fx[...], y, preferred_element_type=F32)
        y = jnp.concatenate([(y[:, b * HALF : (b + 1) * HALF] * mask[...]).astype(BF) for b in range(batch)], axis=1)
        y = jnp.dot(bx[...], y, preferred_element_type=F32).astype(BF)
        y = jnp.concatenate(
            [
                jnp.concatenate([y[h * nx : (h + 1) * nx, b * HALF : (b + 1) * HALF] for h in range(2)], axis=1)
                for b in range(batch)
            ],
            axis=0,
        )
        y = jnp.dot(y, oy[...], preferred_element_type=F32)
        for b, at in enumerate(ats):
            for v in range(3):
                rows[v, at, :] = y[b * nx : (b + 1) * nx, v * 128 : (v + 1) * 128]
        return carry

    lax.fori_loop(0, deep // batch, column, 0)

    first = pl.program_id(0) == 0

    def combine(i, carry):
        at = pl.ds(i * group, group)
        s0, s1, s2 = thirds(s_ref.at[:, 0], at)
        r0, r1, r2 = (cube[v, at, pl.ds(0, deep), :] for v in range(3))
        turned = pltpu.roll(s2, BLK, 2)
        other = pltpu.roll(r2, BLK, 2)
        real = jnp.where(low, s2, turned)
        imag = jnp.where(low, turned, s2)
        terms = (
            s0 * r0 + s1 * r1,
            s0 * r1 - s1 * r0,
            real * r2 + imag * jnp.where(low, other, -other),
        )
        for v in range(3):
            lanes = slice(v * 128, (v + 1) * 128)
            old = o_ref[at, :, lanes]
            start = jnp.zeros_like(old) if fresh else before[at, :, lanes]
            o_ref[at, :, lanes] = jnp.where(first, start, old) + terms[v]
        return carry

    lax.fori_loop(0, nx // group, combine, 0, unroll=4)


def coils(maps, warped, mask, tabs, before, part):
    nx, count, deep, _ = maps.shape
    pad = max(8, deep)
    fresh = before is None
    whole = lambda shape: pl.BlockSpec(
        shape, lambda c: (0,) * len(shape), pipeline_mode=pl.Buffered(1)
    )
    in_specs = [pl.BlockSpec((nx, 1, deep, LANES), lambda c: (0, c, 0, 0))]
    args = [maps, warped, mask, *tabs] + ([] if fresh else [before])
    def columns(array):
        at = part if array.shape[1] > deep else 0
        return pl.BlockSpec(
            (nx, deep, LANES), lambda c: (0, at, 0), pipeline_mode=pl.Buffered(1)
        )

    in_specs += [columns(warped)] + [whole(a.shape) for a in (mask, *tabs)]
    in_specs += [] if fresh else [columns(before)]
    return pl.pallas_call(
        functools.partial(coil_kernel, nx, deep, pad, fresh),
        out_shape=jax.ShapeDtypeStruct((nx, deep, LANES), F32),
        grid=(count,),
        in_specs=in_specs,
        out_specs=pl.BlockSpec((nx, deep, LANES), lambda c: (0, 0, 0)),
        scratch_shapes=[pltpu.VMEM((3, nx * pad, 128), F32)],
        compiler_params=params(),
        cost_estimate=pl.CostEstimate(
            flops=count * deep * 4 * 8 * nx * nx * 192 * 2,
            bytes_accessed=count * nx * deep * LANES * 2 + (14 << 20),
            transcendentals=0,
        ),
        name="coils",
    )(*args)


def update_kernel(count, parts, *refs):
    backs = refs[:parts]
    i_ref, a_ref, o_ref, scratch = refs[parts:]
    part = backs[0].shape[2]
    for x in range(o_ref.shape[1]):
        for h, back in enumerate(backs):
            for d in range(count):
                scratch[x, pl.ds((d * parts + h) * part, part), :] = back[d, x].astype(F32)
        grad = scratch[x].astype(BF).T.astype(F32)
        real = jnp.concatenate([grad[0:128], grad[256:320]], axis=0)
        imag = jnp.concatenate([grad[128:256], grad[320:384]], axis=0)
        for p, value in enumerate((real, imag)):
            o_ref[p, x] = i_ref[p, x] - 0.5 * (value - a_ref[p, x].astype(F32))


def update(backs, image, adjoint):
    parts = len(backs)
    count, planes, part, _ = backs[0].shape
    _, _, ny, nz = image.shape
    group = 3 if planes % 3 == 0 else 1
    block = pl.BlockSpec((2, group, ny, nz), lambda x: (0, x, 0, 0))
    back = pl.BlockSpec((count, group, part, LANES), lambda x: (0, x, 0, 0))
    return pl.pallas_call(
        functools.partial(update_kernel, count, parts),
        out_shape=jax.ShapeDtypeStruct(image.shape, F32),
        grid=(planes // group,),
        in_specs=[back] * parts + [block, block],
        out_specs=block,
        scratch_shapes=[pltpu.VMEM((group, nz, LANES), F32)],
        compiler_params=params(),
        cost_estimate=pl.CostEstimate(flops=0, bytes_accessed=image.size * 12, transcendentals=0),
        name="update",
    )(*backs, image, adjoint)


def exchange(parts):
    return lax.all_to_all(parts, "slab", split_axis=0, concat_axis=0, tiled=True)


def after(value, *others):
    return lax.optimization_barrier((value, *others))[0]


def swap_halves(value):
    count = lax.axis_size("slab")
    half = count // 2
    other = lax.ppermute(value, "slab", [(i, i ^ half) for i in range(count)])
    return jnp.concatenate([value, other], axis=0)


def gather_half(pair):
    count = lax.axis_size("slab")
    half = count // 2
    groups = [list(range(half)), list(range(half, count))]
    gathered = lax.all_gather(pair, "slab", axis=0, tiled=True, axis_index_groups=groups)
    mine = lax.axis_index("slab") // half
    place = jnp.arange(count, dtype=jnp.int32)
    return gathered, place // 2 + half * ((place % 2) ^ mine)


def per_device(image, adjoint_data, coil_maps, masks, sources, weights):
    count = lax.axis_size("slab")
    planes, ny, nz = image.shape[1:]
    nx = planes * count
    deep = nz // count
    total = coil_maps.shape[0]
    tabs = tables(nx, ny)
    sampled = jnp.pad(masks[0].astype(F32), ((0, 0), (0, HALF - ny)))
    mask = jnp.concatenate([sampled, sampled], axis=0)

    targets = 3 * planes
    matrices = weights[0].reshape(targets, 2, BLK, BLK)
    matrices = jnp.transpose(matrices, (0, 2, 1, 3)).reshape(targets * BLK, 2 * BLK)
    chosen = sources[0].T
    digits = jnp.concatenate([chosen // BLK, chosen % BLK], axis=0).astype(BF)
    digits = jnp.pad(digits, ((0, TAIL - 4), (0, 2 * BLK - targets)))
    pair = swap_halves(jnp.concatenate([matrices, digits], axis=0))
    packed, owner = gather_half(pair)
    digits = packed.reshape(count, targets * BLK + TAIL, 2 * BLK)[:, targets * BLK :]
    digits = digits[:, :4, :targets].astype(jnp.int32)
    links = (digits[:, :2] * BLK + digits[:, 2:]).reshape(-1)

    def run(received, before, part):
        size = received.shape[2]
        return coils(received.reshape(nx, size, -1, LANES), warped, mask, tabs, before, part)

    def back(combined, *needs):
        grad = spread(combined, packed, links, owner)
        return exchange(after(grad, *needs).reshape(count, planes, -1, LANES))

    columns = exchange(image_columns(image, count))
    warped = warp(columns.reshape(nx, deep, LANES), packed, links, owner)
    halves = deep % 16 == 0
    early = total - 3 * total // 8 if halves else total - 1
    late = total - early
    maps = maps_columns(coil_maps, count, 0, early)
    arrived = exchange(after(maps, columns, pair))
    if not halves:
        maps = maps_columns(coil_maps, count, early, late)
        last = exchange(after(maps, arrived, warped))
        combined = run(last, run(arrived, None, 0), 0)
        return update([back(combined)], image, adjoint_data)

    first, second = last_maps_columns(coil_maps, count, early, late)
    first = exchange(after(first, arrived, warped))
    combined = run(arrived, None, 0)
    second = exchange(after(second, first, combined))
    back_first = back(run(first, combined, 0), second)
    back_second = back(run(second, combined, 1), back_first)
    return update([back_first, back_second], image, adjoint_data)


def solution(mesh):
    return jax.shard_map(
        per_device,
        mesh=mesh,
        in_specs=(
            P(None, ("grp", "slab"), None, None),
            P(None, ("grp", "slab"), None, None),
            P(None, None, ("grp", "slab"), None, None),
            P(None, "grp", None),
            P(None, ("grp", "slab"), None),
            P(None, ("grp", "slab"), None),
        ),
        out_specs=P(None, ("grp", "slab"), None, None),
        check_vma=False,
    )
```

```python
import functools
import math

import jax
import jax.numpy as jnp
import numpy as np
from jax import lax
from jax.experimental import pallas as pl
from jax.experimental.pallas import tpu as pltpu
from jax.sharding import PartitionSpec as P

BLK = 64
LANES = 384
TAIL = 16
HALF = 256
VMEM_LIMIT = 56 * 1024 * 1024
BF = jnp.bfloat16
F32 = jnp.float32


def lane_order(length):
    lo, rest = 128, length - 128
    part = np.concatenate([np.zeros(lo), np.ones(lo), np.zeros(rest), np.ones(rest)])
    pos = np.concatenate([np.arange(lo), np.arange(lo), lo + np.arange(rest), lo + np.arange(rest)])
    return part.astype(np.int32), pos.astype(np.int32)


def dft_table(length, direction):
    positions = np.arange(length)
    phases = (positions[:, None] * positions[None, :] % length).astype(np.float32)
    phases = phases * np.float32(2.0 * math.pi / length)
    factor = np.float32(1.0 / math.sqrt(length))
    cosine = np.cos(phases) * factor
    sine = np.sin(phases) * (np.float32(direction) * factor)
    upper = np.stack([cosine, -sine], axis=1)
    lower = np.stack([sine, cosine], axis=1)
    return np.stack([upper, lower], axis=0)


def tables(nx, ny):
    part, pos = lane_order(ny)
    fwd_y, inv_y = dft_table(ny, -1.0), dft_table(ny, 1.0)
    into_y = np.zeros((2 * ny, 2, HALF), np.float32)
    into_y[:, :, :ny] = np.transpose(fwd_y[:, :, part, pos], (2, 0, 1))
    from_y = np.zeros((2, HALF, 2 * ny), np.float32)
    from_y[:, :ny, :] = np.transpose(inv_y[part, pos], (1, 2, 0))
    fwd_x = dft_table(nx, -1.0).reshape(2 * nx, 2 * nx)
    inv_x = dft_table(nx, 1.0).reshape(2 * nx, 2 * nx)
    out = (into_y.reshape(2 * ny, 2 * HALF), fwd_x, inv_x, from_y.reshape(2 * HALF, 2 * ny))
    return tuple(jnp.asarray(t, BF) for t in out)


def params():
    return pltpu.CompilerParams(vmem_limit_bytes=VMEM_LIMIT)


def to_rows(parts):
    stacked = jnp.concatenate(
        [parts[0, :128], parts[1, :128], parts[0, 128:], parts[1, 128:]], axis=0
    )
    return stacked.T


def part_rows(scratch, count, deep, parts, d, h):
    part = deep // parts
    return scratch[pl.ds((h * count + d) * part, part), :]


def spread_rows(out, scratch, count, deep, parts):
    for d in range(count):
        rows = [part_rows(scratch, count, deep, parts, d, h) for h in range(parts)]
        out[d] = jnp.concatenate(rows, axis=0).astype(BF)


def parts_of(deep):
    return 2 if deep % 16 == 0 else 1


def image_kernel(count, deep, x_ref, o_ref, scratch):
    for x in range(x_ref.shape[1]):
        scratch[x] = to_rows(x_ref[:, x].astype(BF)).astype(F32)
        spread_rows(o_ref.at[:, x], scratch.at[x], count, deep, parts_of(deep))


def image_columns(image, count):
    _, planes, ny, nz = image.shape
    deep = nz // count
    group = 3 if planes % 3 == 0 else 1
    return pl.pallas_call(
        functools.partial(image_kernel, count, deep),
        out_shape=jax.ShapeDtypeStruct((count, planes, deep, LANES), BF),
        grid=(planes // group,),
        in_specs=[pl.BlockSpec((2, group, ny, nz), lambda x: (0, x, 0, 0))],
        out_specs=pl.BlockSpec((count, group, deep, LANES), lambda x: (0, x, 0, 0)),
        scratch_shapes=[pltpu.VMEM((group, nz, LANES), F32)],
        compiler_params=params(),
        cost_estimate=pl.CostEstimate(flops=0, bytes_accessed=image.size * 6, transcendentals=0),
        name="image_columns",
    )(image)


def maps_kernel(count, deep, x_ref, o_ref, scratch):
    scratch[...] = to_rows(x_ref[0, :, 0]).astype(F32)
    spread_rows(o_ref.at[:, 0, 0], scratch, count, deep, parts_of(deep))


def last_maps_kernel(count, deep, coils, x_ref, first_ref, second_ref, scratch):
    scratch[...] = to_rows(x_ref[0, :, 0]).astype(F32)
    for c in range(coils):

        @pl.when(pl.program_id(1) == c)
        def _():
            for d in range(count):
                half = part_rows(scratch, count, deep, 2, d, 1).astype(BF)
                first_ref[d, 0, c] = part_rows(scratch, count, deep, 2, d, 0).astype(BF)
                if c == 0:
                    first_ref[d, 0, coils] = half
                else:
                    second_ref[d, 0, c - 1] = half


def maps_columns(coil_maps, count, first, coils):
    _, _, planes, ny, nz = coil_maps.shape
    deep = nz // count
    return pl.pallas_call(
        functools.partial(maps_kernel, count, deep),
        out_shape=jax.ShapeDtypeStruct((count, planes, coils, deep, LANES), BF),
        grid=(planes, coils),
        in_specs=[pl.BlockSpec((1, 2, 1, ny, nz), lambda x, c: (first + c, 0, x, 0, 0))],
        out_specs=pl.BlockSpec((count, 1, 1, deep, LANES), lambda x, c: (0, x, c, 0, 0)),
        scratch_shapes=[pltpu.VMEM((nz, LANES), F32)],
        compiler_params=params(),
        cost_estimate=pl.CostEstimate(
            flops=0, bytes_accessed=coils * 2 * planes * ny * nz * 4, transcendentals=0
        ),
        name="maps_columns",
    )(coil_maps)


def last_maps_columns(coil_maps, count, first, coils):
    _, _, planes, ny, nz = coil_maps.shape
    deep = nz // count
    sizes = (coils + 1, coils - 1)
    return pl.pallas_call(
        functools.partial(last_maps_kernel, count, deep, coils),
        out_shape=[jax.ShapeDtypeStruct((count, planes, n, deep // 2, LANES), BF) for n in sizes],
        grid=(planes, coils),
        in_specs=[pl.BlockSpec((1, 2, 1, ny, nz), lambda x, c: (first + c, 0, x, 0, 0))],
        out_specs=[
            pl.BlockSpec((count, 1, n, deep // 2, LANES), lambda x, c: (0, x, 0, 0, 0))
            for n in sizes
        ],
        scratch_shapes=[pltpu.VMEM((nz, LANES), F32)],
        compiler_params=params(),
        cost_estimate=pl.CostEstimate(
            flops=0, bytes_accessed=coils * 2 * planes * ny * nz * 4, transcendentals=0
        ),
        name="last_maps_columns",
    )(coil_maps)


def low_half(shape):
    return lax.broadcasted_iota(jnp.int32, shape, len(shape) - 1) < BLK


def fetch(w_hbm, held, sems, k):
    size = held.shape[0] // sems.shape[0]
    source = w_hbm.at[pl.ds(k * (size + TAIL), size)]
    return pltpu.make_async_copy(source, held.at[pl.ds(k * size, size)], sems.at[k])


def fetch_all(w_hbm, held, sems):
    for k in range(sems.shape[0]):
        fetch(w_hbm, held, sems, k).start()


def warp_kernel(nx, deep, pad, links, owner, g_ref, w_hbm, o_ref, held, twice, sems):
    fetch_all(w_hbm, held, sems)
    count = sems.shape[0]
    planes = nx // count
    low = low_half((deep, 128))

    def split(x, carry):
        for v in range(3):
            row = g_ref[x, :, v * 128 : (v + 1) * 128].astype(F32)
            turned = pltpu.roll(row, BLK, 1)
            first = jnp.where(low, row, turned).astype(BF)
            second = jnp.where(low, turned, row).astype(BF)
            if v < 2:
                twice[3 * x, pl.ds(v * pad, deep), :] = first
                twice[3 * x + 1, pl.ds(v * pad, deep), :] = second
            else:
                twice[3 * x + 2, pl.ds(0, deep), :] = first
                twice[3 * x + 2, pl.ds(pad, deep), :] = second
        return carry

    lax.fori_loop(0, nx, split, 0, unroll=8)
    low_both = low_half((2 * pad, 128))

    def block(k, carry):
        fetch(w_hbm, held, sems, k).wait()
        row = owner[k] * planes
        start = k * 3 * planes
        for x in range(planes):
            outs = []
            for b in range(3):
                t = 3 * x + b
                one, two = links[2 * start + t], links[2 * start + 3 * planes + t]
                both = jnp.where(low_both, twice[one], twice[two])
                weight = held[pl.ds((start + t) * BLK, BLK), :]
                outs.append(
                    lax.dot_general(
                        both, weight, (((1,), (1,)), ((), ())), preferred_element_type=F32
                    )
                )
            a, b, c = outs
            re = jnp.concatenate([a[:deep], b[:deep]], axis=1)
            im = jnp.concatenate([a[pad : pad + deep], b[pad : pad + deep]], axis=1)
            rest = jnp.concatenate([c[:deep], c[pad : pad + deep]], axis=1)
            o_ref[row + x, :, 0:128] = re
            o_ref[row + x, :, 128:256] = im
            o_ref[row + x, :, 256:384] = rest
        return carry

    lax.fori_loop(0, count, block, 0)


def warp(columns, weights, links, owner):
    nx, deep, _ = columns.shape
    blocks = 3 * nx
    pad = max(16, deep)
    whole = pl.BlockSpec((nx, deep, LANES), lambda i, l, p: (0, 0, 0))
    return pl.pallas_call(
        functools.partial(warp_kernel, nx, deep, pad),
        out_shape=jax.ShapeDtypeStruct((nx, deep, LANES), F32),
        grid_spec=pltpu.PrefetchScalarGridSpec(
            num_scalar_prefetch=2,
            grid=(1,),
            in_specs=[whole, pl.BlockSpec(memory_space=pl.ANY)],
            out_specs=whole,
            scratch_shapes=[
                pltpu.VMEM((blocks * BLK, 2 * BLK), BF),
                pltpu.VMEM((blocks, 2 * pad, 128), BF),
                pltpu.SemaphoreType.DMA((owner.shape[0],)),
            ],
        ),
        compiler_params=params(),
        cost_estimate=pl.CostEstimate(
            flops=2 * blocks * 256 * 256 * 32, bytes_accessed=20 << 20, transcendentals=0
        ),
        name="warp",
    )(links, owner, columns, weights)


def spread_kernel(nx, deep, pad, links, owner, c_ref, w_hbm, o_ref, held, total, sems):
    fetch_all(w_hbm, held, sems)
    count = sems.shape[0]
    planes = nx // count

    def clear(i, carry):
        total[pl.ds(i * 3, 3)] = jnp.zeros((3, 2 * pad, 128), F32)
        return carry

    lax.fori_loop(0, nx, clear, 0, unroll=8)
    low = low_half((2 * pad, 128))

    def tall(a, b):
        if deep == pad:
            return jnp.concatenate([a, b], axis=0)
        fill = jnp.zeros((pad - deep, a.shape[1]), a.dtype)
        return jnp.concatenate([a, fill, b, fill], axis=0)

    def block(k, carry):
        fetch(w_hbm, held, sems, k).wait()
        row = owner[k] * planes
        start = k * 3 * planes
        for x in range(planes):
            re, im, rest = (c_ref[row + x, :, v * 128 : (v + 1) * 128] for v in range(3))
            tiles = (
                tall(re[:, :BLK], im[:, :BLK]),
                tall(re[:, BLK:], im[:, BLK:]),
                tall(rest[:, :BLK], rest[:, BLK:]),
            )
            for b in range(3):
                t = 3 * x + b
                one, two = links[2 * start + t], links[2 * start + 3 * planes + t]
                weight = held[pl.ds((start + t) * BLK, BLK), :]
                out = jnp.dot(tiles[b].astype(BF), weight, preferred_element_type=F32)
                zero = jnp.zeros_like(out)
                total[one] += jnp.where(low, out, zero)
                total[two] += jnp.where(low, zero, out)
        return carry

    lax.fori_loop(0, count, block, 0)
    low_row = low_half((deep, 128))

    def gather(x, carry):
        sums = []
        for b in range(3):
            value = total[3 * x + b]
            sums.append(value + pltpu.roll(value, BLK, 1))
        a, b, c = sums
        o_ref[x, :, 0:128] = jnp.where(low_row, a[:deep], b[:deep]).astype(BF)
        o_ref[x, :, 128:256] = jnp.where(
            low_row, a[pad : pad + deep], b[pad : pad + deep]
        ).astype(BF)
        o_ref[x, :, 256:384] = jnp.where(low_row, c[:deep], c[pad : pad + deep]).astype(BF)
        return carry

    lax.fori_loop(0, nx, gather, 0, unroll=8)


def spread(combined, weights, links, owner):
    nx, deep, _ = combined.shape
    blocks = 3 * nx
    pad = max(8, deep)
    whole = pl.BlockSpec((nx, deep, LANES), lambda i, l, p: (0, 0, 0))
    return pl.pallas_call(
        functools.partial(spread_kernel, nx, deep, pad),
        out_shape=jax.ShapeDtypeStruct((nx, deep, LANES), BF),
        grid_spec=pltpu.PrefetchScalarGridSpec(
            num_scalar_prefetch=2,
            grid=(1,),
            in_specs=[whole, pl.BlockSpec(memory_space=pl.ANY)],
            out_specs=whole,
            scratch_shapes=[
                pltpu.VMEM((blocks * BLK, 2 * BLK), BF),
                pltpu.VMEM((blocks, 2 * pad, 128), F32),
                pltpu.SemaphoreType.DMA((owner.shape[0],)),
            ],
        ),
        compiler_params=params(),
        cost_estimate=pl.CostEstimate(
            flops=2 * blocks * 256 * 256 * 32, bytes_accessed=20 << 20, transcendentals=0
        ),
        name="spread",
    )(links, owner, combined, weights)


def coil_kernel(nx, deep, pad, fresh, *refs):
    if fresh:
        s_ref, w_ref, mask, iy, fx, bx, oy, o_ref, rows = refs
    else:
        s_ref, w_ref, mask, iy, fx, bx, oy, before, o_ref, rows = refs
    group = 8 if nx % 8 == 0 else 1
    cube = rows.reshape(3, nx, pad, 128)
    low = low_half((group, deep, 128))

    def thirds(ref, at):
        return tuple(ref[at, :, v * 128 : (v + 1) * 128].astype(F32) for v in range(3))

    def expand(i, carry):
        at = pl.ds(i * group, group)
        s0, s1, s2 = thirds(s_ref.at[:, 0], at)
        w0, w1, w2 = thirds(w_ref, at)
        turned = pltpu.roll(s2, BLK, 2)
        other = pltpu.roll(w2, BLK, 2)
        real = jnp.where(low, s2, turned)
        imag = jnp.where(low, turned, s2)
        cube[0, at, pl.ds(0, deep), :] = s0 * w0 - s1 * w1
        cube[1, at, pl.ds(0, deep), :] = s0 * w1 + s1 * w0
        cube[2, at, pl.ds(0, deep), :] = real * w2 + imag * jnp.where(low, -other, other)
        return carry

    lax.fori_loop(0, nx // group, expand, 0, unroll=4)

    batch = 4 if deep % 4 == 0 else 1

    def column(i, carry):
        ats = [pl.ds(i * batch + b, nx, stride=pad) for b in range(batch)]
        line = jnp.concatenate(
            [jnp.concatenate([rows[v, at, :] for v in range(3)], axis=1) for at in ats], axis=0
        ).astype(BF)
        y = jnp.dot(line, iy[...], preferred_element_type=F32).astype(BF)
        y = jnp.concatenate(
            [
                jnp.concatenate([y[b * nx : (b + 1) * nx, h * HALF : (h + 1) * HALF] for b in range(batch)], axis=1)
                for h in range(2)
            ],
            axis=0,
        )
        y = jnp.dot(fx[...], y, preferred_element_type=F32)
        y = jnp.concatenate([(y[:, b * HALF : (b + 1) * HALF] * mask[...]).astype(BF) for b in range(batch)], axis=1)
        y = jnp.dot(bx[...], y, preferred_element_type=F32).astype(BF)
        y = jnp.concatenate(
            [
                jnp.concatenate([y[h * nx : (h + 1) * nx, b * HALF : (b + 1) * HALF] for h in range(2)], axis=1)
                for b in range(batch)
            ],
            axis=0,
        )
        y = jnp.dot(y, oy[...], preferred_element_type=F32)
        for b, at in enumerate(ats):
            for v in range(3):
                rows[v, at, :] = y[b * nx : (b + 1) * nx, v * 128 : (v + 1) * 128]
        return carry

    lax.fori_loop(0, deep // batch, column, 0)

    first = pl.program_id(0) == 0

    def combine(i, carry):
        at = pl.ds(i * group, group)
        s0, s1, s2 = thirds(s_ref.at[:, 0], at)
        r0, r1, r2 = (cube[v, at, pl.ds(0, deep), :] for v in range(3))
        turned = pltpu.roll(s2, BLK, 2)
        other = pltpu.roll(r2, BLK, 2)
        real = jnp.where(low, s2, turned)
        imag = jnp.where(low, turned, s2)
        terms = (
            s0 * r0 + s1 * r1,
            s0 * r1 - s1 * r0,
            real * r2 + imag * jnp.where(low, other, -other),
        )
        for v in range(3):
            lanes = slice(v * 128, (v + 1) * 128)
            old = o_ref[at, :, lanes]
            start = jnp.zeros_like(old) if fresh else before[at, :, lanes]
            o_ref[at, :, lanes] = jnp.where(first, start, old) + terms[v]
        return carry

    lax.fori_loop(0, nx // group, combine, 0, unroll=4)


def coils(maps, first, count, warped, mask, tabs, before, part):
    nx, _, deep, _ = maps.shape
    pad = max(8, deep)
    fresh = before is None
    whole = lambda shape: pl.BlockSpec(
        shape, lambda c: (0,) * len(shape), pipeline_mode=pl.Buffered(1)
    )
    in_specs = [pl.BlockSpec((nx, 1, deep, LANES), lambda c: (0, first + c, 0, 0))]
    args = [maps, warped, mask, *tabs] + ([] if fresh else [before])
    def columns(array):
        at = part if array.shape[1] > deep else 0
        return pl.BlockSpec(
            (nx, deep, LANES), lambda c: (0, at, 0), pipeline_mode=pl.Buffered(1)
        )

    in_specs += [columns(warped)] + [whole(a.shape) for a in (mask, *tabs)]
    in_specs += [] if fresh else [columns(before)]
    return pl.pallas_call(
        functools.partial(coil_kernel, nx, deep, pad, fresh),
        out_shape=jax.ShapeDtypeStruct((nx, deep, LANES), F32),
        grid=(count,),
        in_specs=in_specs,
        out_specs=pl.BlockSpec((nx, deep, LANES), lambda c: (0, 0, 0)),
        scratch_shapes=[pltpu.VMEM((3, nx * pad, 128), F32)],
        compiler_params=params(),
        cost_estimate=pl.CostEstimate(
            flops=count * deep * 4 * 8 * nx * nx * 192 * 2,
            bytes_accessed=count * nx * deep * LANES * 2 + (14 << 20),
            transcendentals=0,
        ),
        name="coils",
    )(*args)


def update_kernel(count, b_ref, i_ref, a_ref, *refs):
    o_ref, scratch = refs[-2:]
    part = b_ref.shape[2]
    for x in range(o_ref.shape[1]):
        for d in range(count):
            scratch[x, pl.ds(d * part, part), :] = b_ref[d, x].astype(F32)
        grad = scratch[x].astype(BF).T.astype(F32)
        real = jnp.concatenate([grad[0:128], grad[256:320]], axis=0)
        imag = jnp.concatenate([grad[128:256], grad[320:384]], axis=0)
        for p, value in enumerate((real, imag)):
            o_ref[p, x] = i_ref[p, x] - 0.5 * (value - a_ref[p, x].astype(F32))


def update(back, image, adjoint, part, before):
    count, planes, deep, _ = back.shape
    _, _, ny, _ = image.shape
    lanes = count * deep
    group = 3 if planes % 3 == 0 else 1
    block = pl.BlockSpec((2, group, ny, lanes), lambda x: (0, x, 0, part))
    more = [] if before is None else [before]
    return pl.pallas_call(
        functools.partial(update_kernel, count),
        out_shape=jax.ShapeDtypeStruct(image.shape, F32),
        grid=(planes // group,),
        in_specs=[
            pl.BlockSpec((count, group, deep, LANES), lambda x: (0, x, 0, 0)),
            block,
            block,
        ]
        + [pl.BlockSpec(memory_space=pl.ANY)] * len(more),
        out_specs=block,
        scratch_shapes=[pltpu.VMEM((group, lanes, LANES), F32)],
        input_output_aliases={3: 0} if more else {},
        compiler_params=params(),
        cost_estimate=pl.CostEstimate(
            flops=0, bytes_accessed=2 * planes * ny * lanes * 12, transcendentals=0
        ),
        name="update",
    )(back, image, adjoint, *more)


def exchange(parts):
    return lax.all_to_all(parts, "slab", split_axis=0, concat_axis=0, tiled=True)


def after(value, *others):
    return lax.optimization_barrier((value, *others))[0]


def swap_halves(value):
    count = lax.axis_size("slab")
    half = count // 2
    other = lax.ppermute(value, "slab", [(i, i ^ half) for i in range(count)])
    return jnp.concatenate([value, other], axis=0)


def gather_half(pair):
    count = lax.axis_size("slab")
    half = count // 2
    groups = [list(range(half)), list(range(half, count))]
    gathered = lax.all_gather(pair, "slab", axis=0, tiled=True, axis_index_groups=groups)
    mine = lax.axis_index("slab") // half
    place = jnp.arange(count, dtype=jnp.int32)
    return gathered, place // 2 + half * ((place % 2) ^ mine)


def per_device(image, adjoint_data, coil_maps, masks, sources, weights):
    count = lax.axis_size("slab")
    planes, ny, nz = image.shape[1:]
    nx = planes * count
    deep = nz // count
    total = coil_maps.shape[0]
    tabs = tables(nx, ny)
    sampled = jnp.pad(masks[0].astype(F32), ((0, 0), (0, HALF - ny)))
    mask = jnp.concatenate([sampled, sampled], axis=0)

    targets = 3 * planes
    matrices = weights[0].reshape(targets, 2, BLK, BLK)
    matrices = jnp.transpose(matrices, (0, 2, 1, 3)).reshape(targets * BLK, 2 * BLK)
    chosen = sources[0].T
    digits = jnp.concatenate([chosen // BLK, chosen % BLK], axis=0).astype(BF)
    digits = jnp.pad(digits, ((0, TAIL - 4), (0, 2 * BLK - targets)))
    pair = swap_halves(jnp.concatenate([matrices, digits], axis=0))
    packed, owner = gather_half(pair)
    digits = packed.reshape(count, targets * BLK + TAIL, 2 * BLK)[:, targets * BLK :]
    digits = digits[:, :4, :targets].astype(jnp.int32)
    links = (digits[:, :2] * BLK + digits[:, 2:]).reshape(-1)

    def run(received, first, size, before, part):
        maps = received.reshape(nx, received.shape[2], -1, LANES)
        return coils(maps, first, size, warped, mask, tabs, before, part)

    def back(combined, *needs):
        grad = spread(combined, packed, links, owner)
        return exchange(after(grad, *needs).reshape(count, planes, -1, LANES))

    columns = exchange(image_columns(image, count))
    warped = warp(columns.reshape(nx, deep, LANES), packed, links, owner)
    halves = parts_of(deep) == 2
    early = total - 3 * total // 8 if halves else total - 1
    late = total - early
    maps = maps_columns(coil_maps, count, 0, early)
    arrived = exchange(after(maps, columns, pair))
    if not halves:
        maps = maps_columns(coil_maps, count, early, late)
        last = exchange(after(maps, arrived, warped))
        combined = run(last, 0, late, run(arrived, 0, early, None, 0), 0)
        return update(back(combined), image, adjoint_data, 0, None)

    first, second = last_maps_columns(coil_maps, count, early, late)
    first = exchange(after(first, arrived, warped))
    combined = run(arrived, 0, early, None, 0)
    second = exchange(after(second, first, combined))
    half_first = run(first, 0, late, combined, 0)
    half_second = run(first, late, 1, combined, 1)
    back_first = back(half_first, second, half_second)
    half_second = run(second, 0, late - 1, half_second, 1)
    back_second = back(half_second, back_first)
    result = update(back_first, image, adjoint_data, 0, None)
    return update(back_second, image, adjoint_data, 1, result)


def solution(mesh):
    return jax.shard_map(
        per_device,
        mesh=mesh,
        in_specs=(
            P(None, ("grp", "slab"), None, None),
            P(None, ("grp", "slab"), None, None),
            P(None, None, ("grp", "slab"), None, None),
            P(None, "grp", None),
            P(None, ("grp", "slab"), None),
            P(None, ("grp", "slab"), None),
        ),
        out_specs=P(None, ("grp", "slab"), None, None),
        check_vma=False,
    )
```

```python
import functools
import math

import jax
import jax.numpy as jnp
import numpy as np
from jax import lax
from jax.experimental import pallas as pl
from jax.experimental.pallas import tpu as pltpu
from jax.sharding import PartitionSpec as P

BLK = 64
LANES = 384
TAIL = 16
HALF = 256
VMEM_LIMIT = 48 * 1024 * 1024
BF = jnp.bfloat16
F32 = jnp.float32


def lane_order(length):
    lo, rest = 128, length - 128
    part = np.concatenate([np.zeros(lo), np.ones(lo), np.zeros(rest), np.ones(rest)])
    pos = np.concatenate([np.arange(lo), np.arange(lo), lo + np.arange(rest), lo + np.arange(rest)])
    return part.astype(np.int32), pos.astype(np.int32)


def dft_table(length, direction):
    positions = np.arange(length)
    phases = (positions[:, None] * positions[None, :] % length).astype(np.float32)
    phases = phases * np.float32(2.0 * math.pi / length)
    factor = np.float32(1.0 / math.sqrt(length))
    cosine = np.cos(phases) * factor
    sine = np.sin(phases) * (np.float32(direction) * factor)
    upper = np.stack([cosine, -sine], axis=1)
    lower = np.stack([sine, cosine], axis=1)
    return np.stack([upper, lower], axis=0)


def tables(nx, ny):
    part, pos = lane_order(ny)
    fwd_y, inv_y = dft_table(ny, -1.0), dft_table(ny, 1.0)
    into_y = np.zeros((2 * ny, 2, HALF), np.float32)
    into_y[:, :, :ny] = np.transpose(fwd_y[:, :, part, pos], (2, 0, 1))
    from_y = np.zeros((2, HALF, 2 * ny), np.float32)
    from_y[:, :ny, :] = np.transpose(inv_y[part, pos], (1, 2, 0))
    fwd_x = dft_table(nx, -1.0).reshape(2 * nx, 2 * nx)
    inv_x = dft_table(nx, 1.0).reshape(2 * nx, 2 * nx)
    out = (into_y.reshape(2 * ny, 2 * HALF), fwd_x, inv_x, from_y.reshape(2 * HALF, 2 * ny))
    return tuple(jnp.asarray(t, BF) for t in out)


def params():
    return pltpu.CompilerParams(vmem_limit_bytes=VMEM_LIMIT)


def in_vmem(array):
    return pltpu.with_memory_space_constraint(array, pltpu.VMEM)


def to_rows(parts):
    stacked = jnp.concatenate(
        [parts[0, :128], parts[1, :128], parts[0, 128:], parts[1, 128:]], axis=0
    )
    return stacked.T


def part_rows(scratch, count, deep, parts, d, h):
    part = deep // parts
    return scratch[pl.ds((h * count + d) * part, part), :]


def spread_rows(out, scratch, count, deep, parts):
    for d in range(count):
        rows = [part_rows(scratch, count, deep, parts, d, h) for h in range(parts)]
        out[d] = jnp.concatenate(rows, axis=0).astype(BF)


def parts_of(deep):
    return 2 if deep % 16 == 0 else 1


def image_kernel(count, deep, x_ref, o_ref, scratch):
    for x in range(x_ref.shape[1]):
        scratch[x] = to_rows(x_ref[:, x].astype(BF)).astype(F32)
        spread_rows(o_ref.at[:, x], scratch.at[x], count, deep, parts_of(deep))


def image_columns(image, count):
    _, planes, ny, nz = image.shape
    deep = nz // count
    group = 3 if planes % 3 == 0 else 1
    return pl.pallas_call(
        functools.partial(image_kernel, count, deep),
        out_shape=jax.ShapeDtypeStruct((count, planes, deep, LANES), BF),
        grid=(planes // group,),
        in_specs=[pl.BlockSpec((2, group, ny, nz), lambda x: (0, x, 0, 0))],
        out_specs=pl.BlockSpec((count, group, deep, LANES), lambda x: (0, x, 0, 0)),
        scratch_shapes=[pltpu.VMEM((group, nz, LANES), F32)],
        compiler_params=params(),
        cost_estimate=pl.CostEstimate(flops=0, bytes_accessed=image.size * 6, transcendentals=0),
        name="image_columns",
    )(image)


def maps_kernel(count, deep, x_ref, o_ref, scratch):
    scratch[...] = to_rows(x_ref[0, :, 0]).astype(F32)
    spread_rows(o_ref.at[:, 0, 0], scratch, count, deep, parts_of(deep))


def last_maps_kernel(count, deep, coils, x_ref, first_ref, second_ref, scratch):
    scratch[...] = to_rows(x_ref[0, :, 0]).astype(F32)
    for c in range(coils):

        @pl.when(pl.program_id(1) == c)
        def _():
            for d in range(count):
                half = part_rows(scratch, count, deep, 2, d, 1).astype(BF)
                first_ref[d, 0, c] = part_rows(scratch, count, deep, 2, d, 0).astype(BF)
                if c == 0:
                    first_ref[d, 0, coils] = half
                else:
                    second_ref[d, 0, c - 1] = half


def maps_columns(coil_maps, count, first, coils):
    _, _, planes, ny, nz = coil_maps.shape
    deep = nz // count
    return pl.pallas_call(
        functools.partial(maps_kernel, count, deep),
        out_shape=jax.ShapeDtypeStruct((count, planes, coils, deep, LANES), BF),
        grid=(planes, coils),
        in_specs=[pl.BlockSpec((1, 2, 1, ny, nz), lambda x, c: (first + c, 0, x, 0, 0))],
        out_specs=pl.BlockSpec((count, 1, 1, deep, LANES), lambda x, c: (0, x, c, 0, 0)),
        scratch_shapes=[pltpu.VMEM((nz, LANES), F32)],
        compiler_params=params(),
        cost_estimate=pl.CostEstimate(
            flops=0, bytes_accessed=coils * 2 * planes * ny * nz * 4, transcendentals=0
        ),
        name="maps_columns",
    )(coil_maps)


def last_maps_columns(coil_maps, count, first, coils):
    _, _, planes, ny, nz = coil_maps.shape
    deep = nz // count
    sizes = (coils + 1, coils - 1)
    return pl.pallas_call(
        functools.partial(last_maps_kernel, count, deep, coils),
        out_shape=[jax.ShapeDtypeStruct((count, planes, n, deep // 2, LANES), BF) for n in sizes],
        grid=(planes, coils),
        in_specs=[pl.BlockSpec((1, 2, 1, ny, nz), lambda x, c: (first + c, 0, x, 0, 0))],
        out_specs=[
            pl.BlockSpec((count, 1, n, deep // 2, LANES), lambda x, c: (0, x, 0, 0, 0))
            for n in sizes
        ],
        scratch_shapes=[pltpu.VMEM((nz, LANES), F32)],
        compiler_params=params(),
        cost_estimate=pl.CostEstimate(
            flops=0, bytes_accessed=coils * 2 * planes * ny * nz * 4, transcendentals=0
        ),
        name="last_maps_columns",
    )(coil_maps)


def low_half(shape):
    return lax.broadcasted_iota(jnp.int32, shape, len(shape) - 1) < BLK


def fetch(w_hbm, held, sems, k):
    size = held.shape[0] // sems.shape[0]
    source = w_hbm.at[pl.ds(k * (size + TAIL), size)]
    return pltpu.make_async_copy(source, held.at[pl.ds(k * size, size)], sems.at[k])


def fetch_all(w_hbm, held, sems):
    for k in range(sems.shape[0]):
        fetch(w_hbm, held, sems, k).start()


def warp_kernel(nx, deep, pad, links, owner, g_ref, w_hbm, o_ref, held, twice, sems):
    fetch_all(w_hbm, held, sems)
    count = sems.shape[0]
    planes = nx // count
    low = low_half((deep, 128))

    def split(x, carry):
        for v in range(3):
            row = g_ref[x, :, v * 128 : (v + 1) * 128].astype(F32)
            turned = pltpu.roll(row, BLK, 1)
            first = jnp.where(low, row, turned).astype(BF)
            second = jnp.where(low, turned, row).astype(BF)
            if v < 2:
                twice[3 * x, pl.ds(v * pad, deep), :] = first
                twice[3 * x + 1, pl.ds(v * pad, deep), :] = second
            else:
                twice[3 * x + 2, pl.ds(0, deep), :] = first
                twice[3 * x + 2, pl.ds(pad, deep), :] = second
        return carry

    lax.fori_loop(0, nx, split, 0, unroll=8)
    low_both = low_half((2 * pad, 128))

    def block(k, carry):
        fetch(w_hbm, held, sems, k).wait()
        row = owner[k] * planes
        start = k * 3 * planes
        for x in range(planes):
            outs = []
            for b in range(3):
                t = 3 * x + b
                one, two = links[2 * start + t], links[2 * start + 3 * planes + t]
                both = jnp.where(low_both, twice[one], twice[two])
                weight = held[pl.ds((start + t) * BLK, BLK), :]
                outs.append(
                    lax.dot_general(
                        both, weight, (((1,), (1,)), ((), ())), preferred_element_type=F32
                    )
                )
            a, b, c = outs
            re = jnp.concatenate([a[:deep], b[:deep]], axis=1)
            im = jnp.concatenate([a[pad : pad + deep], b[pad : pad + deep]], axis=1)
            rest = jnp.concatenate([c[:deep], c[pad : pad + deep]], axis=1)
            o_ref[row + x, :, 0:128] = re
            o_ref[row + x, :, 128:256] = im
            o_ref[row + x, :, 256:384] = rest
        return carry

    lax.fori_loop(0, count, block, 0)


def warp(columns, weights, links, owner):
    nx, deep, _ = columns.shape
    blocks = 3 * nx
    pad = max(16, deep)
    whole = pl.BlockSpec((nx, deep, LANES), lambda i, l, p: (0, 0, 0))
    return pl.pallas_call(
        functools.partial(warp_kernel, nx, deep, pad),
        out_shape=jax.ShapeDtypeStruct((nx, deep, LANES), F32),
        grid_spec=pltpu.PrefetchScalarGridSpec(
            num_scalar_prefetch=2,
            grid=(1,),
            in_specs=[pl.BlockSpec(memory_space=pltpu.VMEM), pl.BlockSpec(memory_space=pl.ANY)],
            out_specs=whole,
            scratch_shapes=[
                pltpu.VMEM((blocks * BLK, 2 * BLK), BF),
                pltpu.VMEM((blocks, 2 * pad, 128), BF),
                pltpu.SemaphoreType.DMA((owner.shape[0],)),
            ],
        ),
        compiler_params=params(),
        cost_estimate=pl.CostEstimate(
            flops=2 * blocks * 256 * 256 * 32, bytes_accessed=20 << 20, transcendentals=0
        ),
        name="warp",
    )(links, owner, in_vmem(columns), weights)


def spread(nx, deep, pad, links, owner, c_ref, w_hbm, o_ref, held, total, sems):
    count = sems.shape[0]
    planes = nx // count

    def clear(i, carry):
        total[pl.ds(i * 3, 3)] = jnp.zeros((3, 2 * pad, 128), F32)
        return carry

    lax.fori_loop(0, nx, clear, 0, unroll=8)
    low = low_half((2 * pad, 128))

    def tall(a, b):
        if deep == pad:
            return jnp.concatenate([a, b], axis=0)
        fill = jnp.zeros((pad - deep, a.shape[1]), a.dtype)
        return jnp.concatenate([a, fill, b, fill], axis=0)

    def block(k, carry):
        fetch(w_hbm, held, sems, k).wait()
        row = owner[k] * planes
        start = k * 3 * planes
        for x in range(planes):
            re, im, rest = (c_ref[row + x, :, v * 128 : (v + 1) * 128] for v in range(3))
            tiles = (
                tall(re[:, :BLK], im[:, :BLK]),
                tall(re[:, BLK:], im[:, BLK:]),
                tall(rest[:, :BLK], rest[:, BLK:]),
            )
            for b in range(3):
                t = 3 * x + b
                one, two = links[2 * start + t], links[2 * start + 3 * planes + t]
                weight = held[pl.ds((start + t) * BLK, BLK), :]
                out = jnp.dot(tiles[b].astype(BF), weight, preferred_element_type=F32)
                zero = jnp.zeros_like(out)
                total[one] += jnp.where(low, out, zero)
                total[two] += jnp.where(low, zero, out)
        return carry

    lax.fori_loop(0, count, block, 0)
    low_row = low_half((deep, 128))

    def gather(x, carry):
        sums = []
        for b in range(3):
            value = total[3 * x + b]
            sums.append(value + pltpu.roll(value, BLK, 1))
        a, b, c = sums
        o_ref[x, :, 0:128] = jnp.where(low_row, a[:deep], b[:deep]).astype(BF)
        o_ref[x, :, 128:256] = jnp.where(
            low_row, a[pad : pad + deep], b[pad : pad + deep]
        ).astype(BF)
        o_ref[x, :, 256:384] = jnp.where(low_row, c[:deep], c[pad : pad + deep]).astype(BF)
        return carry

    lax.fori_loop(0, nx, gather, 0, unroll=8)


def coil_kernel(nx, deep, pad, fresh, ends, landed, *refs):
    if ends:
        links, owner, *refs = refs
    s_ref, w_ref, mask, iy, fx, bx, oy, *refs = refs
    if not fresh:
        before, *refs = refs
    if ends:
        w_hbm, grad_ref, rows, o_ref, held, total, sems = refs

        @pl.when(pl.program_id(0) == 0)
        def _():
            fetch_all(w_hbm, held, sems)
    else:
        o_ref, rows = refs
    s_ref = s_ref.at[:, pl.program_id(0) if landed else 0]
    group = 8 if nx % 8 == 0 else 1
    cube = rows.reshape(3, nx, pad, 128)
    low = low_half((group, deep, 128))

    def thirds(ref, at):
        return tuple(ref[at, :, v * 128 : (v + 1) * 128].astype(F32) for v in range(3))

    def expand(i, carry):
        at = pl.ds(i * group, group)
        s0, s1, s2 = thirds(s_ref, at)
        w0, w1, w2 = thirds(w_ref, at)
        turned = pltpu.roll(s2, BLK, 2)
        other = pltpu.roll(w2, BLK, 2)
        real = jnp.where(low, s2, turned)
        imag = jnp.where(low, turned, s2)
        cube[0, at, pl.ds(0, deep), :] = s0 * w0 - s1 * w1
        cube[1, at, pl.ds(0, deep), :] = s0 * w1 + s1 * w0
        cube[2, at, pl.ds(0, deep), :] = real * w2 + imag * jnp.where(low, -other, other)
        return carry

    lax.fori_loop(0, nx // group, expand, 0, unroll=4)

    batch = 4 if deep % 4 == 0 else 1

    def column(i, carry):
        ats = [pl.ds(i * batch + b, nx, stride=pad) for b in range(batch)]
        line = jnp.concatenate(
            [jnp.concatenate([rows[v, at, :] for v in range(3)], axis=1) for at in ats], axis=0
        ).astype(BF)
        y = jnp.dot(line, iy[...], preferred_element_type=F32).astype(BF)
        y = jnp.concatenate(
            [
                jnp.concatenate([y[b * nx : (b + 1) * nx, h * HALF : (h + 1) * HALF] for b in range(batch)], axis=1)
                for h in range(2)
            ],
            axis=0,
        )
        y = jnp.dot(fx[...], y, preferred_element_type=F32)
        y = jnp.concatenate([(y[:, b * HALF : (b + 1) * HALF] * mask[...]).astype(BF) for b in range(batch)], axis=1)
        y = jnp.dot(bx[...], y, preferred_element_type=F32).astype(BF)
        y = jnp.concatenate(
            [
                jnp.concatenate([y[h * nx : (h + 1) * nx, b * HALF : (b + 1) * HALF] for h in range(2)], axis=1)
                for b in range(batch)
            ],
            axis=0,
        )
        y = jnp.dot(y, oy[...], preferred_element_type=F32)
        for b, at in enumerate(ats):
            for v in range(3):
                rows[v, at, :] = y[b * nx : (b + 1) * nx, v * 128 : (v + 1) * 128]
        return carry

    lax.fori_loop(0, deep // batch, column, 0)

    first = pl.program_id(0) == 0

    def combine(i, carry):
        at = pl.ds(i * group, group)
        s0, s1, s2 = thirds(s_ref, at)
        r0, r1, r2 = (cube[v, at, pl.ds(0, deep), :] for v in range(3))
        turned = pltpu.roll(s2, BLK, 2)
        other = pltpu.roll(r2, BLK, 2)
        real = jnp.where(low, s2, turned)
        imag = jnp.where(low, turned, s2)
        terms = (
            s0 * r0 + s1 * r1,
            s0 * r1 - s1 * r0,
            real * r2 + imag * jnp.where(low, other, -other),
        )
        for v in range(3):
            lanes = slice(v * 128, (v + 1) * 128)
            old = o_ref[at, :, lanes]
            start = jnp.zeros_like(old) if fresh else before[at, :, lanes]
            o_ref[at, :, lanes] = jnp.where(first, start, old) + terms[v]
        return carry

    lax.fori_loop(0, nx // group, combine, 0, unroll=4)
    if ends:

        @pl.when(pl.program_id(0) == pl.num_programs(0) - 1)
        def _():
            spread(nx, deep, pad, links, owner, o_ref, w_hbm, grad_ref, held, total, sems)


def coils(maps, first, count, warped, mask, tabs, before, part, warping=None, landed=False):
    nx, _, deep, _ = maps.shape
    pad = max(8, deep)
    fresh, ends = before is None, warping is not None

    def whole(shape):
        return pl.BlockSpec(shape, lambda c, *_: (0,) * len(shape), pipeline_mode=pl.Buffered(1))

    def columns(array):
        at = part if array.shape[1] > deep else 0
        return pl.BlockSpec(
            (nx, deep, LANES), lambda c, *_: (0, at, 0), pipeline_mode=pl.Buffered(1)
        )

    if landed:
        maps = in_vmem(maps)
        in_specs = [pl.BlockSpec(memory_space=pltpu.VMEM)]
    else:
        in_specs = [pl.BlockSpec((nx, 1, deep, LANES), lambda c, *_: (0, first + c, 0, 0))]
    args = [maps, warped, mask, *tabs]
    in_specs += [columns(warped)] + [whole(a.shape) for a in (mask, *tabs)]
    if not fresh:
        args += [before]
        in_specs += [columns(before)]
    scratch = [pltpu.VMEM((3, nx * pad, 128), F32)]
    prefetched = []
    if ends:
        weights, *prefetched = warping
        args += [weights]
        in_specs += [pl.BlockSpec(memory_space=pl.ANY)]
        scratch += [
            pltpu.VMEM((nx, deep, LANES), F32),
            pltpu.VMEM((3 * nx * BLK, 2 * BLK), BF),
            pltpu.VMEM((3 * nx, 2 * pad, 128), F32),
            pltpu.SemaphoreType.DMA((prefetched[1].shape[0],)),
        ]
    return pl.pallas_call(
        functools.partial(coil_kernel, nx, deep, pad, fresh, ends, landed),
        out_shape=jax.ShapeDtypeStruct((nx, deep, LANES), BF if ends else F32),
        grid_spec=pltpu.PrefetchScalarGridSpec(
            num_scalar_prefetch=len(prefetched),
            grid=(count,),
            in_specs=in_specs,
            out_specs=pl.BlockSpec((nx, deep, LANES), lambda c, *_: (0, 0, 0)),
            scratch_shapes=scratch,
        ),
        compiler_params=params(),
        cost_estimate=pl.CostEstimate(
            flops=count * deep * 4 * 8 * nx * nx * 192 * 2,
            bytes_accessed=count * nx * deep * LANES * 2 + (14 << 20),
            transcendentals=0,
        ),
        name="coils",
    )(*prefetched, *args)


def update_kernel(count, b_ref, i_ref, a_ref, *refs):
    o_ref, scratch = refs[-2:]
    part = b_ref.shape[2]
    group = o_ref.shape[1]
    for x in range(group):
        plane = pl.program_id(0) * group + x
        for d in range(count):
            scratch[x, pl.ds(d * part, part), :] = b_ref[d, plane].astype(F32)
        grad = scratch[x].astype(BF).T.astype(F32)
        real = jnp.concatenate([grad[0:128], grad[256:320]], axis=0)
        imag = jnp.concatenate([grad[128:256], grad[320:384]], axis=0)
        for p, value in enumerate((real, imag)):
            o_ref[p, x] = i_ref[p, x] - 0.5 * (value - a_ref[p, x].astype(F32))


def update(back, image, adjoint, part, before):
    count, planes, deep, _ = back.shape
    _, _, ny, _ = image.shape
    lanes = count * deep
    group = 3 if planes % 3 == 0 else 1
    block = pl.BlockSpec((2, group, ny, lanes), lambda x: (0, x, 0, part))
    more = [] if before is None else [before]
    return pl.pallas_call(
        functools.partial(update_kernel, count),
        out_shape=jax.ShapeDtypeStruct(image.shape, F32),
        grid=(planes // group,),
        in_specs=[
            pl.BlockSpec(memory_space=pltpu.VMEM),
            block,
            block,
        ]
        + [pl.BlockSpec(memory_space=pl.ANY)] * len(more),
        out_specs=block,
        scratch_shapes=[pltpu.VMEM((group, lanes, LANES), F32)],
        input_output_aliases={3: 0} if more else {},
        compiler_params=params(),
        cost_estimate=pl.CostEstimate(
            flops=0, bytes_accessed=2 * planes * ny * lanes * 12, transcendentals=0
        ),
        name="update",
    )(in_vmem(back), image, adjoint, *more)


def exchange(parts):
    return lax.all_to_all(parts, "slab", split_axis=0, concat_axis=0, tiled=True)


def after(value, *others):
    return lax.optimization_barrier((value, *others))[0]


def swap_halves(value):
    count = lax.axis_size("slab")
    half = count // 2
    return lax.ppermute(value, "slab", [(i, i ^ half) for i in range(count)])


def gather_half(pair):
    count = lax.axis_size("slab")
    half = count // 2
    groups = [list(range(half)), list(range(half, count))]
    gathered = lax.all_gather(pair, "slab", axis=0, tiled=True, axis_index_groups=groups)
    mine = lax.axis_index("slab") // half
    place = jnp.arange(count, dtype=jnp.int32)
    return gathered, place // 2 + half * ((place % 2) ^ mine)


def per_device(image, adjoint_data, coil_maps, masks, sources, weights):
    count = lax.axis_size("slab")
    planes, ny, nz = image.shape[1:]
    nx = planes * count
    deep = nz // count
    total = coil_maps.shape[0]
    tabs = tables(nx, ny)
    sampled = jnp.pad(masks[0].astype(F32), ((0, 0), (0, HALF - ny)))
    mask = jnp.concatenate([sampled, sampled], axis=0)

    targets = 3 * planes
    matrices = weights[0].reshape(targets, 2, BLK, BLK)
    matrices = jnp.transpose(matrices, (0, 2, 1, 3)).reshape(targets * BLK, 2 * BLK)
    chosen = sources[0].T
    digits = jnp.concatenate([chosen // BLK, chosen % BLK], axis=0).astype(BF)
    digits = jnp.pad(digits, ((0, TAIL - 4), (0, 2 * BLK - targets)))
    own = jnp.concatenate([matrices, digits], axis=0)
    crossed = swap_halves(own)
    packed, owner = gather_half(jnp.concatenate([own, crossed], axis=0))
    digits = packed.reshape(count, targets * BLK + TAIL, 2 * BLK)[:, targets * BLK :]
    digits = digits[:, :4, :targets].astype(jnp.int32)
    links = (digits[:, :2] * BLK + digits[:, 2:]).reshape(-1)

    def run(received, first, size, before, part, **more):
        maps = received.reshape(nx, received.shape[2], -1, LANES)
        return coils(maps, first, size, warped, mask, tabs, before, part, **more)

    def back(grad, *needs):
        return exchange(after(grad, *needs).reshape(count, planes, -1, LANES))

    columns = exchange(image_columns(image, count))
    warped = warp(columns.reshape(nx, deep, LANES), packed, links, owner)
    warping = (packed, links, owner)
    halves = parts_of(deep) == 2
    early = total - 3 * total // 8 if halves else total - 1
    late = total - early
    maps = maps_columns(coil_maps, count, 0, early)
    arrived = exchange(after(maps, columns, crossed))
    if not halves:
        maps = maps_columns(coil_maps, count, early, late)
        last = exchange(after(maps, arrived, warped))
        combined = run(arrived, 0, early, None, 0)
        grad = run(last, 0, late, combined, 0, warping=warping)
        return update(back(grad), image, adjoint_data, 0, None)

    first, second = last_maps_columns(coil_maps, count, early, late)
    first = exchange(after(first, arrived, warped))
    combined = run(arrived, 0, early, None, 0)
    second = exchange(after(second, first, combined))
    grad = run(first, 0, late, combined, 0, warping=warping)
    half = run(first, late, 1, combined, 1)
    back_first = back(grad, second, half)
    grad = run(second, 0, late - 1, half, 1, warping=warping, landed=True)
    back_second = back(grad, back_first)
    result = update(back_first, image, adjoint_data, 0, None)
    return update(back_second, image, adjoint_data, 1, result)


def solution(mesh):
    return jax.shard_map(
        per_device,
        mesh=mesh,
        in_specs=(
            P(None, ("grp", "slab"), None, None),
            P(None, ("grp", "slab"), None, None),
            P(None, None, ("grp", "slab"), None, None),
            P(None, "grp", None),
            P(None, ("grp", "slab"), None),
            P(None, ("grp", "slab"), None),
        ),
        out_specs=P(None, ("grp", "slab"), None, None),
        check_vma=False,
    )
```

```python
import functools
import math

import jax
import jax.numpy as jnp
import numpy as np
from jax import lax
from jax.experimental import pallas as pl
from jax.experimental.pallas import tpu as pltpu
from jax.sharding import PartitionSpec as P

BLK = 64
LANES = 384
TAIL = 16
HALF = 256
VMEM_LIMIT = 56 * 1024 * 1024
BF = jnp.bfloat16
F32 = jnp.float32


def lane_order(length):
    lo, rest = 128, length - 128
    part = np.concatenate([np.zeros(lo), np.ones(lo), np.zeros(rest), np.ones(rest)])
    pos = np.concatenate([np.arange(lo), np.arange(lo), lo + np.arange(rest), lo + np.arange(rest)])
    return part.astype(np.int32), pos.astype(np.int32)


def dft_table(length, direction):
    positions = np.arange(length)
    phases = (positions[:, None] * positions[None, :] % length).astype(np.float32)
    phases = phases * np.float32(2.0 * math.pi / length)
    factor = np.float32(1.0 / math.sqrt(length))
    cosine = np.cos(phases) * factor
    sine = np.sin(phases) * (np.float32(direction) * factor)
    upper = np.stack([cosine, -sine], axis=1)
    lower = np.stack([sine, cosine], axis=1)
    return np.stack([upper, lower], axis=0)


def tables(nx, ny):
    part, pos = lane_order(ny)
    fwd_y, inv_y = dft_table(ny, -1.0), dft_table(ny, 1.0)
    into_y = np.zeros((2 * ny, 2, HALF), np.float32)
    into_y[:, :, :ny] = np.transpose(fwd_y[:, :, part, pos], (2, 0, 1))
    from_y = np.zeros((2, HALF, 2 * ny), np.float32)
    from_y[:, :ny, :] = np.transpose(inv_y[part, pos], (1, 2, 0))
    fwd_x = dft_table(nx, -1.0).reshape(2 * nx, 2 * nx)
    inv_x = dft_table(nx, 1.0).reshape(2 * nx, 2 * nx)
    out = (into_y.reshape(2 * ny, 2 * HALF), fwd_x, inv_x, from_y.reshape(2 * HALF, 2 * ny))
    return tuple(jnp.asarray(t, BF) for t in out)


def params():
    return pltpu.CompilerParams(vmem_limit_bytes=VMEM_LIMIT)


def in_vmem(array):
    return pltpu.with_memory_space_constraint(array, pltpu.VMEM)


def to_rows(parts):
    stacked = jnp.concatenate(
        [parts[0, :128], parts[1, :128], parts[0, 128:], parts[1, 128:]], axis=0
    )
    return stacked.T


def part_rows(scratch, count, deep, parts, d, h):
    part = deep // parts
    return scratch[pl.ds((h * count + d) * part, part), :]


def spread_rows(out, scratch, count, deep, parts):
    for d in range(count):
        rows = [part_rows(scratch, count, deep, parts, d, h) for h in range(parts)]
        out[d] = jnp.concatenate(rows, axis=0).astype(BF)


def parts_of(deep):
    return 2 if deep % 16 == 0 else 1


def image_kernel(count, deep, x_ref, o_ref, scratch):
    for x in range(x_ref.shape[1]):
        scratch[x] = to_rows(x_ref[:, x].astype(BF)).astype(F32)
        spread_rows(o_ref.at[:, x], scratch.at[x], count, deep, parts_of(deep))


def image_columns(image, count):
    _, planes, ny, nz = image.shape
    deep = nz // count
    group = 3 if planes % 3 == 0 else 1
    return pl.pallas_call(
        functools.partial(image_kernel, count, deep),
        out_shape=jax.ShapeDtypeStruct((count, planes, deep, LANES), BF),
        grid=(planes // group,),
        in_specs=[pl.BlockSpec((2, group, ny, nz), lambda x: (0, x, 0, 0))],
        out_specs=pl.BlockSpec((count, group, deep, LANES), lambda x: (0, x, 0, 0)),
        scratch_shapes=[pltpu.VMEM((group, nz, LANES), F32)],
        compiler_params=params(),
        cost_estimate=pl.CostEstimate(flops=0, bytes_accessed=image.size * 6, transcendentals=0),
        name="image_columns",
    )(image)


def maps_kernel(count, deep, x_ref, o_ref, scratch):
    scratch[...] = to_rows(x_ref[0, :, 0]).astype(F32)
    spread_rows(o_ref.at[:, 0, 0], scratch, count, deep, parts_of(deep))


def last_maps_kernel(count, deep, coils, x_ref, first_ref, second_ref, scratch):
    scratch[...] = to_rows(x_ref[0, :, 0]).astype(F32)
    for c in range(coils):

        @pl.when(pl.program_id(1) == c)
        def _():
            for d in range(count):
                half = part_rows(scratch, count, deep, 2, d, 1).astype(BF)
                first_ref[d, 0, c] = part_rows(scratch, count, deep, 2, d, 0).astype(BF)
                if c == 0:
                    first_ref[d, 0, coils] = half
                else:
                    second_ref[d, 0, c - 1] = half


def maps_columns(coil_maps, count, first, coils):
    _, _, planes, ny, nz = coil_maps.shape
    deep = nz // count
    return pl.pallas_call(
        functools.partial(maps_kernel, count, deep),
        out_shape=jax.ShapeDtypeStruct((count, planes, coils, deep, LANES), BF),
        grid=(planes, coils),
        in_specs=[pl.BlockSpec((1, 2, 1, ny, nz), lambda x, c: (first + c, 0, x, 0, 0))],
        out_specs=pl.BlockSpec((count, 1, 1, deep, LANES), lambda x, c: (0, x, c, 0, 0)),
        scratch_shapes=[pltpu.VMEM((nz, LANES), F32)],
        compiler_params=params(),
        cost_estimate=pl.CostEstimate(
            flops=0, bytes_accessed=coils * 2 * planes * ny * nz * 4, transcendentals=0
        ),
        name="maps_columns",
    )(coil_maps)


def last_maps_columns(coil_maps, count, first, coils):
    _, _, planes, ny, nz = coil_maps.shape
    deep = nz // count
    sizes = (coils + 1, coils - 1)
    return pl.pallas_call(
        functools.partial(last_maps_kernel, count, deep, coils),
        out_shape=[jax.ShapeDtypeStruct((count, planes, n, deep // 2, LANES), BF) for n in sizes],
        grid=(planes, coils),
        in_specs=[pl.BlockSpec((1, 2, 1, ny, nz), lambda x, c: (first + c, 0, x, 0, 0))],
        out_specs=[
            pl.BlockSpec((count, 1, n, deep // 2, LANES), lambda x, c: (0, x, 0, 0, 0))
            for n in sizes
        ],
        scratch_shapes=[pltpu.VMEM((nz, LANES), F32)],
        compiler_params=params(),
        cost_estimate=pl.CostEstimate(
            flops=0, bytes_accessed=coils * 2 * planes * ny * nz * 4, transcendentals=0
        ),
        name="last_maps_columns",
    )(coil_maps)


def low_half(shape):
    return lax.broadcasted_iota(jnp.int32, shape, len(shape) - 1) < BLK


def fetch(w_hbm, held, sems, k):
    size = held.shape[0] // sems.shape[0]
    source = w_hbm.at[pl.ds(k * (size + TAIL), size)]
    return pltpu.make_async_copy(source, held.at[pl.ds(k * size, size)], sems.at[k])


def fetch_all(w_hbm, held, sems):
    for k in range(sems.shape[0]):
        fetch(w_hbm, held, sems, k).start()


def warp_kernel(nx, deep, pad, links, owner, g_ref, w_hbm, o_ref, held, twice, sems):
    fetch_all(w_hbm, held, sems)
    count = sems.shape[0]
    planes = nx // count
    low = low_half((deep, 128))

    def split(x, carry):
        for v in range(3):
            row = g_ref[x, :, v * 128 : (v + 1) * 128].astype(F32)
            turned = pltpu.roll(row, BLK, 1)
            first = jnp.where(low, row, turned).astype(BF)
            second = jnp.where(low, turned, row).astype(BF)
            if v < 2:
                twice[3 * x, pl.ds(v * pad, deep), :] = first
                twice[3 * x + 1, pl.ds(v * pad, deep), :] = second
            else:
                twice[3 * x + 2, pl.ds(0, deep), :] = first
                twice[3 * x + 2, pl.ds(pad, deep), :] = second
        return carry

    lax.fori_loop(0, nx, split, 0, unroll=8)
    low_both = low_half((2 * pad, 128))

    def block(k, carry):
        fetch(w_hbm, held, sems, k).wait()
        row = owner[k] * planes
        start = k * 3 * planes
        for x in range(planes):
            outs = []
            for b in range(3):
                t = 3 * x + b
                one, two = links[2 * start + t], links[2 * start + 3 * planes + t]
                both = jnp.where(low_both, twice[one], twice[two])
                weight = held[pl.ds((start + t) * BLK, BLK), :]
                outs.append(
                    lax.dot_general(
                        both, weight, (((1,), (1,)), ((), ())), preferred_element_type=F32
                    )
                )
            a, b, c = outs
            re = jnp.concatenate([a[:deep], b[:deep]], axis=1)
            im = jnp.concatenate([a[pad : pad + deep], b[pad : pad + deep]], axis=1)
            rest = jnp.concatenate([c[:deep], c[pad : pad + deep]], axis=1)
            o_ref[row + x, :, 0:128] = re
            o_ref[row + x, :, 128:256] = im
            o_ref[row + x, :, 256:384] = rest
        return carry

    lax.fori_loop(0, count, block, 0)


def warp(columns, weights, links, owner):
    nx, deep, _ = columns.shape
    blocks = 3 * nx
    pad = max(16, deep)
    whole = pl.BlockSpec((nx, deep, LANES), lambda i, l, p: (0, 0, 0))
    return pl.pallas_call(
        functools.partial(warp_kernel, nx, deep, pad),
        out_shape=jax.ShapeDtypeStruct((nx, deep, LANES), F32),
        grid_spec=pltpu.PrefetchScalarGridSpec(
            num_scalar_prefetch=2,
            grid=(1,),
            in_specs=[pl.BlockSpec(memory_space=pltpu.VMEM), pl.BlockSpec(memory_space=pl.ANY)],
            out_specs=whole,
            scratch_shapes=[
                pltpu.VMEM((blocks * BLK, 2 * BLK), BF),
                pltpu.VMEM((blocks, 2 * pad, 128), BF),
                pltpu.SemaphoreType.DMA((owner.shape[0],)),
            ],
        ),
        compiler_params=params(),
        cost_estimate=pl.CostEstimate(
            flops=2 * blocks * 256 * 256 * 32, bytes_accessed=20 << 20, transcendentals=0
        ),
        name="warp",
    )(links, owner, in_vmem(columns), weights)


def spread(nx, deep, pad, links, owner, c_ref, w_hbm, o_ref, held, total, sems):
    count = sems.shape[0]
    planes = nx // count

    def clear(i, carry):
        total[pl.ds(i * 3, 3)] = jnp.zeros((3, 2 * pad, 128), F32)
        return carry

    lax.fori_loop(0, nx, clear, 0, unroll=8)
    low = low_half((2 * pad, 128))

    def tall(a, b):
        if deep == pad:
            return jnp.concatenate([a, b], axis=0)
        fill = jnp.zeros((pad - deep, a.shape[1]), a.dtype)
        return jnp.concatenate([a, fill, b, fill], axis=0)

    def block(k, carry):
        fetch(w_hbm, held, sems, k).wait()
        row = owner[k] * planes
        start = k * 3 * planes
        for x in range(planes):
            re, im, rest = (c_ref[row + x, :, v * 128 : (v + 1) * 128] for v in range(3))
            tiles = (
                tall(re[:, :BLK], im[:, :BLK]),
                tall(re[:, BLK:], im[:, BLK:]),
                tall(rest[:, :BLK], rest[:, BLK:]),
            )
            for b in range(3):
                t = 3 * x + b
                one, two = links[2 * start + t], links[2 * start + 3 * planes + t]
                weight = held[pl.ds((start + t) * BLK, BLK), :]
                out = jnp.dot(tiles[b].astype(BF), weight, preferred_element_type=F32)
                zero = jnp.zeros_like(out)
                total[one] += jnp.where(low, out, zero)
                total[two] += jnp.where(low, zero, out)
        return carry

    lax.fori_loop(0, count, block, 0)
    low_row = low_half((deep, 128))

    def gather(x, carry):
        sums = []
        for b in range(3):
            value = total[3 * x + b]
            sums.append(value + pltpu.roll(value, BLK, 1))
        a, b, c = sums
        o_ref[x, :, 0:128] = jnp.where(low_row, a[:deep], b[:deep]).astype(BF)
        o_ref[x, :, 128:256] = jnp.where(
            low_row, a[pad : pad + deep], b[pad : pad + deep]
        ).astype(BF)
        o_ref[x, :, 256:384] = jnp.where(low_row, c[:deep], c[pad : pad + deep]).astype(BF)
        return carry

    lax.fori_loop(0, nx, gather, 0, unroll=8)


def coil_kernel(nx, deep, pad, fresh, ends, landed, *refs):
    if ends:
        links, owner, *refs = refs
    s_ref, w_ref, mask, iy, fx, bx, oy, *refs = refs
    if not fresh:
        before, *refs = refs
    if ends:
        w_hbm, grad_ref, rows, o_ref, held, total, sems = refs

        @pl.when(pl.program_id(0) == 0)
        def _():
            fetch_all(w_hbm, held, sems)
    else:
        o_ref, rows = refs
    s_ref = s_ref.at[:, pl.program_id(0) if landed else 0]
    group = 8 if nx % 8 == 0 else 1
    cube = rows.reshape(3, nx, pad, 128)
    low = low_half((group, deep, 128))

    def thirds(ref, at):
        return tuple(ref[at, :, v * 128 : (v + 1) * 128].astype(F32) for v in range(3))

    def expand(i, carry):
        at = pl.ds(i * group, group)
        s0, s1, s2 = thirds(s_ref, at)
        w0, w1, w2 = thirds(w_ref, at)
        turned = pltpu.roll(s2, BLK, 2)
        other = pltpu.roll(w2, BLK, 2)
        real = jnp.where(low, s2, turned)
        imag = jnp.where(low, turned, s2)
        cube[0, at, pl.ds(0, deep), :] = s0 * w0 - s1 * w1
        cube[1, at, pl.ds(0, deep), :] = s0 * w1 + s1 * w0
        cube[2, at, pl.ds(0, deep), :] = real * w2 + imag * jnp.where(low, -other, other)
        return carry

    lax.fori_loop(0, nx // group, expand, 0, unroll=4)

    batch = 4 if deep % 4 == 0 else 1

    def column(i, carry):
        ats = [pl.ds(i * batch + b, nx, stride=pad) for b in range(batch)]
        line = jnp.concatenate(
            [jnp.concatenate([rows[v, at, :] for v in range(3)], axis=1) for at in ats], axis=0
        ).astype(BF)
        y = jnp.dot(line, iy[...], preferred_element_type=F32).astype(BF)
        y = jnp.concatenate(
            [
                jnp.concatenate([y[b * nx : (b + 1) * nx, h * HALF : (h + 1) * HALF] for b in range(batch)], axis=1)
                for h in range(2)
            ],
            axis=0,
        )
        y = jnp.dot(fx[...], y, preferred_element_type=F32)
        y = jnp.concatenate([(y[:, b * HALF : (b + 1) * HALF] * mask[...]).astype(BF) for b in range(batch)], axis=1)
        y = jnp.dot(bx[...], y, preferred_element_type=F32).astype(BF)
        y = jnp.concatenate(
            [
                jnp.concatenate([y[h * nx : (h + 1) * nx, b * HALF : (b + 1) * HALF] for h in range(2)], axis=1)
                for b in range(batch)
            ],
            axis=0,
        )
        y = jnp.dot(y, oy[...], preferred_element_type=F32)
        for b, at in enumerate(ats):
            for v in range(3):
                rows[v, at, :] = y[b * nx : (b + 1) * nx, v * 128 : (v + 1) * 128]
        return carry

    lax.fori_loop(0, deep // batch, column, 0)

    first = pl.program_id(0) == 0

    def combine(i, carry):
        at = pl.ds(i * group, group)
        s0, s1, s2 = thirds(s_ref, at)
        r0, r1, r2 = (cube[v, at, pl.ds(0, deep), :] for v in range(3))
        turned = pltpu.roll(s2, BLK, 2)
        other = pltpu.roll(r2, BLK, 2)
        real = jnp.where(low, s2, turned)
        imag = jnp.where(low, turned, s2)
        terms = (
            s0 * r0 + s1 * r1,
            s0 * r1 - s1 * r0,
            real * r2 + imag * jnp.where(low, other, -other),
        )
        for v in range(3):
            lanes = slice(v * 128, (v + 1) * 128)
            old = o_ref[at, :, lanes]
            start = jnp.zeros_like(old) if fresh else before[at, :, lanes]
            o_ref[at, :, lanes] = jnp.where(first, start, old) + terms[v]
        return carry

    lax.fori_loop(0, nx // group, combine, 0, unroll=4)
    if ends:

        @pl.when(pl.program_id(0) == pl.num_programs(0) - 1)
        def _():
            spread(nx, deep, pad, links, owner, o_ref, w_hbm, grad_ref, held, total, sems)


def coils(maps, first, count, warped, mask, tabs, before, part, warping=None, landed=False):
    nx, _, deep, _ = maps.shape
    pad = max(8, deep)
    fresh, ends = before is None, warping is not None

    def whole(shape):
        return pl.BlockSpec(shape, lambda c, *_: (0,) * len(shape), pipeline_mode=pl.Buffered(1))

    def columns(array):
        at = part if array.shape[1] > deep else 0
        return pl.BlockSpec(
            (nx, deep, LANES), lambda c, *_: (0, at, 0), pipeline_mode=pl.Buffered(1)
        )

    if landed:
        maps = in_vmem(maps)
        in_specs = [pl.BlockSpec(memory_space=pltpu.VMEM)]
    else:
        in_specs = [pl.BlockSpec((nx, 1, deep, LANES), lambda c, *_: (0, first + c, 0, 0))]
    args = [maps, warped, mask, *tabs]
    in_specs += [columns(warped)] + [whole(a.shape) for a in (mask, *tabs)]
    if not fresh:
        args += [before]
        in_specs += [columns(before)]
    scratch = [pltpu.VMEM((3, nx * pad, 128), F32)]
    prefetched = []
    if ends:
        weights, *prefetched = warping
        args += [weights]
        in_specs += [pl.BlockSpec(memory_space=pl.ANY)]
        scratch += [
            pltpu.VMEM((nx, deep, LANES), F32),
            pltpu.VMEM((3 * nx * BLK, 2 * BLK), BF),
            pltpu.VMEM((3 * nx, 2 * pad, 128), F32),
            pltpu.SemaphoreType.DMA((prefetched[1].shape[0],)),
        ]
    return pl.pallas_call(
        functools.partial(coil_kernel, nx, deep, pad, fresh, ends, landed),
        out_shape=jax.ShapeDtypeStruct((nx, deep, LANES), BF if ends else F32),
        grid_spec=pltpu.PrefetchScalarGridSpec(
            num_scalar_prefetch=len(prefetched),
            grid=(count,),
            in_specs=in_specs,
            out_specs=pl.BlockSpec((nx, deep, LANES), lambda c, *_: (0, 0, 0)),
            scratch_shapes=scratch,
        ),
        compiler_params=params(),
        cost_estimate=pl.CostEstimate(
            flops=count * deep * 4 * 8 * nx * nx * 192 * 2,
            bytes_accessed=count * nx * deep * LANES * 2 + (14 << 20),
            transcendentals=0,
        ),
        name="coils",
    )(*prefetched, *args)


def update_kernel(count, b_ref, i_ref, a_ref, *refs):
    o_ref, scratch = refs[-2:]
    part = b_ref.shape[2]
    group = o_ref.shape[1]
    for x in range(group):
        plane = pl.program_id(0) * group + x
        for d in range(count):
            scratch[x, pl.ds(d * part, part), :] = b_ref[d, plane].astype(F32)
        grad = scratch[x].astype(BF).T.astype(F32)
        real = jnp.concatenate([grad[0:128], grad[256:320]], axis=0)
        imag = jnp.concatenate([grad[128:256], grad[320:384]], axis=0)
        for p, value in enumerate((real, imag)):
            o_ref[p, x] = i_ref[p, x] - 0.5 * (value - a_ref[p, x].astype(F32))


def update(back, image, adjoint, part, before):
    count, planes, deep, _ = back.shape
    _, _, ny, _ = image.shape
    lanes = count * deep
    group = 3 if planes % 3 == 0 else 1
    block = pl.BlockSpec((2, group, ny, lanes), lambda x: (0, x, 0, part))
    more = [] if before is None else [before]
    return pl.pallas_call(
        functools.partial(update_kernel, count),
        out_shape=jax.ShapeDtypeStruct(image.shape, F32),
        grid=(planes // group,),
        in_specs=[
            pl.BlockSpec(memory_space=pltpu.VMEM),
            block,
            block,
        ]
        + [pl.BlockSpec(memory_space=pl.ANY)] * len(more),
        out_specs=block,
        scratch_shapes=[pltpu.VMEM((group, lanes, LANES), F32)],
        input_output_aliases={3: 0} if more else {},
        compiler_params=params(),
        cost_estimate=pl.CostEstimate(
            flops=0, bytes_accessed=2 * planes * ny * lanes * 12, transcendentals=0
        ),
        name="update",
    )(in_vmem(back), image, adjoint, *more)


def exchange(parts):
    return lax.all_to_all(parts, "slab", split_axis=0, concat_axis=0, tiled=True)


def after(value, *others):
    return lax.optimization_barrier((value, *others))[0]


def swap_halves(value):
    count = lax.axis_size("slab")
    half = count // 2
    return lax.ppermute(value, "slab", [(i, i ^ half) for i in range(count)])


def gather_half(pair):
    count = lax.axis_size("slab")
    half = count // 2
    groups = [list(range(half)), list(range(half, count))]
    gathered = lax.all_gather(pair, "slab", axis=0, tiled=True, axis_index_groups=groups)
    mine = lax.axis_index("slab") // half
    place = jnp.arange(count, dtype=jnp.int32)
    return gathered, place // 2 + half * ((place % 2) ^ mine)


def per_device(image, adjoint_data, coil_maps, masks, sources, weights):
    count = lax.axis_size("slab")
    planes, ny, nz = image.shape[1:]
    nx = planes * count
    deep = nz // count
    total = coil_maps.shape[0]
    tabs = tables(nx, ny)
    sampled = jnp.pad(masks[0].astype(F32), ((0, 0), (0, HALF - ny)))
    mask = jnp.concatenate([sampled, sampled], axis=0)

    targets = 3 * planes
    matrices = weights[0].reshape(targets, 2, BLK, BLK)
    matrices = jnp.transpose(matrices, (0, 2, 1, 3)).reshape(targets * BLK, 2 * BLK)
    chosen = sources[0].T
    digits = jnp.concatenate([chosen // BLK, chosen % BLK], axis=0).astype(BF)
    digits = jnp.pad(digits, ((0, TAIL - 4), (0, 2 * BLK - targets)))
    own = jnp.concatenate([matrices, digits], axis=0)
    crossed = swap_halves(own)
    packed, owner = gather_half(jnp.concatenate([own, crossed], axis=0))
    digits = packed.reshape(count, targets * BLK + TAIL, 2 * BLK)[:, targets * BLK :]
    digits = digits[:, :4, :targets].astype(jnp.int32)
    links = (digits[:, :2] * BLK + digits[:, 2:]).reshape(-1)

    def run(received, first, size, before, part, **more):
        maps = received.reshape(nx, received.shape[2], -1, LANES)
        return coils(maps, first, size, warped, mask, tabs, before, part, **more)

    def back(grad, *needs):
        return exchange(after(grad, *needs).reshape(count, planes, -1, LANES))

    columns = exchange(image_columns(image, count))
    warped = warp(columns.reshape(nx, deep, LANES), packed, links, owner)
    warping = (packed, links, owner)
    halves = parts_of(deep) == 2
    early = total - 3 * total // 8 if halves else total - 1
    late = total - early
    maps = maps_columns(coil_maps, count, 0, early)
    arrived = exchange(after(maps, columns, crossed))
    if not halves:
        maps = maps_columns(coil_maps, count, early, late)
        last = exchange(after(maps, arrived, warped))
        combined = run(arrived, 0, early, None, 0)
        grad = run(last, 0, late, combined, 0, warping=warping)
        return update(back(grad), image, adjoint_data, 0, None)

    first, second = last_maps_columns(coil_maps, count, early, late)
    first = exchange(after(first, arrived, warped))
    combined = run(arrived, 0, early, None, 0)
    second = exchange(after(second, first, combined))
    grad = run(first, 0, late, combined, 0, warping=warping)
    half = run(first, late, 1, combined, 1)
    back_first = back(grad, second, half)
    grad = run(second, 0, late - 1, half, 1, warping=warping, landed=True)
    back_second = back(grad, back_first)
    result = update(back_first, image, adjoint_data, 0, None)
    return update(back_second, image, adjoint_data, 1, result)


def solution(mesh):
    return jax.shard_map(
        per_device,
        mesh=mesh,
        in_specs=(
            P(None, ("grp", "slab"), None, None),
            P(None, ("grp", "slab"), None, None),
            P(None, None, ("grp", "slab"), None, None),
            P(None, "grp", None),
            P(None, ("grp", "slab"), None),
            P(None, ("grp", "slab"), None),
        ),
        out_specs=P(None, ("grp", "slab"), None, None),
        check_vma=False,
    )
```

```python
import functools
import math

import jax
import jax.numpy as jnp
import numpy as np
from jax import lax
from jax.experimental import pallas as pl
from jax.experimental.pallas import tpu as pltpu
from jax.sharding import PartitionSpec as P

BLK = 64
LANES = 384
TAIL = 16
HALF = 256
VMEM_LIMIT = 56 * 1024 * 1024
BF = jnp.bfloat16
F32 = jnp.float32


def lane_order(length):
    lo, rest = 128, length - 128
    part = np.concatenate([np.zeros(lo), np.ones(lo), np.zeros(rest), np.ones(rest)])
    pos = np.concatenate([np.arange(lo), np.arange(lo), lo + np.arange(rest), lo + np.arange(rest)])
    return part.astype(np.int32), pos.astype(np.int32)


def dft_table(length, direction):
    positions = np.arange(length)
    phases = (positions[:, None] * positions[None, :] % length).astype(np.float32)
    phases = phases * np.float32(2.0 * math.pi / length)
    factor = np.float32(1.0 / math.sqrt(length))
    cosine = np.cos(phases) * factor
    sine = np.sin(phases) * (np.float32(direction) * factor)
    upper = np.stack([cosine, -sine], axis=1)
    lower = np.stack([sine, cosine], axis=1)
    return np.stack([upper, lower], axis=0)


def tables(nx, ny):
    part, pos = lane_order(ny)
    fwd_y, inv_y = dft_table(ny, -1.0), dft_table(ny, 1.0)
    into_y = np.zeros((2 * ny, 2, HALF), np.float32)
    into_y[:, :, :ny] = np.transpose(fwd_y[:, :, part, pos], (2, 0, 1))
    from_y = np.zeros((2, HALF, 2 * ny), np.float32)
    from_y[:, :ny, :] = np.transpose(inv_y[part, pos], (1, 2, 0))
    fwd_x = dft_table(nx, -1.0).reshape(2 * nx, 2 * nx)
    inv_x = dft_table(nx, 1.0).reshape(2 * nx, 2 * nx)
    out = (into_y.reshape(2 * ny, 2 * HALF), fwd_x, inv_x, from_y.reshape(2 * HALF, 2 * ny))
    return tuple(jnp.asarray(t, BF) for t in out)


def params():
    return pltpu.CompilerParams(vmem_limit_bytes=VMEM_LIMIT)


def in_vmem(array):
    return pltpu.with_memory_space_constraint(array, pltpu.VMEM)


def to_rows(parts):
    stacked = jnp.concatenate(
        [parts[0, :128], parts[1, :128], parts[0, 128:], parts[1, 128:]], axis=0
    )
    return stacked.T


def part_rows(scratch, count, deep, parts, d, h):
    part = deep // parts
    return scratch[pl.ds((h * count + d) * part, part), :]


def spread_rows(out, scratch, count, deep, parts):
    for d in range(count):
        rows = [part_rows(scratch, count, deep, parts, d, h) for h in range(parts)]
        out[d] = jnp.concatenate(rows, axis=0).astype(BF)


def parts_of(deep):
    return 2 if deep % 16 == 0 else 1


def image_kernel(count, deep, x_ref, o_ref, scratch):
    for x in range(x_ref.shape[1]):
        scratch[x] = to_rows(x_ref[:, x].astype(BF)).astype(F32)
        spread_rows(o_ref.at[:, x], scratch.at[x], count, deep, parts_of(deep))


def image_columns(image, count):
    _, planes, ny, nz = image.shape
    deep = nz // count
    group = math.gcd(planes, 6)
    return pl.pallas_call(
        functools.partial(image_kernel, count, deep),
        out_shape=jax.ShapeDtypeStruct((count, planes, deep, LANES), BF),
        grid=(planes // group,),
        in_specs=[pl.BlockSpec((2, group, ny, nz), lambda x: (0, x, 0, 0))],
        out_specs=pl.BlockSpec((count, group, deep, LANES), lambda x: (0, x, 0, 0)),
        scratch_shapes=[pltpu.VMEM((group, nz, LANES), F32)],
        compiler_params=params(),
        cost_estimate=pl.CostEstimate(flops=0, bytes_accessed=image.size * 6, transcendentals=0),
        name="image_columns",
    )(image)


def maps_kernel(count, deep, x_ref, o_ref, scratch):
    scratch[...] = to_rows(x_ref[0, :, 0]).astype(F32)
    spread_rows(o_ref.at[:, 0, 0], scratch, count, deep, parts_of(deep))


def last_maps_kernel(count, deep, coils, x_ref, first_ref, second_ref, scratch):
    scratch[...] = to_rows(x_ref[0, :, 0]).astype(F32)
    for c in range(coils):

        @pl.when(pl.program_id(1) == c)
        def _():
            for d in range(count):
                half = part_rows(scratch, count, deep, 2, d, 1).astype(BF)
                first_ref[d, 0, c] = part_rows(scratch, count, deep, 2, d, 0).astype(BF)
                if c == 0:
                    first_ref[d, 0, coils] = half
                else:
                    second_ref[d, 0, c - 1] = half


def maps_columns(coil_maps, count, first, coils):
    _, _, planes, ny, nz = coil_maps.shape
    deep = nz // count
    return pl.pallas_call(
        functools.partial(maps_kernel, count, deep),
        out_shape=jax.ShapeDtypeStruct((count, planes, coils, deep, LANES), BF),
        grid=(planes, coils),
        in_specs=[pl.BlockSpec((1, 2, 1, ny, nz), lambda x, c: (first + c, 0, x, 0, 0))],
        out_specs=pl.BlockSpec((count, 1, 1, deep, LANES), lambda x, c: (0, x, c, 0, 0)),
        scratch_shapes=[pltpu.VMEM((nz, LANES), F32)],
        compiler_params=params(),
        cost_estimate=pl.CostEstimate(
            flops=0, bytes_accessed=coils * 2 * planes * ny * nz * 4, transcendentals=0
        ),
        name="maps_columns",
    )(coil_maps)


def last_maps_columns(coil_maps, count, first, coils):
    _, _, planes, ny, nz = coil_maps.shape
    deep = nz // count
    sizes = (coils + 1, coils - 1)
    return pl.pallas_call(
        functools.partial(last_maps_kernel, count, deep, coils),
        out_shape=[jax.ShapeDtypeStruct((count, planes, n, deep // 2, LANES), BF) for n in sizes],
        grid=(planes, coils),
        in_specs=[pl.BlockSpec((1, 2, 1, ny, nz), lambda x, c: (first + c, 0, x, 0, 0))],
        out_specs=[
            pl.BlockSpec((count, 1, n, deep // 2, LANES), lambda x, c: (0, x, 0, 0, 0))
            for n in sizes
        ],
        scratch_shapes=[pltpu.VMEM((nz, LANES), F32)],
        compiler_params=params(),
        cost_estimate=pl.CostEstimate(
            flops=0, bytes_accessed=coils * 2 * planes * ny * nz * 4, transcendentals=0
        ),
        name="last_maps_columns",
    )(coil_maps)


def low_half(shape):
    return lax.broadcasted_iota(jnp.int32, shape, len(shape) - 1) < BLK


def fetch(w_hbm, held, sems, k):
    size = held.shape[0] // sems.shape[0]
    source = w_hbm.at[pl.ds(k * (size + TAIL), size)]
    return pltpu.make_async_copy(source, held.at[pl.ds(k * size, size)], sems.at[k])


def fetch_all(w_hbm, held, sems):
    for k in range(sems.shape[0]):
        fetch(w_hbm, held, sems, k).start()


def warp_kernel(nx, deep, pad, links, owner, g_ref, w_hbm, o_ref, held, twice, sems):
    fetch_all(w_hbm, held, sems)
    count = sems.shape[0]
    planes = nx // count
    low = low_half((deep, 128))

    def split(x, carry):
        for v in range(3):
            row = g_ref[x, :, v * 128 : (v + 1) * 128].astype(F32)
            turned = pltpu.roll(row, BLK, 1)
            first = jnp.where(low, row, turned).astype(BF)
            second = jnp.where(low, turned, row).astype(BF)
            if v < 2:
                twice[3 * x, pl.ds(v * pad, deep), :] = first
                twice[3 * x + 1, pl.ds(v * pad, deep), :] = second
            else:
                twice[3 * x + 2, pl.ds(0, deep), :] = first
                twice[3 * x + 2, pl.ds(pad, deep), :] = second
        return carry

    lax.fori_loop(0, nx, split, 0, unroll=8)
    low_both = low_half((2 * pad, 128))

    def block(k, carry):
        fetch(w_hbm, held, sems, k).wait()
        row = owner[k] * planes
        start = k * 3 * planes
        for x in range(planes):
            outs = []
            for b in range(3):
                t = 3 * x + b
                one, two = links[2 * start + t], links[2 * start + 3 * planes + t]
                both = jnp.where(low_both, twice[one], twice[two])
                weight = held[pl.ds((start + t) * BLK, BLK), :]
                outs.append(
                    lax.dot_general(
                        both, weight, (((1,), (1,)), ((), ())), preferred_element_type=F32
                    )
                )
            a, b, c = outs
            re = jnp.concatenate([a[:deep], b[:deep]], axis=1)
            im = jnp.concatenate([a[pad : pad + deep], b[pad : pad + deep]], axis=1)
            rest = jnp.concatenate([c[:deep], c[pad : pad + deep]], axis=1)
            o_ref[row + x, :, 0:128] = re
            o_ref[row + x, :, 128:256] = im
            o_ref[row + x, :, 256:384] = rest
        return carry

    lax.fori_loop(0, count, block, 0)


def warp(columns, weights, links, owner):
    nx, deep, _ = columns.shape
    blocks = 3 * nx
    pad = max(16, deep)
    whole = pl.BlockSpec((nx, deep, LANES), lambda i, l, p: (0, 0, 0))
    return pl.pallas_call(
        functools.partial(warp_kernel, nx, deep, pad),
        out_shape=jax.ShapeDtypeStruct((nx, deep, LANES), F32),
        grid_spec=pltpu.PrefetchScalarGridSpec(
            num_scalar_prefetch=2,
            grid=(1,),
            in_specs=[pl.BlockSpec(memory_space=pltpu.VMEM), pl.BlockSpec(memory_space=pl.ANY)],
            out_specs=whole,
            scratch_shapes=[
                pltpu.VMEM((blocks * BLK, 2 * BLK), BF),
                pltpu.VMEM((blocks, 2 * pad, 128), BF),
                pltpu.SemaphoreType.DMA((owner.shape[0],)),
            ],
        ),
        compiler_params=params(),
        cost_estimate=pl.CostEstimate(
            flops=2 * blocks * 256 * 256 * 32, bytes_accessed=20 << 20, transcendentals=0
        ),
        name="warp",
    )(links, owner, in_vmem(columns), weights)


def spread(nx, deep, pad, links, owner, c_ref, w_hbm, o_ref, held, total, sems):
    count = sems.shape[0]
    planes = nx // count

    def clear(i, carry):
        total[pl.ds(i * 3, 3)] = jnp.zeros((3, 2 * pad, 128), F32)
        return carry

    lax.fori_loop(0, nx, clear, 0, unroll=8)
    low = low_half((2 * pad, 128))

    def tall(a, b):
        if deep == pad:
            return jnp.concatenate([a, b], axis=0)
        fill = jnp.zeros((pad - deep, a.shape[1]), a.dtype)
        return jnp.concatenate([a, fill, b, fill], axis=0)

    def block(k, carry):
        fetch(w_hbm, held, sems, k).wait()
        row = owner[k] * planes
        start = k * 3 * planes
        for x in range(planes):
            re, im, rest = (c_ref[row + x, :, v * 128 : (v + 1) * 128] for v in range(3))
            tiles = (
                tall(re[:, :BLK], im[:, :BLK]),
                tall(re[:, BLK:], im[:, BLK:]),
                tall(rest[:, :BLK], rest[:, BLK:]),
            )
            for b in range(3):
                t = 3 * x + b
                one, two = links[2 * start + t], links[2 * start + 3 * planes + t]
                weight = held[pl.ds((start + t) * BLK, BLK), :]
                out = jnp.dot(tiles[b].astype(BF), weight, preferred_element_type=F32)
                zero = jnp.zeros_like(out)
                total[one] += jnp.where(low, out, zero)
                total[two] += jnp.where(low, zero, out)
        return carry

    lax.fori_loop(0, count, block, 0)
    low_row = low_half((deep, 128))

    def gather(x, carry):
        sums = []
        for b in range(3):
            value = total[3 * x + b]
            sums.append(value + pltpu.roll(value, BLK, 1))
        a, b, c = sums
        o_ref[x, :, 0:128] = jnp.where(low_row, a[:deep], b[:deep]).astype(BF)
        o_ref[x, :, 128:256] = jnp.where(
            low_row, a[pad : pad + deep], b[pad : pad + deep]
        ).astype(BF)
        o_ref[x, :, 256:384] = jnp.where(low_row, c[:deep], c[pad : pad + deep]).astype(BF)
        return carry

    lax.fori_loop(0, nx, gather, 0, unroll=8)


def coil_kernel(nx, deep, pad, skip, ends, landed, *refs):
    fresh = skip is None
    if ends:
        links, owner, *refs = refs
    s_ref, w_ref, mask, iy, fx, bx, oy, *refs = refs
    if not fresh:
        before, *refs, sem = refs
    if ends:
        w_hbm, grad_ref, rows, o_ref, held, total, sems = refs

        @pl.when(pl.program_id(0) == 0)
        def _():
            fetch_all(w_hbm, held, sems)
    else:
        o_ref, rows = refs
    first = pl.program_id(0) == 0
    if not fresh:
        earlier = pltpu.make_async_copy(before.at[:, pl.ds(skip, deep), :], o_ref, sem)
        pl.when(first)(earlier.start)
    s_ref = s_ref.at[:, pl.program_id(0) if landed else 0]
    group = 8 if nx % 8 == 0 else 1
    cube = rows.reshape(3, nx, pad, 128)
    low = low_half((group, deep, 128))

    def thirds(ref, at):
        return tuple(ref[at, :, v * 128 : (v + 1) * 128].astype(F32) for v in range(3))

    def expand(i, carry):
        at = pl.ds(i * group, group)
        s0, s1, s2 = thirds(s_ref, at)
        w0, w1, w2 = thirds(w_ref, at)
        turned = pltpu.roll(s2, BLK, 2)
        other = pltpu.roll(w2, BLK, 2)
        real = jnp.where(low, s2, turned)
        imag = jnp.where(low, turned, s2)
        cube[0, at, pl.ds(0, deep), :] = s0 * w0 - s1 * w1
        cube[1, at, pl.ds(0, deep), :] = s0 * w1 + s1 * w0
        cube[2, at, pl.ds(0, deep), :] = real * w2 + imag * jnp.where(low, -other, other)
        return carry

    lax.fori_loop(0, nx // group, expand, 0, unroll=4)

    batch = 4 if deep % 4 == 0 else 1

    def column(i, carry):
        ats = [pl.ds(i * batch + b, nx, stride=pad) for b in range(batch)]
        line = jnp.concatenate(
            [jnp.concatenate([rows[v, at, :] for v in range(3)], axis=1) for at in ats], axis=0
        ).astype(BF)
        y = jnp.dot(line, iy[...], preferred_element_type=F32).astype(BF)
        y = jnp.concatenate(
            [
                jnp.concatenate([y[b * nx : (b + 1) * nx, h * HALF : (h + 1) * HALF] for b in range(batch)], axis=1)
                for h in range(2)
            ],
            axis=0,
        )
        y = jnp.dot(fx[...], y, preferred_element_type=F32)
        y = jnp.concatenate([(y[:, b * HALF : (b + 1) * HALF] * mask[...]).astype(BF) for b in range(batch)], axis=1)
        y = jnp.dot(bx[...], y, preferred_element_type=F32).astype(BF)
        y = jnp.concatenate(
            [
                jnp.concatenate([y[h * nx : (h + 1) * nx, b * HALF : (b + 1) * HALF] for h in range(2)], axis=1)
                for b in range(batch)
            ],
            axis=0,
        )
        y = jnp.dot(y, oy[...], preferred_element_type=F32)
        for b, at in enumerate(ats):
            for v in range(3):
                rows[v, at, :] = y[b * nx : (b + 1) * nx, v * 128 : (v + 1) * 128]
        return carry

    lax.fori_loop(0, deep // batch, column, 0)

    if not fresh:
        pl.when(first)(earlier.wait)

    def combine(i, carry):
        at = pl.ds(i * group, group)
        s0, s1, s2 = thirds(s_ref, at)
        r0, r1, r2 = (cube[v, at, pl.ds(0, deep), :] for v in range(3))
        turned = pltpu.roll(s2, BLK, 2)
        other = pltpu.roll(r2, BLK, 2)
        real = jnp.where(low, s2, turned)
        imag = jnp.where(low, turned, s2)
        terms = (
            s0 * r0 + s1 * r1,
            s0 * r1 - s1 * r0,
            real * r2 + imag * jnp.where(low, other, -other),
        )
        for v in range(3):
            lanes = slice(v * 128, (v + 1) * 128)
            old = o_ref[at, :, lanes]
            if fresh:
                old = jnp.where(first, jnp.zeros_like(old), old)
            o_ref[at, :, lanes] = old + terms[v]
        return carry

    lax.fori_loop(0, nx // group, combine, 0, unroll=4)
    if ends:

        @pl.when(pl.program_id(0) == pl.num_programs(0) - 1)
        def _():
            spread(nx, deep, pad, links, owner, o_ref, w_hbm, grad_ref, held, total, sems)


def coils(maps, first, count, warped, mask, tabs, before, part, warping=None, landed=False):
    nx, _, deep, _ = maps.shape
    pad = max(8, deep)
    fresh, ends = before is None, warping is not None

    def whole(shape):
        return pl.BlockSpec(shape, lambda c, *_: (0,) * len(shape), pipeline_mode=pl.Buffered(1))

    def columns(array):
        at = part if array.shape[1] > deep else 0
        return pl.BlockSpec(
            (nx, deep, LANES), lambda c, *_: (0, at, 0), pipeline_mode=pl.Buffered(1)
        )

    if landed:
        maps = in_vmem(maps)
        in_specs = [pl.BlockSpec(memory_space=pltpu.VMEM)]
    else:
        in_specs = [pl.BlockSpec((nx, 1, deep, LANES), lambda c, *_: (0, first + c, 0, 0))]
    args = [maps, warped, mask, *tabs]
    in_specs += [columns(warped)] + [whole(a.shape) for a in (mask, *tabs)]
    skip = None
    if not fresh:
        args += [before]
        in_specs += [pl.BlockSpec(memory_space=pl.ANY)]
        skip = part * deep if before.shape[1] > deep else 0
    scratch = [pltpu.VMEM((3, nx * pad, 128), F32)]
    prefetched = []
    if ends:
        weights, *prefetched = warping
        args += [weights]
        in_specs += [pl.BlockSpec(memory_space=pl.ANY)]
        scratch += [
            pltpu.VMEM((nx, deep, LANES), F32),
            pltpu.VMEM((3 * nx * BLK, 2 * BLK), BF),
            pltpu.VMEM((3 * nx, 2 * pad, 128), F32),
            pltpu.SemaphoreType.DMA((prefetched[1].shape[0],)),
        ]
    if not fresh:
        scratch += [pltpu.SemaphoreType.DMA]
    return pl.pallas_call(
        functools.partial(coil_kernel, nx, deep, pad, skip, ends, landed),
        out_shape=jax.ShapeDtypeStruct((nx, deep, LANES), BF if ends else F32),
        grid_spec=pltpu.PrefetchScalarGridSpec(
            num_scalar_prefetch=len(prefetched),
            grid=(count,),
            in_specs=in_specs,
            out_specs=pl.BlockSpec((nx, deep, LANES), lambda c, *_: (0, 0, 0)),
            scratch_shapes=scratch,
        ),
        compiler_params=params(),
        cost_estimate=pl.CostEstimate(
            flops=count * deep * 4 * 8 * nx * nx * 192 * 2,
            bytes_accessed=count * nx * deep * LANES * 2 + (14 << 20),
            transcendentals=0,
        ),
        name="coils",
    )(*prefetched, *args)


def update_kernel(count, b_ref, i_ref, a_ref, *refs):
    o_ref, scratch = refs[-2:]
    part = b_ref.shape[2]
    group = o_ref.shape[1]
    for x in range(group):
        plane = pl.program_id(0) * group + x
        for d in range(count):
            scratch[x, pl.ds(d * part, part), :] = b_ref[d, plane].astype(F32)
        grad = scratch[x].astype(BF).T.astype(F32)
        real = jnp.concatenate([grad[0:128], grad[256:320]], axis=0)
        imag = jnp.concatenate([grad[128:256], grad[320:384]], axis=0)
        for p, value in enumerate((real, imag)):
            o_ref[p, x] = i_ref[p, x] - 0.5 * (value - a_ref[p, x].astype(F32))


def update(back, image, adjoint, part, before):
    count, planes, deep, _ = back.shape
    _, _, ny, _ = image.shape
    lanes = count * deep
    group = math.gcd(planes, 6)
    block = pl.BlockSpec((2, group, ny, lanes), lambda x: (0, x, 0, part))
    more = [] if before is None else [before]
    return pl.pallas_call(
        functools.partial(update_kernel, count),
        out_shape=jax.ShapeDtypeStruct(image.shape, F32),
        grid=(planes // group,),
        in_specs=[
            pl.BlockSpec(memory_space=pltpu.VMEM),
            block,
            block,
        ]
        + [pl.BlockSpec(memory_space=pl.ANY)] * len(more),
        out_specs=block,
        scratch_shapes=[pltpu.VMEM((group, lanes, LANES), F32)],
        input_output_aliases={3: 0} if more else {},
        compiler_params=params(),
        cost_estimate=pl.CostEstimate(
            flops=0, bytes_accessed=2 * planes * ny * lanes * 12, transcendentals=0
        ),
        name="update",
    )(in_vmem(back), image, adjoint, *more)


def exchange(parts):
    return lax.all_to_all(parts, "slab", split_axis=0, concat_axis=0, tiled=True)


def after(value, *others):
    return lax.optimization_barrier((value, *others))[0]


def swap_halves(value):
    count = lax.axis_size("slab")
    half = count // 2
    return lax.ppermute(value, "slab", [(i, i ^ half) for i in range(count)])


def gather_half(pair):
    count = lax.axis_size("slab")
    half = count // 2
    groups = [list(range(half)), list(range(half, count))]
    gathered = lax.all_gather(pair, "slab", axis=0, tiled=True, axis_index_groups=groups)
    mine = lax.axis_index("slab") // half
    place = jnp.arange(count, dtype=jnp.int32)
    return gathered, place // 2 + half * ((place % 2) ^ mine)


def per_device(image, adjoint_data, coil_maps, masks, sources, weights):
    count = lax.axis_size("slab")
    planes, ny, nz = image.shape[1:]
    nx = planes * count
    deep = nz // count
    total = coil_maps.shape[0]
    tabs = tables(nx, ny)
    sampled = jnp.pad(masks[0].astype(F32), ((0, 0), (0, HALF - ny)))
    mask = jnp.concatenate([sampled, sampled], axis=0)

    targets = 3 * planes
    matrices = weights[0].reshape(targets, 2, BLK, BLK)
    matrices = jnp.transpose(matrices, (0, 2, 1, 3)).reshape(targets * BLK, 2 * BLK)
    chosen = sources[0].T
    digits = jnp.concatenate([chosen // BLK, chosen % BLK], axis=0).astype(BF)
    digits = jnp.pad(digits, ((0, TAIL - 4), (0, 2 * BLK - targets)))
    own = jnp.concatenate([matrices, digits], axis=0)
    crossed = swap_halves(own)
    packed, owner = gather_half(jnp.concatenate([own, crossed], axis=0))
    digits = packed.reshape(count, targets * BLK + TAIL, 2 * BLK)[:, targets * BLK :]
    digits = digits[:, :4, :targets].astype(jnp.int32)
    links = (digits[:, :2] * BLK + digits[:, 2:]).reshape(-1)

    def run(received, first, size, before, part, **more):
        maps = received.reshape(nx, received.shape[2], -1, LANES)
        return coils(maps, first, size, warped, mask, tabs, before, part, **more)

    def back(grad, *needs):
        return exchange(after(grad, *needs).reshape(count, planes, -1, LANES))

    columns = exchange(image_columns(image, count))
    warped = warp(columns.reshape(nx, deep, LANES), packed, links, owner)
    warping = (packed, links, owner)
    halves = parts_of(deep) == 2
    early = total - 3 * total // 8 if halves else total - 1
    late = total - early
    maps = maps_columns(coil_maps, count, 0, early)
    arrived = exchange(after(maps, columns, crossed))
    if not halves:
        maps = maps_columns(coil_maps, count, early, late)
        last = exchange(after(maps, arrived, warped))
        combined = run(arrived, 0, early, None, 0)
        grad = run(last, 0, late, combined, 0, warping=warping)
        return update(back(grad), image, adjoint_data, 0, None)

    first, second = last_maps_columns(coil_maps, count, early, late)
    first = exchange(after(first, arrived, warped))
    combined = run(arrived, 0, early, None, 0)
    second = exchange(after(second, first, combined))
    grad = run(first, 0, late, combined, 0, warping=warping)
    half = run(first, late, 1, combined, 1)
    back_first = back(grad, second, half)
    grad = run(second, 0, late - 1, half, 1, warping=warping, landed=True)
    back_second = back(grad, back_first)
    result = update(back_first, image, adjoint_data, 0, None)
    return update(back_second, image, adjoint_data, 1, result)


def solution(mesh):
    return jax.shard_map(
        per_device,
        mesh=mesh,
        in_specs=(
            P(None, ("grp", "slab"), None, None),
            P(None, ("grp", "slab"), None, None),
            P(None, None, ("grp", "slab"), None, None),
            P(None, "grp", None),
            P(None, ("grp", "slab"), None),
            P(None, ("grp", "slab"), None),
        ),
        out_specs=P(None, ("grp", "slab"), None, None),
        check_vma=False,
    )
```

```python
import functools
import math

import jax
import jax.numpy as jnp
import numpy as np
from jax import lax
from jax.experimental import pallas as pl
from jax.experimental.pallas import tpu as pltpu
from jax.sharding import PartitionSpec as P

BLK = 64
LANES = 384
TAIL = 16
HALF = 256
VMEM_LIMIT = 56 * 1024 * 1024
BF = jnp.bfloat16
F32 = jnp.float32


def lane_order(length):
    lo, rest = 128, length - 128
    part = np.concatenate([np.zeros(lo), np.ones(lo), np.zeros(rest), np.ones(rest)])
    pos = np.concatenate([np.arange(lo), np.arange(lo), lo + np.arange(rest), lo + np.arange(rest)])
    return part.astype(np.int32), pos.astype(np.int32)


def dft_table(length, direction):
    positions = np.arange(length)
    phases = (positions[:, None] * positions[None, :] % length).astype(np.float32)
    phases = phases * np.float32(2.0 * math.pi / length)
    factor = np.float32(1.0 / math.sqrt(length))
    cosine = np.cos(phases) * factor
    sine = np.sin(phases) * (np.float32(direction) * factor)
    upper = np.stack([cosine, -sine], axis=1)
    lower = np.stack([sine, cosine], axis=1)
    return np.stack([upper, lower], axis=0)


def tables(nx, ny):
    part, pos = lane_order(ny)
    fwd_y, inv_y = dft_table(ny, -1.0), dft_table(ny, 1.0)
    into_y = np.zeros((2 * ny, 2, HALF), np.float32)
    into_y[:, :, :ny] = np.transpose(fwd_y[:, :, part, pos], (2, 0, 1))
    from_y = np.zeros((2, HALF, 2 * ny), np.float32)
    from_y[:, :ny, :] = np.transpose(inv_y[part, pos], (1, 2, 0))
    fwd_x = dft_table(nx, -1.0).reshape(2 * nx, 2 * nx)
    inv_x = dft_table(nx, 1.0).reshape(2 * nx, 2 * nx)
    out = (into_y.reshape(2 * ny, 2 * HALF), fwd_x, inv_x, from_y.reshape(2 * HALF, 2 * ny))
    return tuple(jnp.asarray(t, BF) for t in out)


def params():
    return pltpu.CompilerParams(vmem_limit_bytes=VMEM_LIMIT)


def in_vmem(array):
    return pltpu.with_memory_space_constraint(array, pltpu.VMEM)


def to_rows(parts):
    stacked = jnp.concatenate(
        [parts[0, :128], parts[1, :128], parts[0, 128:], parts[1, 128:]], axis=0
    )
    return stacked.T


def part_rows(scratch, count, deep, parts, d, h):
    part = deep // parts
    return scratch[pl.ds((h * count + d) * part, part), :]


def spread_rows(out, scratch, count, deep, parts):
    for d in range(count):
        rows = [part_rows(scratch, count, deep, parts, d, h) for h in range(parts)]
        out[d] = jnp.concatenate(rows, axis=0).astype(BF)


def parts_of(deep):
    return 2 if deep % 16 == 0 else 1


def image_kernel(count, deep, x_ref, o_ref, scratch):
    for x in range(x_ref.shape[1]):
        scratch[x] = to_rows(x_ref[:, x].astype(BF)).astype(F32)
        spread_rows(o_ref.at[:, x], scratch.at[x], count, deep, parts_of(deep))


def image_columns(image, count):
    _, planes, ny, nz = image.shape
    deep = nz // count
    group = math.gcd(planes, 6)
    return pl.pallas_call(
        functools.partial(image_kernel, count, deep),
        out_shape=jax.ShapeDtypeStruct((count, planes, deep, LANES), BF),
        grid=(planes // group,),
        in_specs=[pl.BlockSpec((2, group, ny, nz), lambda x: (0, x, 0, 0))],
        out_specs=pl.BlockSpec((count, group, deep, LANES), lambda x: (0, x, 0, 0)),
        scratch_shapes=[pltpu.VMEM((group, nz, LANES), F32)],
        compiler_params=params(),
        cost_estimate=pl.CostEstimate(flops=0, bytes_accessed=image.size * 6, transcendentals=0),
        name="image_columns",
    )(image)


def maps_kernel(count, deep, x_ref, o_ref, scratch):
    scratch[...] = to_rows(x_ref[0, :, 0]).astype(F32)
    spread_rows(o_ref.at[:, 0, 0], scratch, count, deep, parts_of(deep))


def last_maps_kernel(count, deep, coils, x_ref, first_ref, second_ref, scratch):
    scratch[...] = to_rows(x_ref[0, :, 0]).astype(F32)
    for c in range(coils):

        @pl.when(pl.program_id(1) == c)
        def _():
            for d in range(count):
                half = part_rows(scratch, count, deep, 2, d, 1).astype(BF)
                first_ref[d, 0, c] = part_rows(scratch, count, deep, 2, d, 0).astype(BF)
                if c == 0:
                    first_ref[d, 0, coils] = half
                else:
                    second_ref[d, 0, c - 1] = half


def maps_columns(coil_maps, count, first, coils):
    _, _, planes, ny, nz = coil_maps.shape
    deep = nz // count
    return pl.pallas_call(
        functools.partial(maps_kernel, count, deep),
        out_shape=jax.ShapeDtypeStruct((count, planes, coils, deep, LANES), BF),
        grid=(planes, coils),
        in_specs=[pl.BlockSpec((1, 2, 1, ny, nz), lambda x, c: (first + c, 0, x, 0, 0))],
        out_specs=pl.BlockSpec((count, 1, 1, deep, LANES), lambda x, c: (0, x, c, 0, 0)),
        scratch_shapes=[pltpu.VMEM((nz, LANES), F32)],
        compiler_params=params(),
        cost_estimate=pl.CostEstimate(
            flops=0, bytes_accessed=coils * 2 * planes * ny * nz * 4, transcendentals=0
        ),
        name="maps_columns",
    )(coil_maps)


def last_maps_columns(coil_maps, count, first, coils):
    _, _, planes, ny, nz = coil_maps.shape
    deep = nz // count
    sizes = (coils + 1, coils - 1)
    return pl.pallas_call(
        functools.partial(last_maps_kernel, count, deep, coils),
        out_shape=[jax.ShapeDtypeStruct((count, planes, n, deep // 2, LANES), BF) for n in sizes],
        grid=(planes, coils),
        in_specs=[pl.BlockSpec((1, 2, 1, ny, nz), lambda x, c: (first + c, 0, x, 0, 0))],
        out_specs=[
            pl.BlockSpec((count, 1, n, deep // 2, LANES), lambda x, c: (0, x, 0, 0, 0))
            for n in sizes
        ],
        scratch_shapes=[pltpu.VMEM((nz, LANES), F32)],
        compiler_params=params(),
        cost_estimate=pl.CostEstimate(
            flops=0, bytes_accessed=coils * 2 * planes * ny * nz * 4, transcendentals=0
        ),
        name="last_maps_columns",
    )(coil_maps)


def low_half(shape):
    return lax.broadcasted_iota(jnp.int32, shape, len(shape) - 1) < BLK


def fetch(w_hbm, held, sems, k):
    size = held.shape[0] // sems.shape[0]
    source = w_hbm.at[pl.ds(k * (size + TAIL), size)]
    return pltpu.make_async_copy(source, held.at[pl.ds(k * size, size)], sems.at[k])


def fetch_all(w_hbm, held, sems):
    for k in range(sems.shape[0]):
        fetch(w_hbm, held, sems, k).start()


def warp_kernel(nx, deep, pad, links, owner, g_ref, w_hbm, o_ref, held, twice, sems):
    fetch_all(w_hbm, held, sems)
    count = sems.shape[0]
    planes = nx // count
    low = low_half((deep, 128))

    def split(x, carry):
        for v in range(3):
            row = g_ref[x, :, v * 128 : (v + 1) * 128].astype(F32)
            turned = pltpu.roll(row, BLK, 1)
            first = jnp.where(low, row, turned).astype(BF)
            second = jnp.where(low, turned, row).astype(BF)
            if v < 2:
                twice[3 * x, pl.ds(v * pad, deep), :] = first
                twice[3 * x + 1, pl.ds(v * pad, deep), :] = second
            else:
                twice[3 * x + 2, pl.ds(0, deep), :] = first
                twice[3 * x + 2, pl.ds(pad, deep), :] = second
        return carry

    lax.fori_loop(0, nx, split, 0, unroll=8)
    low_both = low_half((2 * pad, 128))

    def block(k, carry):
        fetch(w_hbm, held, sems, k).wait()
        row = owner[k] * planes
        start = k * 3 * planes
        for x in range(planes):
            outs = []
            for b in range(3):
                t = 3 * x + b
                one, two = links[2 * start + t], links[2 * start + 3 * planes + t]
                both = jnp.where(low_both, twice[one], twice[two])
                weight = held[pl.ds((start + t) * BLK, BLK), :]
                outs.append(
                    lax.dot_general(
                        both, weight, (((1,), (1,)), ((), ())), preferred_element_type=F32
                    )
                )
            a, b, c = outs
            re = jnp.concatenate([a[:deep], b[:deep]], axis=1)
            im = jnp.concatenate([a[pad : pad + deep], b[pad : pad + deep]], axis=1)
            rest = jnp.concatenate([c[:deep], c[pad : pad + deep]], axis=1)
            o_ref[row + x, :, 0:128] = re
            o_ref[row + x, :, 128:256] = im
            o_ref[row + x, :, 256:384] = rest
        return carry

    lax.fori_loop(0, count, block, 0)


def warp(columns, weights, links, owner):
    nx, deep, _ = columns.shape
    blocks = 3 * nx
    pad = max(16, deep)
    whole = pl.BlockSpec((nx, deep, LANES), lambda i, l, p: (0, 0, 0))
    return pl.pallas_call(
        functools.partial(warp_kernel, nx, deep, pad),
        out_shape=jax.ShapeDtypeStruct((nx, deep, LANES), F32),
        grid_spec=pltpu.PrefetchScalarGridSpec(
            num_scalar_prefetch=2,
            grid=(1,),
            in_specs=[pl.BlockSpec(memory_space=pltpu.VMEM), pl.BlockSpec(memory_space=pl.ANY)],
            out_specs=whole,
            scratch_shapes=[
                pltpu.VMEM((blocks * BLK, 2 * BLK), BF),
                pltpu.VMEM((blocks, 2 * pad, 128), BF),
                pltpu.SemaphoreType.DMA((owner.shape[0],)),
            ],
        ),
        compiler_params=params(),
        cost_estimate=pl.CostEstimate(
            flops=2 * blocks * 256 * 256 * 32, bytes_accessed=20 << 20, transcendentals=0
        ),
        name="warp",
    )(links, owner, in_vmem(columns), weights)


def spread(nx, deep, pad, links, owner, c_ref, w_hbm, o_ref, held, total, sems):
    count = sems.shape[0]
    planes = nx // count

    def clear(i, carry):
        total[pl.ds(i * 3, 3)] = jnp.zeros((3, 2 * pad, 128), F32)
        return carry

    lax.fori_loop(0, nx, clear, 0, unroll=8)
    low = low_half((2 * pad, 128))

    def tall(a, b):
        if deep == pad:
            return jnp.concatenate([a, b], axis=0)
        fill = jnp.zeros((pad - deep, a.shape[1]), a.dtype)
        return jnp.concatenate([a, fill, b, fill], axis=0)

    def block(k, carry):
        fetch(w_hbm, held, sems, k).wait()
        row = owner[k] * planes
        start = k * 3 * planes
        for x in range(planes):
            re, im, rest = (c_ref[row + x, :, v * 128 : (v + 1) * 128] for v in range(3))
            tiles = (
                tall(re[:, :BLK], im[:, :BLK]),
                tall(re[:, BLK:], im[:, BLK:]),
                tall(rest[:, :BLK], rest[:, BLK:]),
            )
            for b in range(3):
                t = 3 * x + b
                one, two = links[2 * start + t], links[2 * start + 3 * planes + t]
                weight = held[pl.ds((start + t) * BLK, BLK), :]
                out = jnp.dot(tiles[b].astype(BF), weight, preferred_element_type=F32)
                zero = jnp.zeros_like(out)
                total[one] += jnp.where(low, out, zero)
                total[two] += jnp.where(low, zero, out)
        return carry

    lax.fori_loop(0, count, block, 0)
    low_row = low_half((deep, 128))

    def gather(x, carry):
        sums = []
        for b in range(3):
            value = total[3 * x + b]
            sums.append(value + pltpu.roll(value, BLK, 1))
        a, b, c = sums
        o_ref[x, :, 0:128] = jnp.where(low_row, a[:deep], b[:deep]).astype(BF)
        o_ref[x, :, 128:256] = jnp.where(
            low_row, a[pad : pad + deep], b[pad : pad + deep]
        ).astype(BF)
        o_ref[x, :, 256:384] = jnp.where(low_row, c[:deep], c[pad : pad + deep]).astype(BF)
        return carry

    lax.fori_loop(0, nx, gather, 0, unroll=8)


def coil_kernel(nx, deep, pad, skip, ends, landed, *refs):
    fresh = skip is None
    if ends:
        links, owner, *refs = refs
    s_ref, w_ref, mask, iy, fx, bx, oy, *refs = refs
    if not fresh:
        before, *refs, sem = refs
    if ends:
        w_hbm, grad_ref, rows, o_ref, held, total, sems = refs

        @pl.when(pl.program_id(0) == 0)
        def _():
            fetch_all(w_hbm, held, sems)
    else:
        o_ref, rows = refs
    first = pl.program_id(0) == 0
    if not fresh:
        earlier = pltpu.make_async_copy(before.at[:, pl.ds(skip, deep), :], o_ref, sem)
        pl.when(first)(earlier.start)
    s_ref = s_ref.at[:, pl.program_id(0) if landed else 0]
    group = 8 if nx % 8 == 0 else 1
    cube = rows.reshape(3, nx, pad, 128)
    low = low_half((group, deep, 128))

    def thirds(ref, at):
        return tuple(ref[at, :, v * 128 : (v + 1) * 128].astype(F32) for v in range(3))

    def expand(i, carry):
        at = pl.ds(i * group, group)
        s0, s1, s2 = thirds(s_ref, at)
        w0, w1, w2 = thirds(w_ref, at)
        turned = pltpu.roll(s2, BLK, 2)
        other = pltpu.roll(w2, BLK, 2)
        real = jnp.where(low, s2, turned)
        imag = jnp.where(low, turned, s2)
        cube[0, at, pl.ds(0, deep), :] = s0 * w0 - s1 * w1
        cube[1, at, pl.ds(0, deep), :] = s0 * w1 + s1 * w0
        cube[2, at, pl.ds(0, deep), :] = real * w2 + imag * jnp.where(low, -other, other)
        return carry

    lax.fori_loop(0, nx // group, expand, 0, unroll=4)

    batch = 4 if deep % 4 == 0 else 1

    def column(i, carry):
        ats = [pl.ds(i * batch + b, nx, stride=pad) for b in range(batch)]
        line = jnp.concatenate(
            [jnp.concatenate([rows[v, at, :] for v in range(3)], axis=1) for at in ats], axis=0
        ).astype(BF)
        y = jnp.dot(line, iy[...], preferred_element_type=F32).astype(BF)
        y = jnp.concatenate(
            [
                jnp.concatenate([y[b * nx : (b + 1) * nx, h * HALF : (h + 1) * HALF] for b in range(batch)], axis=1)
                for h in range(2)
            ],
            axis=0,
        )
        y = jnp.dot(fx[...], y, preferred_element_type=F32)
        y = jnp.concatenate([(y[:, b * HALF : (b + 1) * HALF] * mask[...]).astype(BF) for b in range(batch)], axis=1)
        y = jnp.dot(bx[...], y, preferred_element_type=F32).astype(BF)
        y = jnp.concatenate(
            [
                jnp.concatenate([y[h * nx : (h + 1) * nx, b * HALF : (b + 1) * HALF] for h in range(2)], axis=1)
                for b in range(batch)
            ],
            axis=0,
        )
        y = jnp.dot(y, oy[...], preferred_element_type=F32)
        for b, at in enumerate(ats):
            for v in range(3):
                rows[v, at, :] = y[b * nx : (b + 1) * nx, v * 128 : (v + 1) * 128]
        return carry

    lax.fori_loop(0, deep // batch, column, 0)

    if not fresh:
        pl.when(first)(earlier.wait)

    def combine(i, carry):
        at = pl.ds(i * group, group)
        s0, s1, s2 = thirds(s_ref, at)
        r0, r1, r2 = (cube[v, at, pl.ds(0, deep), :] for v in range(3))
        turned = pltpu.roll(s2, BLK, 2)
        other = pltpu.roll(r2, BLK, 2)
        real = jnp.where(low, s2, turned)
        imag = jnp.where(low, turned, s2)
        terms = (
            s0 * r0 + s1 * r1,
            s0 * r1 - s1 * r0,
            real * r2 + imag * jnp.where(low, other, -other),
        )
        for v in range(3):
            lanes = slice(v * 128, (v + 1) * 128)
            old = o_ref[at, :, lanes]
            if fresh:
                old = jnp.where(first, jnp.zeros_like(old), old)
            o_ref[at, :, lanes] = old + terms[v]
        return carry

    lax.fori_loop(0, nx // group, combine, 0, unroll=4)
    if ends:

        @pl.when(pl.program_id(0) == pl.num_programs(0) - 1)
        def _():
            spread(nx, deep, pad, links, owner, o_ref, w_hbm, grad_ref, held, total, sems)


def coils(maps, first, count, warped, mask, tabs, before, part, warping=None, landed=False):
    nx, _, deep, _ = maps.shape
    pad = max(8, deep)
    fresh, ends = before is None, warping is not None

    def whole(shape):
        return pl.BlockSpec(shape, lambda c, *_: (0,) * len(shape), pipeline_mode=pl.Buffered(1))

    def columns(array):
        at = part if array.shape[1] > deep else 0
        return pl.BlockSpec(
            (nx, deep, LANES), lambda c, *_: (0, at, 0), pipeline_mode=pl.Buffered(1)
        )

    if landed:
        maps = in_vmem(maps)
        in_specs = [pl.BlockSpec(memory_space=pltpu.VMEM)]
    else:
        in_specs = [pl.BlockSpec((nx, 1, deep, LANES), lambda c, *_: (0, first + c, 0, 0))]
    args = [maps, warped, mask, *tabs]
    in_specs += [columns(warped)] + [whole(a.shape) for a in (mask, *tabs)]
    skip = None
    if not fresh:
        args += [before]
        in_specs += [pl.BlockSpec(memory_space=pl.ANY)]
        skip = part * deep if before.shape[1] > deep else 0
    scratch = [pltpu.VMEM((3, nx * pad, 128), F32)]
    prefetched = []
    if ends:
        weights, *prefetched = warping
        args += [weights]
        in_specs += [pl.BlockSpec(memory_space=pl.ANY)]
        scratch += [
            pltpu.VMEM((nx, deep, LANES), F32),
            pltpu.VMEM((3 * nx * BLK, 2 * BLK), BF),
            pltpu.VMEM((3 * nx, 2 * pad, 128), F32),
            pltpu.SemaphoreType.DMA((prefetched[1].shape[0],)),
        ]
    if not fresh:
        scratch += [pltpu.SemaphoreType.DMA]
    return pl.pallas_call(
        functools.partial(coil_kernel, nx, deep, pad, skip, ends, landed),
        out_shape=jax.ShapeDtypeStruct((nx, deep, LANES), BF if ends else F32),
        grid_spec=pltpu.PrefetchScalarGridSpec(
            num_scalar_prefetch=len(prefetched),
            grid=(count,),
            in_specs=in_specs,
            out_specs=pl.BlockSpec((nx, deep, LANES), lambda c, *_: (0, 0, 0)),
            scratch_shapes=scratch,
        ),
        compiler_params=params(),
        cost_estimate=pl.CostEstimate(
            flops=count * deep * 4 * 8 * nx * nx * 192 * 2,
            bytes_accessed=count * nx * deep * LANES * 2 + (14 << 20),
            transcendentals=0,
        ),
        name="coils",
    )(*prefetched, *args)


def update_kernel(count, b_ref, i_ref, a_ref, *refs):
    o_ref, scratch = refs[-2:]
    part = b_ref.shape[2]
    group = o_ref.shape[1]
    for x in range(group):
        plane = pl.program_id(0) * group + x
        for d in range(count):
            scratch[x, pl.ds(d * part, part), :] = b_ref[d, plane].astype(F32)
        grad = scratch[x].astype(BF).T.astype(F32)
        real = jnp.concatenate([grad[0:128], grad[256:320]], axis=0)
        imag = jnp.concatenate([grad[128:256], grad[320:384]], axis=0)
        for p, value in enumerate((real, imag)):
            o_ref[p, x] = i_ref[p, x] - 0.5 * (value - a_ref[p, x].astype(F32))


def update(back, image, adjoint, part, before):
    count, planes, deep, _ = back.shape
    _, _, ny, _ = image.shape
    lanes = count * deep
    group = math.gcd(planes, 6)
    block = pl.BlockSpec((2, group, ny, lanes), lambda x: (0, x, 0, part))
    more = [] if before is None else [before]
    return pl.pallas_call(
        functools.partial(update_kernel, count),
        out_shape=jax.ShapeDtypeStruct(image.shape, F32),
        grid=(planes // group,),
        in_specs=[
            pl.BlockSpec(memory_space=pltpu.VMEM),
            block,
            block,
        ]
        + [pl.BlockSpec(memory_space=pl.ANY)] * len(more),
        out_specs=block,
        scratch_shapes=[pltpu.VMEM((group, lanes, LANES), F32)],
        input_output_aliases={3: 0} if more else {},
        compiler_params=params(),
        cost_estimate=pl.CostEstimate(
            flops=0, bytes_accessed=2 * planes * ny * lanes * 12, transcendentals=0
        ),
        name="update",
    )(in_vmem(back), image, adjoint, *more)


def exchange(parts):
    return lax.all_to_all(parts, "slab", split_axis=0, concat_axis=0, tiled=True)


def after(value, *others):
    return lax.optimization_barrier((value, *others))[0]


def gather_all(value):
    count = lax.axis_size("slab")
    half = count // 2
    pairs = [[i, i + half] for i in range(half)]
    halves = [list(range(half)), list(range(half, count))]
    for groups in (pairs, halves):
        value = lax.all_gather(value, "slab", axis=0, tiled=True, axis_index_groups=groups)
    place = jnp.arange(count, dtype=jnp.int32)
    return value, place // 2 + half * (place % 2)


def per_device(image, adjoint_data, coil_maps, masks, sources, weights):
    count = lax.axis_size("slab")
    planes, ny, nz = image.shape[1:]
    nx = planes * count
    deep = nz // count
    total = coil_maps.shape[0]
    tabs = tables(nx, ny)
    sampled = jnp.pad(masks[0].astype(F32), ((0, 0), (0, HALF - ny)))
    mask = jnp.concatenate([sampled, sampled], axis=0)

    targets = 3 * planes
    matrices = weights[0].reshape(targets, 2, BLK, BLK)
    matrices = jnp.transpose(matrices, (0, 2, 1, 3)).reshape(targets * BLK, 2 * BLK)
    chosen = sources[0].T
    digits = jnp.concatenate([chosen // BLK, chosen % BLK], axis=0).astype(BF)
    digits = jnp.pad(digits, ((0, TAIL - 4), (0, 2 * BLK - targets)))
    own = jnp.concatenate([matrices, digits], axis=0)
    packed, owner = gather_all(own)
    digits = packed.reshape(count, targets * BLK + TAIL, 2 * BLK)[:, targets * BLK :]
    digits = digits[:, :4, :targets].astype(jnp.int32)
    links = (digits[:, :2] * BLK + digits[:, 2:]).reshape(-1)

    def run(received, first, size, before, part, **more):
        maps = received.reshape(nx, received.shape[2], -1, LANES)
        return coils(maps, first, size, warped, mask, tabs, before, part, **more)

    def back(grad, *needs):
        return exchange(after(grad, *needs).reshape(count, planes, -1, LANES))

    columns = exchange(image_columns(image, count))
    warped = warp(columns.reshape(nx, deep, LANES), packed, links, owner)
    warping = (packed, links, owner)
    halves = parts_of(deep) == 2
    early = total - 3 * total // 8 if halves else total - 1
    late = total - early
    maps = maps_columns(coil_maps, count, 0, early)
    arrived = exchange(after(maps, columns))
    if not halves:
        maps = maps_columns(coil_maps, count, early, late)
        last = exchange(after(maps, arrived, warped))
        combined = run(arrived, 0, early, None, 0)
        grad = run(last, 0, late, combined, 0, warping=warping)
        return update(back(grad), image, adjoint_data, 0, None)

    first, second = last_maps_columns(coil_maps, count, early, late)
    first = exchange(after(first, arrived))
    combined = run(arrived, 0, early, None, 0)
    second = exchange(after(second, first, combined))
    grad = run(first, 0, late, combined, 0, warping=warping)
    half = run(first, late, 1, combined, 1)
    back_first = back(grad, second, half)
    grad = run(second, 0, late - 1, half, 1, warping=warping, landed=True)
    back_second = back(grad, back_first)
    result = update(back_first, image, adjoint_data, 0, None)
    return update(back_second, image, adjoint_data, 1, result)


def solution(mesh):
    return jax.shard_map(
        per_device,
        mesh=mesh,
        in_specs=(
            P(None, ("grp", "slab"), None, None),
            P(None, ("grp", "slab"), None, None),
            P(None, None, ("grp", "slab"), None, None),
            P(None, "grp", None),
            P(None, ("grp", "slab"), None),
            P(None, ("grp", "slab"), None),
        ),
        out_specs=P(None, ("grp", "slab"), None, None),
        check_vma=False,
    )
```

```python
import functools
import math

import jax
import jax.numpy as jnp
import numpy as np
from jax import lax
from jax.experimental import pallas as pl
from jax.experimental.pallas import tpu as pltpu
from jax.sharding import PartitionSpec as P

BLK = 64
LANES = 384
TAIL = 16
HALF = 256
VMEM_LIMIT = 56 * 1024 * 1024
BF = jnp.bfloat16
F32 = jnp.float32


def lane_order(length):
    lo, rest = 128, length - 128
    part = np.concatenate([np.zeros(lo), np.ones(lo), np.zeros(rest), np.ones(rest)])
    pos = np.concatenate([np.arange(lo), np.arange(lo), lo + np.arange(rest), lo + np.arange(rest)])
    return part.astype(np.int32), pos.astype(np.int32)


def dft_table(length, direction):
    positions = np.arange(length)
    phases = (positions[:, None] * positions[None, :] % length).astype(np.float32)
    phases = phases * np.float32(2.0 * math.pi / length)
    factor = np.float32(1.0 / math.sqrt(length))
    cosine = np.cos(phases) * factor
    sine = np.sin(phases) * (np.float32(direction) * factor)
    upper = np.stack([cosine, -sine], axis=1)
    lower = np.stack([sine, cosine], axis=1)
    return np.stack([upper, lower], axis=0)


def tables(nx, ny):
    part, pos = lane_order(ny)
    fwd_y, inv_y = dft_table(ny, -1.0), dft_table(ny, 1.0)
    into_y = np.zeros((2 * ny, 2, HALF), np.float32)
    into_y[:, :, :ny] = np.transpose(fwd_y[:, :, part, pos], (2, 0, 1))
    from_y = np.zeros((2, HALF, 2 * ny), np.float32)
    from_y[:, :ny, :] = np.transpose(inv_y[part, pos], (1, 2, 0))
    fwd_x = dft_table(nx, -1.0).reshape(2 * nx, 2 * nx)
    inv_x = dft_table(nx, 1.0).reshape(2 * nx, 2 * nx)
    out = (into_y.reshape(2 * ny, 2 * HALF), fwd_x, inv_x, from_y.reshape(2 * HALF, 2 * ny))
    return tuple(jnp.asarray(t, BF) for t in out)


def params():
    return pltpu.CompilerParams(vmem_limit_bytes=VMEM_LIMIT)


def in_vmem(array):
    return pltpu.with_memory_space_constraint(array, pltpu.VMEM)


def to_rows(parts):
    stacked = jnp.concatenate(
        [parts[0, :128], parts[1, :128], parts[0, 128:], parts[1, 128:]], axis=0
    )
    return stacked.T


def part_rows(scratch, count, deep, parts, d, h):
    part = deep // parts
    return scratch[pl.ds((h * count + d) * part, part), :]


def spread_rows(out, scratch, count, deep, parts):
    for d in range(count):
        rows = [part_rows(scratch, count, deep, parts, d, h) for h in range(parts)]
        out[d] = jnp.concatenate(rows, axis=0).astype(BF)


def parts_of(deep):
    return 2 if deep % 16 == 0 else 1


def image_kernel(count, deep, x_ref, o_ref, scratch):
    for x in range(x_ref.shape[1]):
        scratch[x] = to_rows(x_ref[:, x].astype(BF)).astype(F32)
        spread_rows(o_ref.at[:, x], scratch.at[x], count, deep, parts_of(deep))


def image_columns(image, count):
    _, planes, ny, nz = image.shape
    deep = nz // count
    group = math.gcd(planes, 6)
    return pl.pallas_call(
        functools.partial(image_kernel, count, deep),
        out_shape=jax.ShapeDtypeStruct((count, planes, deep, LANES), BF),
        grid=(planes // group,),
        in_specs=[pl.BlockSpec((2, group, ny, nz), lambda x: (0, x, 0, 0))],
        out_specs=pl.BlockSpec((count, group, deep, LANES), lambda x: (0, x, 0, 0)),
        scratch_shapes=[pltpu.VMEM((group, nz, LANES), F32)],
        compiler_params=params(),
        cost_estimate=pl.CostEstimate(flops=0, bytes_accessed=image.size * 6, transcendentals=0),
        name="image_columns",
    )(image)


def maps_kernel(count, deep, x_ref, o_ref, scratch):
    scratch[...] = to_rows(x_ref[0, :, 0]).astype(F32)
    spread_rows(o_ref.at[:, 0, 0], scratch, count, deep, parts_of(deep))


def last_maps_kernel(count, deep, coils, x_ref, first_ref, second_ref, scratch):
    scratch[...] = to_rows(x_ref[0, :, 0]).astype(F32)
    for c in range(coils):

        @pl.when(pl.program_id(1) == c)
        def _():
            for d in range(count):
                half = part_rows(scratch, count, deep, 2, d, 1).astype(BF)
                first_ref[d, 0, c] = part_rows(scratch, count, deep, 2, d, 0).astype(BF)
                if c == 0:
                    first_ref[d, 0, coils] = half
                else:
                    second_ref[d, 0, c - 1] = half


def maps_columns(coil_maps, count, first, coils):
    _, _, planes, ny, nz = coil_maps.shape
    deep = nz // count
    return pl.pallas_call(
        functools.partial(maps_kernel, count, deep),
        out_shape=jax.ShapeDtypeStruct((count, planes, coils, deep, LANES), BF),
        grid=(planes, coils),
        in_specs=[pl.BlockSpec((1, 2, 1, ny, nz), lambda x, c: (first + c, 0, x, 0, 0))],
        out_specs=pl.BlockSpec((count, 1, 1, deep, LANES), lambda x, c: (0, x, c, 0, 0)),
        scratch_shapes=[pltpu.VMEM((nz, LANES), F32)],
        compiler_params=params(),
        cost_estimate=pl.CostEstimate(
            flops=0, bytes_accessed=coils * 2 * planes * ny * nz * 4, transcendentals=0
        ),
        name="maps_columns",
    )(coil_maps)


def last_maps_columns(coil_maps, count, first, coils):
    _, _, planes, ny, nz = coil_maps.shape
    deep = nz // count
    sizes = (coils + 1, coils - 1)
    return pl.pallas_call(
        functools.partial(last_maps_kernel, count, deep, coils),
        out_shape=[jax.ShapeDtypeStruct((count, planes, n, deep // 2, LANES), BF) for n in sizes],
        grid=(planes, coils),
        in_specs=[pl.BlockSpec((1, 2, 1, ny, nz), lambda x, c: (first + c, 0, x, 0, 0))],
        out_specs=[
            pl.BlockSpec((count, 1, n, deep // 2, LANES), lambda x, c: (0, x, 0, 0, 0))
            for n in sizes
        ],
        scratch_shapes=[pltpu.VMEM((nz, LANES), F32)],
        compiler_params=params(),
        cost_estimate=pl.CostEstimate(
            flops=0, bytes_accessed=coils * 2 * planes * ny * nz * 4, transcendentals=0
        ),
        name="last_maps_columns",
    )(coil_maps)


def low_half(shape):
    return lax.broadcasted_iota(jnp.int32, shape, len(shape) - 1) < BLK


def fetch(w_hbm, held, sems, k):
    size = held.shape[0] // sems.shape[0]
    source = w_hbm.at[pl.ds(k * (size + TAIL), size)]
    return pltpu.make_async_copy(source, held.at[pl.ds(k * size, size)], sems.at[k])


def fetch_all(w_hbm, held, sems):
    for k in range(sems.shape[0]):
        fetch(w_hbm, held, sems, k).start()


def warp_kernel(nx, deep, pad, links, owner, g_ref, w_hbm, o_ref, held, twice, sems):
    fetch_all(w_hbm, held, sems)
    count = sems.shape[0]
    planes = nx // count
    low = low_half((deep, 128))

    def split(x, carry):
        for v in range(3):
            row = g_ref[x, :, v * 128 : (v + 1) * 128].astype(F32)
            turned = pltpu.roll(row, BLK, 1)
            first = jnp.where(low, row, turned).astype(BF)
            second = jnp.where(low, turned, row).astype(BF)
            if v < 2:
                twice[3 * x, pl.ds(v * pad, deep), :] = first
                twice[3 * x + 1, pl.ds(v * pad, deep), :] = second
            else:
                twice[3 * x + 2, pl.ds(0, deep), :] = first
                twice[3 * x + 2, pl.ds(pad, deep), :] = second
        return carry

    lax.fori_loop(0, nx, split, 0, unroll=8)
    low_both = low_half((2 * pad, 128))

    def block(k, carry):
        fetch(w_hbm, held, sems, k).wait()
        row = owner[k] * planes
        start = k * 3 * planes
        for x in range(planes):
            outs = []
            for b in range(3):
                t = 3 * x + b
                one, two = links[2 * start + t], links[2 * start + 3 * planes + t]
                both = jnp.where(low_both, twice[one], twice[two])
                weight = held[pl.ds((start + t) * BLK, BLK), :]
                outs.append(
                    lax.dot_general(
                        both, weight, (((1,), (1,)), ((), ())), preferred_element_type=F32
                    )
                )
            a, b, c = outs
            re = jnp.concatenate([a[:deep], b[:deep]], axis=1)
            im = jnp.concatenate([a[pad : pad + deep], b[pad : pad + deep]], axis=1)
            rest = jnp.concatenate([c[:deep], c[pad : pad + deep]], axis=1)
            o_ref[row + x, :, 0:128] = re
            o_ref[row + x, :, 128:256] = im
            o_ref[row + x, :, 256:384] = rest
        return carry

    lax.fori_loop(0, count, block, 0)


def warp(columns, weights, links, owner):
    nx, deep, _ = columns.shape
    blocks = 3 * nx
    pad = max(16, deep)
    whole = pl.BlockSpec((nx, deep, LANES), lambda i, l, p: (0, 0, 0))
    return pl.pallas_call(
        functools.partial(warp_kernel, nx, deep, pad),
        out_shape=jax.ShapeDtypeStruct((nx, deep, LANES), F32),
        grid_spec=pltpu.PrefetchScalarGridSpec(
            num_scalar_prefetch=2,
            grid=(1,),
            in_specs=[pl.BlockSpec(memory_space=pltpu.VMEM), pl.BlockSpec(memory_space=pl.ANY)],
            out_specs=whole,
            scratch_shapes=[
                pltpu.VMEM((blocks * BLK, 2 * BLK), BF),
                pltpu.VMEM((blocks, 2 * pad, 128), BF),
                pltpu.SemaphoreType.DMA((owner.shape[0],)),
            ],
        ),
        compiler_params=params(),
        cost_estimate=pl.CostEstimate(
            flops=2 * blocks * 256 * 256 * 32, bytes_accessed=20 << 20, transcendentals=0
        ),
        name="warp",
    )(links, owner, in_vmem(columns), weights)


def spread(nx, deep, pad, links, owner, c_ref, w_hbm, o_ref, held, total, sems):
    count = sems.shape[0]
    planes = nx // count

    def clear(i, carry):
        total[pl.ds(i * 3, 3)] = jnp.zeros((3, 2 * pad, 128), F32)
        return carry

    lax.fori_loop(0, nx, clear, 0, unroll=8)
    low = low_half((2 * pad, 128))

    def tall(a, b):
        if deep == pad:
            return jnp.concatenate([a, b], axis=0)
        fill = jnp.zeros((pad - deep, a.shape[1]), a.dtype)
        return jnp.concatenate([a, fill, b, fill], axis=0)

    def block(k, carry):
        fetch(w_hbm, held, sems, k).wait()
        row = owner[k] * planes
        start = k * 3 * planes
        for x in range(planes):
            re, im, rest = (c_ref[row + x, :, v * 128 : (v + 1) * 128] for v in range(3))
            tiles = (
                tall(re[:, :BLK], im[:, :BLK]),
                tall(re[:, BLK:], im[:, BLK:]),
                tall(rest[:, :BLK], rest[:, BLK:]),
            )
            for b in range(3):
                t = 3 * x + b
                one, two = links[2 * start + t], links[2 * start + 3 * planes + t]
                weight = held[pl.ds((start + t) * BLK, BLK), :]
                out = jnp.dot(tiles[b].astype(BF), weight, preferred_element_type=F32)
                zero = jnp.zeros_like(out)
                total[one] += jnp.where(low, out, zero)
                total[two] += jnp.where(low, zero, out)
        return carry

    lax.fori_loop(0, count, block, 0)
    low_row = low_half((deep, 128))

    def gather(x, carry):
        sums = []
        for b in range(3):
            value = total[3 * x + b]
            sums.append(value + pltpu.roll(value, BLK, 1))
        a, b, c = sums
        o_ref[x, :, 0:128] = jnp.where(low_row, a[:deep], b[:deep]).astype(BF)
        o_ref[x, :, 128:256] = jnp.where(
            low_row, a[pad : pad + deep], b[pad : pad + deep]
        ).astype(BF)
        o_ref[x, :, 256:384] = jnp.where(low_row, c[:deep], c[pad : pad + deep]).astype(BF)
        return carry

    lax.fori_loop(0, nx, gather, 0, unroll=8)


def coil_kernel(nx, deep, pad, skip, ends, landed, *refs):
    fresh = skip is None
    if ends:
        links, owner, *refs = refs
    s_ref, w_ref, mask, iy, fx, bx, oy, *refs = refs
    if not fresh:
        before, *refs, sem = refs
    if ends:
        w_hbm, grad_ref, rows, o_ref, held, total, sems = refs

        @pl.when(pl.program_id(0) == 0)
        def _():
            fetch_all(w_hbm, held, sems)
    else:
        o_ref, rows = refs
    first = pl.program_id(0) == 0
    if not fresh:
        earlier = pltpu.make_async_copy(before.at[:, pl.ds(skip, deep), :], o_ref, sem)
        pl.when(first)(earlier.start)
    s_ref = s_ref.at[:, pl.program_id(0) if landed else 0]
    group = 8 if nx % 8 == 0 else 1
    cube = rows.reshape(3, nx, pad, 128)
    low = low_half((group, deep, 128))

    def thirds(ref, at):
        return tuple(ref[at, :, v * 128 : (v + 1) * 128].astype(F32) for v in range(3))

    def expand(i, carry):
        at = pl.ds(i * group, group)
        s0, s1, s2 = thirds(s_ref, at)
        w0, w1, w2 = thirds(w_ref, at)
        turned = pltpu.roll(s2, BLK, 2)
        other = pltpu.roll(w2, BLK, 2)
        real = jnp.where(low, s2, turned)
        imag = jnp.where(low, turned, s2)
        cube[0, at, pl.ds(0, deep), :] = s0 * w0 - s1 * w1
        cube[1, at, pl.ds(0, deep), :] = s0 * w1 + s1 * w0
        cube[2, at, pl.ds(0, deep), :] = real * w2 + imag * jnp.where(low, -other, other)
        return carry

    lax.fori_loop(0, nx // group, expand, 0, unroll=8)

    batch = 4 if deep % 4 == 0 else 1

    def column(i, carry):
        ats = [pl.ds(i * batch + b, nx, stride=pad) for b in range(batch)]
        line = jnp.concatenate(
            [jnp.concatenate([rows[v, at, :] for v in range(3)], axis=1) for at in ats], axis=0
        ).astype(BF)
        y = jnp.dot(line, iy[...], preferred_element_type=F32).astype(BF)
        y = jnp.concatenate(
            [
                jnp.concatenate([y[b * nx : (b + 1) * nx, h * HALF : (h + 1) * HALF] for b in range(batch)], axis=1)
                for h in range(2)
            ],
            axis=0,
        )
        y = jnp.dot(fx[...], y, preferred_element_type=F32)
        y = jnp.concatenate([(y[:, b * HALF : (b + 1) * HALF] * mask[...]).astype(BF) for b in range(batch)], axis=1)
        y = jnp.dot(bx[...], y, preferred_element_type=F32).astype(BF)
        y = jnp.concatenate(
            [
                jnp.concatenate([y[h * nx : (h + 1) * nx, b * HALF : (b + 1) * HALF] for h in range(2)], axis=1)
                for b in range(batch)
            ],
            axis=0,
        )
        y = jnp.dot(y, oy[...], preferred_element_type=F32)
        for b, at in enumerate(ats):
            for v in range(3):
                rows[v, at, :] = y[b * nx : (b + 1) * nx, v * 128 : (v + 1) * 128]
        return carry

    lax.fori_loop(0, deep // batch, column, 0)

    if not fresh:
        pl.when(first)(earlier.wait)

    def combine(i, carry):
        at = pl.ds(i * group, group)
        s0, s1, s2 = thirds(s_ref, at)
        r0, r1, r2 = (cube[v, at, pl.ds(0, deep), :] for v in range(3))
        turned = pltpu.roll(s2, BLK, 2)
        other = pltpu.roll(r2, BLK, 2)
        real = jnp.where(low, s2, turned)
        imag = jnp.where(low, turned, s2)
        terms = (
            s0 * r0 + s1 * r1,
            s0 * r1 - s1 * r0,
            real * r2 + imag * jnp.where(low, other, -other),
        )
        for v in range(3):
            lanes = slice(v * 128, (v + 1) * 128)
            old = o_ref[at, :, lanes]
            if fresh:
                old = jnp.where(first, jnp.zeros_like(old), old)
            o_ref[at, :, lanes] = old + terms[v]
        return carry

    lax.fori_loop(0, nx // group, combine, 0, unroll=8)
    if ends:

        @pl.when(pl.program_id(0) == pl.num_programs(0) - 1)
        def _():
            spread(nx, deep, pad, links, owner, o_ref, w_hbm, grad_ref, held, total, sems)


def coils(maps, first, count, warped, mask, tabs, before, part, warping=None, landed=False):
    nx, _, deep, _ = maps.shape
    pad = max(8, deep)
    fresh, ends = before is None, warping is not None

    def whole(shape):
        return pl.BlockSpec(shape, lambda c, *_: (0,) * len(shape), pipeline_mode=pl.Buffered(1))

    def columns(array):
        at = part if array.shape[1] > deep else 0
        return pl.BlockSpec(
            (nx, deep, LANES), lambda c, *_: (0, at, 0), pipeline_mode=pl.Buffered(1)
        )

    if landed:
        maps = in_vmem(maps)
        in_specs = [pl.BlockSpec(memory_space=pltpu.VMEM)]
    else:
        in_specs = [pl.BlockSpec((nx, 1, deep, LANES), lambda c, *_: (0, first + c, 0, 0))]
    args = [maps, warped, mask, *tabs]
    in_specs += [columns(warped)] + [whole(a.shape) for a in (mask, *tabs)]
    skip = None
    if not fresh:
        args += [before]
        in_specs += [pl.BlockSpec(memory_space=pl.ANY)]
        skip = part * deep if before.shape[1] > deep else 0
    scratch = [pltpu.VMEM((3, nx * pad, 128), F32)]
    prefetched = []
    if ends:
        weights, *prefetched = warping
        args += [weights]
        in_specs += [pl.BlockSpec(memory_space=pl.ANY)]
        scratch += [
            pltpu.VMEM((nx, deep, LANES), F32),
            pltpu.VMEM((3 * nx * BLK, 2 * BLK), BF),
            pltpu.VMEM((3 * nx, 2 * pad, 128), F32),
            pltpu.SemaphoreType.DMA((prefetched[1].shape[0],)),
        ]
    if not fresh:
        scratch += [pltpu.SemaphoreType.DMA]
    return pl.pallas_call(
        functools.partial(coil_kernel, nx, deep, pad, skip, ends, landed),
        out_shape=jax.ShapeDtypeStruct((nx, deep, LANES), BF if ends else F32),
        grid_spec=pltpu.PrefetchScalarGridSpec(
            num_scalar_prefetch=len(prefetched),
            grid=(count,),
            in_specs=in_specs,
            out_specs=pl.BlockSpec((nx, deep, LANES), lambda c, *_: (0, 0, 0)),
            scratch_shapes=scratch,
        ),
        compiler_params=params(),
        cost_estimate=pl.CostEstimate(
            flops=count * deep * 4 * 8 * nx * nx * 192 * 2,
            bytes_accessed=count * nx * deep * LANES * 2 + (14 << 20),
            transcendentals=0,
        ),
        name="coils",
    )(*prefetched, *args)


def update_kernel(count, b_ref, i_ref, a_ref, *refs):
    o_ref, scratch = refs[-2:]
    part = b_ref.shape[2]
    group = o_ref.shape[1]
    for x in range(group):
        plane = pl.program_id(0) * group + x
        for d in range(count):
            scratch[x, pl.ds(d * part, part), :] = b_ref[d, plane].astype(F32)
        grad = scratch[x].astype(BF).T.astype(F32)
        real = jnp.concatenate([grad[0:128], grad[256:320]], axis=0)
        imag = jnp.concatenate([grad[128:256], grad[320:384]], axis=0)
        for p, value in enumerate((real, imag)):
            o_ref[p, x] = i_ref[p, x] - 0.5 * (value - a_ref[p, x].astype(F32))


def update(back, image, adjoint, part, before):
    count, planes, deep, _ = back.shape
    _, _, ny, _ = image.shape
    lanes = count * deep
    group = math.gcd(planes, 6)
    block = pl.BlockSpec((2, group, ny, lanes), lambda x: (0, x, 0, part))
    more = [] if before is None else [before]
    return pl.pallas_call(
        functools.partial(update_kernel, count),
        out_shape=jax.ShapeDtypeStruct(image.shape, F32),
        grid=(planes // group,),
        in_specs=[
            pl.BlockSpec(memory_space=pltpu.VMEM),
            block,
            block,
        ]
        + [pl.BlockSpec(memory_space=pl.ANY)] * len(more),
        out_specs=block,
        scratch_shapes=[pltpu.VMEM((group, lanes, LANES), F32)],
        input_output_aliases={3: 0} if more else {},
        compiler_params=params(),
        cost_estimate=pl.CostEstimate(
            flops=0, bytes_accessed=2 * planes * ny * lanes * 12, transcendentals=0
        ),
        name="update",
    )(in_vmem(back), image, adjoint, *more)


def exchange(parts):
    return lax.all_to_all(parts, "slab", split_axis=0, concat_axis=0, tiled=True)


def after(value, *others):
    return lax.optimization_barrier((value, *others))[0]


def swap_halves(value):
    count = lax.axis_size("slab")
    half = count // 2
    return lax.ppermute(value, "slab", [(i, i ^ half) for i in range(count)])


def gather_half(pair):
    count = lax.axis_size("slab")
    half = count // 2
    groups = [list(range(half)), list(range(half, count))]
    gathered = lax.all_gather(pair, "slab", axis=0, tiled=True, axis_index_groups=groups)
    mine = lax.axis_index("slab") // half
    place = jnp.arange(count, dtype=jnp.int32)
    return gathered, place // 2 + half * ((place % 2) ^ mine)


def per_device(image, adjoint_data, coil_maps, masks, sources, weights):
    count = lax.axis_size("slab")
    planes, ny, nz = image.shape[1:]
    nx = planes * count
    deep = nz // count
    total = coil_maps.shape[0]
    tabs = tables(nx, ny)
    sampled = jnp.pad(masks[0].astype(F32), ((0, 0), (0, HALF - ny)))
    mask = jnp.concatenate([sampled, sampled], axis=0)

    targets = 3 * planes
    matrices = weights[0].reshape(targets, 2, BLK, BLK)
    matrices = jnp.transpose(matrices, (0, 2, 1, 3)).reshape(targets * BLK, 2 * BLK)
    chosen = sources[0].T
    digits = jnp.concatenate([chosen // BLK, chosen % BLK], axis=0).astype(BF)
    digits = jnp.pad(digits, ((0, TAIL - 4), (0, 2 * BLK - targets)))
    own = jnp.concatenate([matrices, digits], axis=0)
    crossed = swap_halves(own)
    packed, owner = gather_half(jnp.concatenate([own, crossed], axis=0))
    digits = packed.reshape(count, targets * BLK + TAIL, 2 * BLK)[:, targets * BLK :]
    digits = digits[:, :4, :targets].astype(jnp.int32)
    links = (digits[:, :2] * BLK + digits[:, 2:]).reshape(-1)

    def run(received, first, size, before, part, **more):
        maps = received.reshape(nx, received.shape[2], -1, LANES)
        return coils(maps, first, size, warped, mask, tabs, before, part, **more)

    def back(grad, *needs):
        return exchange(after(grad, *needs).reshape(count, planes, -1, LANES))

    columns = exchange(image_columns(image, count))
    warped = warp(columns.reshape(nx, deep, LANES), packed, links, owner)
    warping = (packed, links, owner)
    halves = parts_of(deep) == 2
    early = total - 3 * total // 8 if halves else total - 1
    late = total - early
    maps = maps_columns(coil_maps, count, 0, early)
    arrived = exchange(after(maps, columns, crossed))
    if not halves:
        maps = maps_columns(coil_maps, count, early, late)
        last = exchange(after(maps, arrived, warped))
        combined = run(arrived, 0, early, None, 0)
        grad = run(last, 0, late, combined, 0, warping=warping)
        return update(back(grad), image, adjoint_data, 0, None)

    first, second = last_maps_columns(coil_maps, count, early, late)
    first = exchange(after(first, arrived, warped))
    combined = run(arrived, 0, early, None, 0)
    second = exchange(after(second, first, combined))
    grad = run(first, 0, late, combined, 0, warping=warping)
    half = run(first, late, 1, combined, 1)
    back_first = back(grad, second, half)
    grad = run(second, 0, late - 1, half, 1, warping=warping, landed=True)
    back_second = back(grad, back_first)
    result = update(back_first, image, adjoint_data, 0, None)
    return update(back_second, image, adjoint_data, 1, result)


def solution(mesh):
    return jax.shard_map(
        per_device,
        mesh=mesh,
        in_specs=(
            P(None, ("grp", "slab"), None, None),
            P(None, ("grp", "slab"), None, None),
            P(None, None, ("grp", "slab"), None, None),
            P(None, "grp", None),
            P(None, ("grp", "slab"), None),
            P(None, ("grp", "slab"), None),
        ),
        out_specs=P(None, ("grp", "slab"), None, None),
        check_vma=False,
    )
```
